512 devices in a mesh: dp: 8 (over y, x_hi), context: 64 (over x_lo, z, core).
Axes of the slice: x: 4 (x_hi: 2, x_lo: 2; x = x_hi * 2 + x_lo), y: 4, z: 16, core: 2. Of those that a mesh axis runs over, the one named last changes fastest.
Arguments:
- codes: int32 [8, 65536], P('dp', 'context'), may hold values from 0 to 3
- variant_pos: int32 [8, 64], P('dp'), may hold values from 0 to 65535
- variant_shift: int32 [8, 64], P('dp'), may hold values from 1 to 3
- stem_weight: float32 [15, 4, 384], replicated, may hold values from -1.5 to 1.5
- conv_weight: bfloat16 [5, 384, 384], replicated, may hold values from -0.125 to 0.125
- cotangent: bfloat16 [8, 32768, 384], P('dp', 'context'), may hold values from -6 to 6
Outputs:
- features: bfloat16 [8, 32768, 384], P('dp', 'context')
- d_pooled: bfloat16 [8, 32768, 384], P('dp', 'context')
- conv_grad: float32 [5, 384, 384], replicated
- stem_grad: float32 [15, 4, 384], replicated
The draws below stay inside these ranges and needn't reach their ends.
All inputs are finite; a program needn't handle non-finite values.
Results may differ from the reference program's by a relative error of at most 0.009.
Values may be sent and summed in bfloat16 or wider, within the bound.
A program may use at most 64 MiB of HBM per device.

```python
import math
import jax
import jax.numpy as jnp
from jax import lax

C = 384
VAR = 64
SEQ = 65536
POOLED = 32768
BATCH = 8


def with_ends(array, stream_key, smallest, largest):
    longest = array.shape.index(max(array.shape))
    spots = []
    for shift in (0, 1):
        where = [jax.random.randint(jax.random.fold_in(stream_key, axis), (), 0, length) for axis, length in enumerate(array.shape)]
        where[longest] = (where[longest] + shift) % array.shape[longest]
        spots.append(tuple(where))
    return array.at[spots[0]].set(smallest).at[spots[1]].set(largest)


def level_of(key, shape, shards, smallest, high):
    gain = 1.0
    for position, blocks in shards:
        draws = jax.random.uniform(jax.random.fold_in(jax.random.fold_in(key, 6), position), (blocks,), jnp.float32, smallest / len(shards), high / len(shards))
        gain = gain * jnp.repeat(jnp.exp(draws), shape[position] // blocks).reshape((-1,) + (1,) * (len(shape) - 1 - position))
    return gain


def scatter_about(key, dims, spread, most, split=(), kind=jnp.bfloat16):
    result = jax.random.normal(key, dims, jnp.float32) * spread
    if len(split) > 0:
        result = level_of(key, dims, split, -0.22, 0.18) * result
    return jnp.clip(result, min=-most, max=most).astype(kind)


def setup_inputs(seed: int = 0) -> dict:
    arg_keys = jax.random.split(jax.random.key(seed), 7)
    codes = with_ends(jax.random.randint(arg_keys[0], (BATCH, SEQ), 0, 4), jax.random.fold_in(arg_keys[0], 1), 0, 3).astype(jnp.int32)
    variant_pos = with_ends(jax.random.randint(arg_keys[1], (BATCH, VAR), 0, SEQ), jax.random.fold_in(arg_keys[1], 1), 0, SEQ - 1).astype(jnp.int32)
    variant_shift = with_ends(jax.random.randint(arg_keys[2], (BATCH, VAR), 1, 4), jax.random.fold_in(arg_keys[2], 1), 1, 3).astype(jnp.int32)
    stem_weight = scatter_about(arg_keys[3], (15, 4, C), 15 ** -0.5, 1.5, (), jnp.float32)
    conv_weight = scatter_about(arg_keys[4], (5, C, C), (5 * C) ** -0.5, 0.125)
    cotangent = scatter_about(arg_keys[5], (BATCH, POOLED, C), 1.0, 6.0, ((0, 8), (1, 64)))
    return dict(codes=codes, variant_pos=variant_pos, variant_shift=variant_shift, stem_weight=stem_weight, conv_weight=conv_weight, cotangent=cotangent)


root_scale = math.sqrt(2.0 / math.pi)
cubic = 0.044715

def gelu_tanh(value):
    return 0.5 * value * (1.0 + jnp.tanh(root_scale * (value + cubic * value * value * value)))

def gelu_slope(value):
    inner = jnp.tanh(root_scale * (value + cubic * value * value * value))
    return 0.5 * (1.0 + inner) + 0.5 * value * (1.0 - inner * inner) * root_scale * (1.0 + 3.0 * cubic * value * value)

def reference(codes, variant_pos, variant_shift, stem_weight, conv_weight, cotangent):
    length = codes.shape[1]
    rows = length // 2
    width = stem_weight.shape[2]
    flat_stem = stem_weight.reshape(60, width)

    def one_sequence(carry, items):
        conv_total, stem_total = carry
        base_row, positions, amounts, cot_row = items
        shifts = jnp.zeros((length,), jnp.int32).at[positions].add(amounts)
        mutated = (base_row + shifts) % 4
        onehot = (mutated[:, None] == jnp.arange(4, dtype=jnp.int32)[None, :]).astype(jnp.float32)
        padded = jnp.pad(onehot, ((7, 7), (0, 0)))
        windows = jnp.concatenate([padded[k:k + length] for k in range(15)], axis=1)
        stem = jnp.dot(windows, flat_stem, precision=lax.Precision.HIGHEST, preferred_element_type=jnp.float32)
        active = gelu_tanh(stem)
        pooled = (0.5 * (active[0::2] + active[1::2])).astype(jnp.bfloat16)
        pooled_f = pooled.astype(jnp.float32)
        gated = gelu_tanh(pooled_f).astype(jnp.bfloat16)
        gated_pad = jnp.pad(gated, ((2, 2), (0, 0)))
        conv_out = jnp.zeros((rows, width), jnp.float32)
        for offset in range(5):
            conv_out = conv_out + jnp.dot(gated_pad[offset:offset + rows], conv_weight[offset], preferred_element_type=jnp.float32)
        features = (pooled_f + conv_out).astype(jnp.bfloat16)
        cot_pad = jnp.pad(cot_row, ((2, 2), (0, 0)))
        back = jnp.zeros((rows, width), jnp.float32)
        for offset in range(5):
            back = back + jnp.dot(cot_pad[4 - offset:4 - offset + rows], conv_weight[offset].T, preferred_element_type=jnp.float32)
        dpool = cot_row.astype(jnp.float32) + back * gelu_slope(pooled_f)
        grads = jnp.stack([jnp.dot(gated_pad[offset:offset + rows].T, cot_row, preferred_element_type=jnp.float32) for offset in range(5)])
        dstem = 0.5 * jnp.repeat(dpool, 2, axis=0) * gelu_slope(stem)
        stem_part = jnp.dot(windows.T, dstem, precision=lax.Precision.HIGHEST, preferred_element_type=jnp.float32)
        return ((conv_total + grads, stem_total + stem_part), (features, dpool.astype(jnp.bfloat16)))
    init = (jnp.zeros((5, width, width), jnp.float32), jnp.zeros((60, width), jnp.float32))
    (conv_grad, stem_grad), (features, d_pooled) = lax.scan(one_sequence, init, (codes, variant_pos, variant_shift, cotangent))
    return (features, d_pooled, conv_grad, stem_grad.reshape(15, 4, width))
```

```python
import math
import functools

import jax
import jax.numpy as jnp
from jax import lax
from jax.experimental import pallas as pl
from jax.experimental.pallas import tpu as pltpu

MESH = pl.DeviceIdType.MESH
SUB = 96
from jax.sharding import PartitionSpec as P


root_scale = math.sqrt(2.0 / math.pi)
cubic = 0.044715


def places(ring, deep, high):
    low = ring // high
    dp, ctx = lax.axis_index("dp"), lax.axis_index("context")
    y, xh = lax.div(dp, high), lax.rem(dp, high)
    core, z = lax.rem(ctx, 2), lax.rem(lax.div(ctx, 2), deep)
    x = xh * low + lax.div(ctx, 2 * deep)

    def device(x, y, z, core):
        return {
            "dp": y * high + lax.div(x, low),
            "context": (lax.rem(x, low) * deep + z) * 2 + core,
        }

    return x, y, z, core, device


def reduce_kernel(
    ring, deep, high, part, gathered,
    s0, r0, s1, r1, a2, s2, r2, v3, s3, r3, g3, w3,
    c0s, c0r, c1s, c1r, c2s, c2r, c3s, c3r, d3s, d3r, d2s, d2r, d1s, d1r, d0s, d0r,
):
    f32, bf16 = jnp.float32, jnp.bfloat16
    x, y, z, core, device = places(ring, deep, high)
    other = 1 - core
    per = 16 // ring
    fine = per // ring

    def along(half, level, step):
        if (half == 0) == (level == 1):
            return device(lax.rem(x + step, ring), y, z, core)
        return device(x, lax.rem(y + step, ring), z, core)

    def mine(half, level):
        return x if (half == 0) == (level == 1) else y

    def deeper(step):
        return device(x, y, lax.rem(z + step, deep), core)

    sibling = device(x, y, z, other)

    barrier = pltpu.get_barrier_semaphore()
    pl.semaphore_signal(barrier, inc=1, device_id=sibling, device_id_type=MESH)
    for step in range(1, ring):
        for half in range(2):
            pl.semaphore_signal(barrier, inc=1, device_id=along(half, 1, step), device_id_type=MESH)

    def greet(step, carry):
        pl.semaphore_signal(barrier, inc=1, device_id=deeper(step), device_id_type=MESH)
        return carry

    lax.fori_loop(1, deep, greet, 0)
    pl.semaphore_wait(barrier, 1 + 2 * (ring - 1) + deep - 1)

    def remote(src, dst, send, recv, to):
        return pltpu.make_async_remote_copy(
            src_ref=src, dst_ref=dst, send_sem=send, recv_sem=recv, device_id=to, device_id_type=MESH
        )

    order = sorted(range(1, ring), key=lambda d: -min(d, ring - d)) + [0]

    def level0(half, step):
        piece = lax.rem(mine(half, 1) + step, ring)
        return remote(
            s0.at[half, piece], r0.at[half, piece], c0s.at[half, step], c0r.at[half, step], sibling
        )

    for step in order:
        for half in range(2):
            piece = lax.rem(mine(half, 1) + step, ring)
            s0[half, piece] = part[other, half, piece].astype(bf16)
            level0(half, step).start()

    def level1(half, step):
        piece = lax.rem(mine(half, 1) + step, ring)
        return remote(
            s1.at[half, step - 1], r1.at[half, step - 1], c1s.at[half, step - 1], c1r.at[half, step - 1],
            along(half, 1, step),
        )

    for step in order:
        for half in range(2):
            piece = lax.rem(mine(half, 1) + step, ring)
            level0(half, step).wait_recv()
            if step:
                s1[half, step - 1] = (part[core, half, piece] + r0[half, piece].astype(f32)).astype(bf16)
                level1(half, step).start()

    def level2(half, step):
        return remote(
            s2.at[half, lax.rem(mine(half, 2) + step, ring)], r2.at[half, step - 1],
            c2s.at[half, step - 1], c2r.at[half, step - 1], along(half, 2, step),
        )

    for half in range(2):
        piece = mine(half, 1)
        total = part[core, half, piece] + r0[half, piece].astype(f32)
        for step in range(1, ring):
            level1(half, step).wait_recv()
            total = total + r1[half, step - 1].astype(f32)
        total = total.reshape(a2.shape[1:])
        a2[half] = total
        s2[half] = total.astype(bf16)
        for step in order[:-1]:
            level2(half, step).start()

    rows = fine * SUB
    for half in range(2):
        total = a2[half, mine(half, 2)]
        for step in range(1, ring):
            level2(half, step).wait_recv()
            total = total + r2[half, step - 1].astype(f32)
        v3[half * rows : (half + 1) * rows] = total
    share = 2 * rows // deep
    wide = s3.shape[1]
    for piece in range(deep):
        s3[piece] = v3[piece * share : piece * share + wide].astype(bf16)

    def level3(step):
        return remote(
            s3.at[lax.rem(z + step, deep)], r3.at[step - 1], c3s.at[step - 1], c3r.at[step - 1], deeper(step)
        )

    def back3(step):
        return remote(g3.at[z], g3.at[z], d3s.at[step - 1], d3r.at[step - 1], deeper(step))

    def far(i):
        near = deep // 2 - lax.div(i + 1, 2)
        return jnp.where(lax.rem(i, 2) == 0, near, deep - near)

    def send3(i, carry):
        level3(far(i)).start()
        return carry

    lax.fori_loop(0, deep - 1, send3, 0)

    def take3(i, total):
        step = i + 1
        level3(step).wait_recv()
        return total + r3[i].astype(f32)

    total = lax.fori_loop(0, deep - 1, take3, s3[z].astype(f32))
    g3[z] = total.astype(bf16)

    def spread3(i, carry):
        back3(far(i)).start()
        return carry

    lax.fori_loop(0, deep - 1, spread3, 0)

    def got3(i, carry):
        back3(i + 1).wait_recv()
        return carry

    lax.fori_loop(0, deep - 1, got3, 0)
    for piece in range(deep):
        w3[piece * share : piece * share + wide] = g3[piece].astype(f32)

    def back2(half, step):
        spot = gathered.at[core, half, mine(half, 1), mine(half, 2)]
        return remote(spot, spot, d2s.at[half, step - 1], d2r.at[half, step - 1], along(half, 2, step))

    for half in range(2):
        gathered[core, half, mine(half, 1), mine(half, 2)] = w3[half * rows : (half + 1) * rows].astype(bf16)
        for step in order[:-1]:
            back2(half, step).start()

    def back1(half, step):
        spot = gathered.at[core, half, mine(half, 1)]
        return remote(spot, spot, d1s.at[half, step - 1], d1r.at[half, step - 1], along(half, 1, step))

    def back0(half, step):
        spot = gathered.at[core, half, lax.rem(mine(half, 1) + ring - step, ring)]
        return remote(spot, spot, d0s.at[half, step], d0r.at[half, step], sibling)

    for half in range(2):
        for step in range(1, ring):
            back2(half, step).wait_recv()
        for step in order[:-1]:
            back1(half, step).start()
        back0(half, 0).start()
    near = sorted(range(1, ring), key=lambda d: min(d, ring - d))
    for step in near:
        for half in range(2):
            back1(half, step).wait_recv()
            back0(half, step).start()
    for half in range(2):
        for step in range(ring):
            back0(half, step).wait()
            level0(half, step).wait_send()
        for step in range(1, ring):
            level1(half, step).wait_send()
            level2(half, step).wait_send()
            back2(half, step).wait_send()
            back1(half, step).wait_send()

    def sent3(i, carry):
        level3(i + 1).wait_send()
        back3(i + 1).wait_send()
        return carry

    lax.fori_loop(0, deep - 1, sent3, 0)


def all_reduce(ring, deep, high, part):
    f32, bf16 = jnp.float32, jnp.bfloat16
    per = 16 // ring
    fine = per // ring
    share = 2 * fine * SUB // deep
    wide = -(-share // 16) * 16
    dma = pltpu.SemaphoreType.DMA
    level = lambda *lead: pltpu.VMEM((2,) + lead, bf16)
    pair = lambda *dims: [dma(dims), dma(dims)]
    return pl.pallas_call(
        functools.partial(reduce_kernel, ring, deep, high),
        out_shape=jax.ShapeDtypeStruct((2, 2, ring, ring, fine * SUB, 128), bf16),
        in_specs=[pl.BlockSpec(memory_space=pltpu.VMEM)],
        out_specs=pl.BlockSpec(memory_space=pltpu.VMEM),
        scratch_shapes=[
            level(ring, per * SUB, 128),
            level(ring, per * SUB, 128),
            level(ring - 1, per * SUB, 128),
            level(ring - 1, per * SUB, 128),
            pltpu.VMEM((2, ring, fine * SUB, 128), f32),
            level(ring, fine * SUB, 128),
            level(ring - 1, fine * SUB, 128),
            pltpu.VMEM((2 * fine * SUB + wide, 128), f32),
            pltpu.VMEM((deep, wide, 128), bf16),
            pltpu.VMEM((deep - 1, wide, 128), bf16),
            pltpu.VMEM((deep, wide, 128), bf16),
            pltpu.VMEM((2 * fine * SUB + wide, 128), f32),
            *pair(2, ring), *pair(2, ring - 1), *pair(2, ring - 1), *pair(deep - 1),
            *pair(deep - 1), *pair(2, ring - 1), *pair(2, ring - 1), *pair(2, ring),
        ],
        compiler_params=pltpu.CompilerParams(collective_id=0, has_side_effects=True),
        name="reduce",
    )(part.reshape(2, 2, ring, per * SUB, 128))


def finish_kernel(summed, conv, stem):
    t = pl.program_id(0)
    for k in range(3):
        for r in range(4):
            n = 12 * t + 4 * k + r
            conv[0, r * SUB : (r + 1) * SUB, k * 128 : (k + 1) * 128] = summed[
                lax.div(n, 15), lax.rem(n, 15)
            ].astype(jnp.float32)

    @pl.when(t == 0)
    def _():
        rows = jnp.concatenate([summed[0, 15], summed[2, 15]], axis=0).astype(jnp.float32)
        for k in range(3):
            for tap in range(15):
                stem[tap, :, k * 128 : (k + 1) * 128] = rows[k * 64 + 4 * tap : k * 64 + 4 * tap + 4]


def finish(summed):
    return pl.pallas_call(
        finish_kernel,
        grid=(5,),
        out_shape=(
            jax.ShapeDtypeStruct((5, 384, 384), jnp.float32),
            jax.ShapeDtypeStruct((15, 4, 384), jnp.float32),
        ),
        in_specs=[pl.BlockSpec((4, 16, SUB, 128), lambda t: (0, 0, 0, 0))],
        out_specs=(
            pl.BlockSpec((1, 384, 384), lambda t: (t, 0, 0)),
            pl.BlockSpec((15, 4, 384), lambda t: (0, 0, 0)),
        ),
        name="finish",
    )(summed.reshape(4, 16, SUB, 128))


def pack(taps, stem):
    width = 384
    blocks = taps.reshape(5, 4, SUB, 3, 128).transpose(0, 3, 1, 2, 4).reshape(4, 15, SUB, 128)
    stem = jnp.pad(stem, ((0, 4), (0, 0))).reshape(64, 3, 128).transpose(1, 0, 2).reshape(2, SUB, 128)
    last = jnp.zeros((4, 1, SUB, 128), jnp.float32).at[0, 0].set(stem[0]).at[2, 0].set(stem[1])
    return jnp.concatenate([blocks, last], axis=1).reshape(2, 2, 16 * SUB, 128)


def with_halo(block, sides, width):
    for axis, dim in sides:
        count = lax.axis_size(axis)
        forward = [(i, i + 1) for i in range(count - 1)]
        backward = [(target, source) for source, target in forward]
        low = lax.ppermute(
            lax.slice_in_dim(block, block.shape[dim] - width, None, axis=dim), axis, forward
        )
        high = lax.ppermute(lax.slice_in_dim(block, 0, width, axis=dim), axis, backward)
        block = jnp.concatenate([low, block, high], axis=dim)
    return block


def gelu_tanh(value):
    return 0.5 * value * (1.0 + jnp.tanh(root_scale * (value + cubic * value * value * value)))


def gelu_slope(value):
    inner = jnp.tanh(root_scale * (value + cubic * value * value * value))
    return 0.5 * (1.0 + inner) + 0.5 * value * (1.0 - inner * inner) * root_scale * (
        1.0 + 3.0 * cubic * value * value
    )


def per_device(codes, variant_pos, variant_shift, stem_weight, conv_weight, cotangent):
    length = codes.shape[1]
    half_rows = length // 2
    width = stem_weight.shape[2]
    first_base = lax.axis_index("context") * length
    places = first_base + jnp.arange(length, dtype=jnp.int32)
    matches = (variant_pos[:, None, :] == places[None, :, None]).astype(jnp.int32)
    shifts = jnp.sum(matches * variant_shift[:, None, :], axis=2)
    mutated = (codes + shifts) % 4 + 1
    extended = with_halo(mutated, (("context", 1),), 7)
    onehot = (extended[:, :, None] == jnp.arange(1, 5, dtype=jnp.int32)[None, None, :]).astype(
        jnp.float32
    )
    windows = jnp.concatenate([onehot[:, k : k + length] for k in range(15)], axis=2)
    flat_stem = stem_weight.reshape(60, width)
    stem = jnp.einsum(
        "blk,kc->blc",
        windows,
        flat_stem,
        precision=lax.Precision.HIGHEST,
        preferred_element_type=jnp.float32,
    )
    active = gelu_tanh(stem)
    pooled = (0.5 * (active[:, 0::2] + active[:, 1::2])).astype(jnp.bfloat16)
    pooled_f = pooled.astype(jnp.float32)
    gated = gelu_tanh(pooled_f).astype(jnp.bfloat16)
    gated_ext = with_halo(gated, (("context", 1),), 2)
    cot_ext = with_halo(cotangent, (("context", 1),), 2)
    conv_out = jnp.zeros((gated.shape[0], half_rows, width), jnp.float32)
    back = jnp.zeros((gated.shape[0], half_rows, width), jnp.float32)
    for offset in range(5):
        conv_out = conv_out + jnp.einsum(
            "brc,cd->brd",
            gated_ext[:, offset : offset + half_rows],
            conv_weight[offset],
            preferred_element_type=jnp.float32,
        )
        back = back + jnp.einsum(
            "brd,cd->brc",
            cot_ext[:, 4 - offset : 4 - offset + half_rows],
            conv_weight[offset],
            preferred_element_type=jnp.float32,
        )
    features = (pooled_f + conv_out).astype(jnp.bfloat16)
    dpool = cotangent.astype(jnp.float32) + back * gelu_slope(pooled_f)
    d_pooled = dpool.astype(jnp.bfloat16)
    tap_grads = jnp.stack(
        [
            jnp.einsum(
                "brc,brd->cd",
                gated_ext[:, offset : offset + half_rows],
                cotangent,
                preferred_element_type=jnp.float32,
            )
            for offset in range(5)
        ]
    )
    dstem = 0.5 * jnp.repeat(dpool, 2, axis=1) * gelu_slope(stem)
    stem_part = jnp.einsum(
        "blk,blc->kc",
        windows,
        dstem,
        precision=lax.Precision.HIGHEST,
        preferred_element_type=jnp.float32,
    )
    conv_grad, stem_grad = finish(all_reduce(4, 16, 2, pack(tap_grads, stem_part[0] if stem_part.ndim == 3 else stem_part)))
    return (features, d_pooled, conv_grad, stem_grad)


def solution(mesh):
    placed = (P("dp", "context"), P("dp", None), P("dp", None), P(), P(), P("dp", "context", None))
    return jax.shard_map(
        per_device,
        mesh=mesh,
        in_specs=placed,
        out_specs=(P("dp", "context", None), P("dp", "context", None), P(), P()),
        check_vma=False,
    )
```

```python
import functools
import math

import jax
import jax.numpy as jnp
from jax import lax
from jax.experimental import pallas as pl
from jax.experimental.pallas import tpu as pltpu
from jax.sharding import PartitionSpec as P

MESH = pl.DeviceIdType.MESH
f32, bf16 = jnp.float32, jnp.bfloat16
root_scale = math.sqrt(2.0 / math.pi)
cubic = 0.044715

C = 384
ROWS = 512
LEAD = 16
TALL = ROWS + 2 * LEAD
LANES = 640
PAIRS = 44


def places(ring, deep, high):
    low = ring // high
    dp, ctx = lax.axis_index("dp"), lax.axis_index("context")
    y, xh = lax.div(dp, high), lax.rem(dp, high)
    core, z = lax.rem(ctx, 2), lax.rem(lax.div(ctx, 2), deep)
    x = xh * low + lax.div(ctx, 2 * deep)

    def device(x, y, z, core):
        return {
            "dp": y * high + lax.div(x, low),
            "context": (lax.rem(x, low) * deep + z) * 2 + core,
        }

    return x, y, z, core, device


def remote(src, dst, send, recv, to):
    return pltpu.make_async_remote_copy(
        src_ref=src, dst_ref=dst, send_sem=send, recv_sem=recv, device_id=to, device_id_type=MESH
    )


def halo_kernel(count, codes, cot, near_codes, near_cot, sends, recvs):
    ctx = lax.axis_index("context")
    left = {"context": lax.rem(ctx + count - 1, count)}
    right = {"context": lax.rem(ctx + 1, count)}
    barrier = pltpu.get_barrier_semaphore()
    for to in (left, right):
        pl.semaphore_signal(barrier, inc=1, device_id=to, device_id_type=MESH)
    pl.semaphore_wait(barrier, 2)
    copies = [
        remote(codes, near_codes.at[0], sends.at[0], recvs.at[0], right),
        remote(codes, near_codes.at[1], sends.at[1], recvs.at[1], left),
        remote(cot.at[ROWS - LEAD : ROWS], near_cot.at[0], sends.at[2], recvs.at[2], right),
        remote(cot.at[0:LEAD], near_cot.at[1], sends.at[3], recvs.at[3], left),
    ]
    for copy in copies:
        copy.start()
    for copy in copies:
        copy.wait()


def halo(count, codes, cot):
    return pl.pallas_call(
        functools.partial(halo_kernel, count),
        out_shape=(
            jax.ShapeDtypeStruct((2, 8, 128), jnp.int32),
            jax.ShapeDtypeStruct((2, LEAD, C), bf16),
        ),
        in_specs=[pl.BlockSpec(memory_space=pltpu.VMEM)] * 2,
        out_specs=(pl.BlockSpec(memory_space=pltpu.VMEM),) * 2,
        scratch_shapes=[pltpu.SemaphoreType.DMA((4,)), pltpu.SemaphoreType.DMA((4,))],
        compiler_params=pltpu.CompilerParams(collective_id=0, has_side_effects=True),
        name="halo",
    )(codes, cot)


def main_kernel(
    ring, deep, high, count,
    vpos, vshift, codes, near_codes, cot, near_cot, stem_weight, weight,
    features, d_pooled, gathered, stem_all,
    wt, wf, wsem, ws, stem, slopes, cotx, gx, pooled, pslope, shifted, spread, wins_t, gated_t, dstem,
    own, s0, r0, s1, r1, a2, s2, r2,
    t0, u0, tsum, t1, u1, t2, u2,
    v3, s3, r3, g3, w3,
    c0s, c0r, c1s, c1r, c2s, c2r, c3s, c3r, d3s, d3r, d2s, d2r, d1s, d1r, d0s, d0r,
    e0s, e0r, e1s, e1r, e2s, e2r, h0s, h0r,
):
    x, y, z, core, device = places(ring, deep, high)
    ctx = lax.axis_index("context")
    other = 1 - core
    per = 4 // ring
    rows1 = per * C
    rows2 = rows1 // ring

    def along(half, level, step):
        if (half == 0) == (level == 1):
            return device(lax.rem(x + step, ring), y, z, core)
        return device(x, lax.rem(y + step, ring), z, core)

    def mine(half, level):
        return x if (half == 0) == (level == 1) else y

    def deeper(step):
        return device(x, y, lax.rem(z + step, deep), core)

    sibling = device(x, y, z, other)
    order = sorted(range(1, ring), key=lambda d: -min(d, ring - d))
    near = order[::-1]

    barrier = pltpu.get_barrier_semaphore()
    pl.semaphore_signal(barrier, inc=1, device_id=sibling, device_id_type=MESH)

    def greet(step, carry):
        pl.semaphore_signal(barrier, inc=1, device_id=deeper(step), device_id_type=MESH)
        return carry

    lax.fori_loop(1, deep, greet, 0)
    for step in range(1, ring):
        for half in range(2):
            pl.semaphore_signal(barrier, inc=1, device_id=along(half, 1, step), device_id_type=MESH)

    loads = [pltpu.make_async_copy(weight.at[t], wt.at[:, t * C : (t + 1) * C], wsem.at[t]) for t in range(5)]
    loads += [pltpu.make_async_copy(weight.at[t], wf.at[t * C : (t + 1) * C], wsem.at[5 + t]) for t in range(5)]
    for load in loads:
        load.start()

    bases = jnp.concatenate(
        [near_codes[0, 7:8], codes[...], near_codes[1, 0:1], jnp.zeros((6, 128), jnp.int32)], axis=0
    )
    spot = (
        ctx * (2 * ROWS) - 128
        + 128 * lax.broadcasted_iota(jnp.int32, (16, 128), 0)
        + lax.broadcasted_iota(jnp.int32, (16, 128), 1)
    )
    for v in range(vpos.shape[1]):
        bases = bases + jnp.where(spot == vpos[0, v], vshift[0, v], 0)
    bases = jnp.where((spot >= 0) & (spot < count * (2 * ROWS)), bases & 3, 4)
    lane_in = lax.broadcasted_iota(jnp.int32, (128, 128), 0)
    lane_out = lax.broadcasted_iota(jnp.int32, (128, 128), 1)
    pick = (lane_in == 2 * (lane_out & 63) + lax.shift_right_logical(lane_out, 6)).astype(f32).astype(bf16)
    split = jnp.dot(bases.astype(f32).astype(bf16), pick, preferred_element_type=f32)
    turned = pltpu.roll(split, 64, 1)
    first = lax.broadcasted_iota(jnp.int32, (1, 128), 1) < 64
    evens, odds = [], []
    for p in range(5):
        evens.append(jnp.where(first, split[2 * p : 2 * p + 1], turned[2 * p + 1 : 2 * p + 2]))
        odds.append(jnp.where(first, turned[2 * p : 2 * p + 1], split[2 * p + 1 : 2 * p + 2]))
    even = jnp.broadcast_to(jnp.concatenate(evens, axis=1), (8, LANES))
    odd = jnp.broadcast_to(jnp.concatenate(odds, axis=1), (8, LANES))
    line = lax.broadcasted_iota(jnp.int32, (8, LANES), 0)
    both = jnp.where(line < 4, odd, pltpu.roll(even, LANES - 1, 1))
    hot = (both == (line & 3).astype(f32)).astype(f32)
    wide = [pltpu.roll(hot, LANES - (PAIRS + q), 1) for q in range(8)]
    windows_t = jnp.concatenate(wide + wide, axis=0)
    windows = windows_t.T[:TALL].astype(bf16)
    kept = jnp.concatenate(
        [pltpu.roll(hot, LANES - (PAIRS + LEAD + q), 1)[:, :ROWS] for q in range(8)], axis=0
    )
    wins_t[...] = kept.astype(bf16)

    ws[...] = jnp.zeros_like(ws)
    for k in range(15):
        ws[4 * k : 4 * k + 4, 0:C] = stem_weight[k]
        ws[4 * k + 4 : 4 * k + 8, C:] = stem_weight[k]
    taps = ws[...]
    upper = taps.astype(bf16)
    lower = (taps - upper.astype(f32)).astype(bf16)
    stem[...] = jnp.dot(windows, jnp.concatenate([upper, lower], axis=0), preferred_element_type=f32)

    def bend(value):
        square = value * value
        inner = jnp.tanh(value * (root_scale + (root_scale * cubic) * square))
        active = 0.5 * value * (1.0 + inner)
        slope = 0.5 * (1.0 + inner) + 0.5 * value * (1.0 - inner * inner) * (
            root_scale + (3.0 * root_scale * cubic) * square
        )
        return active, slope

    def activate(i, carry):
        rows = pl.ds(pl.multiple_of(i * 16, 16), 16)
        active_e, slope_e = bend(stem[rows, 0:C])
        active_o, slope_o = bend(stem[rows, C:])
        slopes[rows, 0:C] = 0.5 * slope_e
        slopes[rows, C:] = 0.5 * slope_o
        pool = (0.5 * (active_e + active_o)).astype(bf16).astype(f32)
        pooled[rows] = pool
        gate, slope = bend(pool)
        gx[rows] = gate.astype(bf16).astype(f32)
        pslope[rows] = slope
        return carry

    lax.fori_loop(0, TALL // 16, activate, 0)
    inside_left = jnp.where(ctx > 0, 1.0, 0.0)
    inside_right = jnp.where(ctx < count - 1, 1.0, 0.0)
    gx[0:LEAD] = gx[0:LEAD] * inside_left
    gx[LEAD + ROWS :] = gx[LEAD + ROWS :] * inside_right
    cotx[0:LEAD] = near_cot[0].astype(f32) * inside_left
    cotx[LEAD + ROWS :] = near_cot[1].astype(f32) * inside_right
    cotx[LEAD : LEAD + ROWS] = cot[...].astype(f32)
    gated_t[...] = gx[LEAD : LEAD + ROWS].T.astype(bf16)
    for t in range(5):
        shifted[:, t * C : (t + 1) * C] = cotx[LEAD + 2 - t : LEAD + 2 - t + ROWS].astype(bf16)
    shifted[:, 5 * C :] = jnp.zeros((ROWS, 128), bf16)

    pl.semaphore_wait(barrier, 1 + 2 * (ring - 1) + deep - 1)

    def level0(half, piece):
        return remote(
            s0.at[half, piece], r0.at[half, piece], c0s.at[half, piece], c0r.at[half, piece], sibling
        )

    def product(owner, j):
        at = pl.multiple_of(owner * 1024 + 256 * j, 256)
        return jnp.dot(gated_t[...], shifted[:, pl.ds(at, 256)], preferred_element_type=f32)

    for j in range(4):
        block = product(other, j)
        for k in range(2):
            half, sub = divmod(2 * j + k, 4)
            piece, sub = divmod(sub, per)
            s0[half, piece, sub * C : (sub + 1) * C] = block[:, 128 * k : 128 * (k + 1)].astype(bf16)
            if sub == per - 1:
                level0(half, piece).start()
    for j in range(4):
        block = product(core, j)
        for k in range(2):
            half, sub = divmod(2 * j + k, 4)
            piece, sub = divmod(sub, per)
            own[half, piece, sub * C : (sub + 1) * C] = block[:, 128 * k : 128 * (k + 1)]

    def level1(half, step):
        return remote(
            s1.at[half, step - 1], r1.at[half, step - 1], c1s.at[half, step - 1], c1r.at[half, step - 1],
            along(half, 1, step),
        )

    for half in range(2):
        for piece in range(ring):
            level0(half, piece).wait_recv()
    for step in order:
        for half in range(2):
            piece = lax.rem(mine(half, 1) + step, ring)
            s1[half, step - 1] = (own[half, piece] + r0[half, piece].astype(f32)).astype(bf16)
            level1(half, step).start()

    for load in loads:
        load.wait()
    for block in range(2):
        at = block * (ROWS // 2)
        rows = slice(at, at + ROWS // 2)
        more = slice(LEAD + at, LEAD + at + ROWS // 2)
        back = lax.dot_general(
            shifted[rows, : 5 * C], wt[...], (((1,), (1,)), ((), ())), preferred_element_type=f32
        )
        dpool = cotx[more] + back * pslope[more]
        d_pooled[rows] = dpool.astype(bf16)
        dstem[rows, 0:C] = (dpool * slopes[more, 0:C]).astype(bf16)
        dstem[rows, C:] = (dpool * slopes[more, C:]).astype(bf16)
    grad = jnp.dot(wins_t[...], dstem[...], preferred_element_type=f32)
    for k in range(3):
        tsum[k * 64 : k * 64 + 64] = grad[:, 128 * k : 128 * (k + 1)]
    for k in range(3):
        tsum[k * 64 : k * 64 + 60] = tsum[k * 64 : k * 64 + 60] + grad[4:64, C + 128 * k : C + 128 * (k + 1)]

    def stem0():
        return remote(t0, u0, e0s, e0r, sibling)

    t0[...] = tsum[pl.ds(pl.multiple_of(other * 96, 96), 96)].astype(bf16)
    stem0().start()

    for t in range(5):
        spread[:, t * C : (t + 1) * C] = gx[LEAD - 2 + t : LEAD - 2 + t + ROWS].astype(bf16)
    for block in range(2):
        at = block * (ROWS // 2)
        rows = slice(at, at + ROWS // 2)
        conv = jnp.dot(spread[rows], wf[...], preferred_element_type=f32)
        features[rows] = (pooled[LEAD + at : LEAD + at + ROWS // 2] + conv).astype(bf16)

    def stem1(step):
        return remote(t1, u1.at[step - 1], e1s.at[step - 1], e1r.at[step - 1], along(0, 1, step))

    def stem2(step):
        return remote(t2, u2.at[step - 1], e2s.at[step - 1], e2r.at[step - 1], along(0, 2, step))

    stem0().wait_recv()
    small = tsum[pl.ds(pl.multiple_of(core * 96, 96), 96)] + u0[...].astype(f32)
    t1[...] = small.astype(bf16)
    for step in order:
        stem1(step).start()

    def level2(half, step):
        return remote(
            s2.at[half, lax.rem(mine(half, 2) + step, ring)], r2.at[half, step - 1],
            c2s.at[half, step - 1], c2r.at[half, step - 1], along(half, 2, step),
        )

    for half in range(2):
        piece = mine(half, 1)
        total = own[half, piece] + r0[half, piece].astype(f32)
        for step in range(1, ring):
            level1(half, step).wait_recv()
            total = total + r1[half, step - 1].astype(f32)
        total = total.reshape(a2.shape[1:])
        a2[half] = total
        s2[half] = total.astype(bf16)
        for step in order:
            level2(half, step).start()

    for step in range(1, ring):
        stem1(step).wait_recv()
        small = small + u1[step - 1].astype(f32)
    t2[...] = small.astype(bf16)
    for step in order:
        stem2(step).start()

    for half in range(2):
        total = a2[half, mine(half, 2)]
        for step in range(1, ring):
            level2(half, step).wait_recv()
            total = total + r2[half, step - 1].astype(f32)
        v3[half * rows2 : (half + 1) * rows2] = total
    for step in range(1, ring):
        stem2(step).wait_recv()
        small = small + u2[step - 1].astype(f32)
    v3[2 * rows2 : 2 * rows2 + 96] = small
    share = (2 * rows2 + 96) // deep
    tall = s3.shape[1]
    for piece in range(deep):
        s3[piece] = v3[piece * share : piece * share + tall].astype(bf16)

    def level3(step):
        return remote(
            s3.at[lax.rem(z + step, deep)], r3.at[step - 1], c3s.at[step - 1], c3r.at[step - 1], deeper(step)
        )

    def back3(step):
        return remote(g3.at[z], g3.at[z], d3s.at[step - 1], d3r.at[step - 1], deeper(step))

    def far(i):
        half_way = deep // 2 - lax.div(i + 1, 2)
        return jnp.where(lax.rem(i, 2) == 0, half_way, deep - half_way)

    def send3(i, carry):
        level3(far(i)).start()
        return carry

    lax.fori_loop(0, deep - 1, send3, 0)

    def take3(i, total):
        level3(i + 1).wait_recv()
        return total + r3[i].astype(f32)

    g3[z] = lax.fori_loop(0, deep - 1, take3, s3[z].astype(f32)).astype(bf16)

    def spread3(i, carry):
        back3(far(i)).start()
        return carry

    lax.fori_loop(0, deep - 1, spread3, 0)

    def got3(i, carry):
        back3(i + 1).wait_recv()
        return carry

    lax.fori_loop(0, deep - 1, got3, 0)
    for piece in range(deep):
        w3[piece * share : piece * share + tall] = g3[piece].astype(f32)

    def back2(half, step):
        spot = gathered.at[core, half, mine(half, 1), mine(half, 2)]
        return remote(spot, spot, d2s.at[half, step - 1], d2r.at[half, step - 1], along(half, 2, step))

    for half in range(2):
        gathered[core, half, mine(half, 1), mine(half, 2)] = w3[half * rows2 : (half + 1) * rows2].astype(bf16)
        for step in order:
            back2(half, step).start()

    def back_stem():
        return remote(stem_all.at[core], stem_all.at[core], h0s, h0r, sibling)

    stem_all[core] = w3[2 * rows2 : 2 * rows2 + 96].astype(bf16)
    back_stem().start()

    def back1(half, step):
        spot = gathered.at[core, half, mine(half, 1)]
        return remote(spot, spot, d1s.at[half, step - 1], d1r.at[half, step - 1], along(half, 1, step))

    def back0(half, step):
        spot = gathered.at[core, half, lax.rem(mine(half, 1) + ring - step, ring)]
        return remote(spot, spot, d0s.at[half, step], d0r.at[half, step], sibling)

    for half in range(2):
        for step in range(1, ring):
            back2(half, step).wait_recv()
        for step in order:
            back1(half, step).start()
        back0(half, 0).start()
    for step in near:
        for half in range(2):
            back1(half, step).wait_recv()
            back0(half, step).start()
    back_stem().wait()
    stem0().wait_send()
    for half in range(2):
        for step in range(ring):
            back0(half, step).wait()
            level0(half, step).wait_send()
        for step in range(1, ring):
            level1(half, step).wait_send()
            level2(half, step).wait_send()
            back2(half, step).wait_send()
            back1(half, step).wait_send()
    for step in range(1, ring):
        stem1(step).wait_send()
        stem2(step).wait_send()

    def sent3(i, carry):
        level3(i + 1).wait_send()
        back3(i + 1).wait_send()
        return carry

    lax.fori_loop(0, deep - 1, sent3, 0)


def main(ring, deep, high, vpos, vshift, codes, near_codes, cot, near_cot, stem_weight, weight):
    per = 4 // ring
    rows1 = per * C
    rows2 = rows1 // ring
    share = (2 * rows2 + 96) // deep
    tall = -(-share // 8) * 8
    count = 2 * (ring // high) * deep
    dma = pltpu.SemaphoreType.DMA
    halves = lambda *lead: pltpu.VMEM((2,) + lead, bf16)
    pair = lambda *dims: [dma(dims), dma(dims)]
    vmem = pl.BlockSpec(memory_space=pltpu.VMEM)
    smem = pl.BlockSpec(memory_space=pltpu.SMEM)
    return pl.pallas_call(
        functools.partial(main_kernel, ring, deep, high, count),
        out_shape=(
            jax.ShapeDtypeStruct((ROWS, C), bf16),
            jax.ShapeDtypeStruct((ROWS, C), bf16),
            jax.ShapeDtypeStruct((2, 2, ring, ring, rows2, 128), bf16),
            jax.ShapeDtypeStruct((2, 96, 128), bf16),
        ),
        in_specs=[smem, smem, vmem, vmem, vmem, vmem, vmem, pl.BlockSpec(memory_space=pl.ANY)],
        out_specs=(vmem,) * 4,
        scratch_shapes=[
            pltpu.VMEM((C, 5 * C), bf16),
            pltpu.VMEM((5 * C, C), bf16),
            dma((10,)),
            pltpu.VMEM((64, 2 * C), f32),
            pltpu.VMEM((TALL, 2 * C), f32),
            pltpu.VMEM((TALL, 2 * C), f32),
            pltpu.VMEM((TALL, C), f32),
            pltpu.VMEM((TALL, C), f32),
            pltpu.VMEM((TALL, C), f32),
            pltpu.VMEM((TALL, C), f32),
            pltpu.VMEM((ROWS, 2048), bf16),
            pltpu.VMEM((ROWS, 5 * C), bf16),
            pltpu.VMEM((64, ROWS), bf16),
            pltpu.VMEM((C, ROWS), bf16),
            pltpu.VMEM((ROWS, 2 * C), bf16),
            pltpu.VMEM((2, ring, rows1, 128), f32),
            halves(ring, rows1, 128),
            halves(ring, rows1, 128),
            halves(ring - 1, rows1, 128),
            halves(ring - 1, rows1, 128),
            pltpu.VMEM((2, ring, rows2, 128), f32),
            halves(ring, rows2, 128),
            halves(ring - 1, rows2, 128),
            pltpu.VMEM((96, 128), bf16),
            pltpu.VMEM((96, 128), bf16),
            pltpu.VMEM((192, 128), f32),
            pltpu.VMEM((96, 128), bf16),
            pltpu.VMEM((ring - 1, 96, 128), bf16),
            pltpu.VMEM((96, 128), bf16),
            pltpu.VMEM((ring - 1, 96, 128), bf16),
            pltpu.VMEM((2 * rows2 + 96 + tall, 128), f32),
            pltpu.VMEM((deep, tall, 128), bf16),
            pltpu.VMEM((deep - 1, tall, 128), bf16),
            pltpu.VMEM((deep, tall, 128), bf16),
            pltpu.VMEM((2 * rows2 + 96 + tall, 128), f32),
            *pair(2, ring), *pair(2, ring - 1), *pair(2, ring - 1), *pair(deep - 1),
            *pair(deep - 1), *pair(2, ring - 1), *pair(2, ring - 1), *pair(2, ring),
            *pair(), *pair(ring - 1), *pair(ring - 1), *pair(),
        ],
        compiler_params=pltpu.CompilerParams(
            collective_id=1, has_side_effects=True, vmem_limit_bytes=60 * 1024 * 1024
        ),
        name="block",
    )(vpos, vshift, codes, near_codes, cot, near_cot, stem_weight, weight)


def finish_kernel(summed, small, conv, stem):
    t = pl.program_id(0)
    for k in range(3):
        conv[0, :, k * 128 : (k + 1) * 128] = summed[3 * t + k].astype(f32)

    @pl.when(t == 0)
    def _():
        rows = jnp.concatenate([small[0], small[1]], axis=0).astype(f32)
        for k in range(3):
            for tap in range(15):
                stem[tap, :, k * 128 : (k + 1) * 128] = rows[k * 64 + 4 * tap : k * 64 + 4 * tap + 4]


def finish(summed, small):
    vmem = pl.BlockSpec(memory_space=pltpu.VMEM)
    return pl.pallas_call(
        finish_kernel,
        grid=(5,),
        out_shape=(
            jax.ShapeDtypeStruct((5, C, C), f32),
            jax.ShapeDtypeStruct((15, 4, C), f32),
        ),
        in_specs=[vmem, vmem],
        out_specs=(
            pl.BlockSpec((1, C, C), lambda t: (t, 0, 0)),
            pl.BlockSpec((15, 4, C), lambda t: (0, 0, 0)),
        ),
        name="finish",
    )(summed.reshape(16, C, 128), small)


def per_device(ring, deep, high, codes, variant_pos, variant_shift, stem_weight, conv_weight, cotangent):
    codes = codes.reshape(8, 128)
    cot = cotangent.reshape(ROWS, C)
    near_codes, near_cot = halo(2 * (ring // high) * deep, codes, cot)
    features, d_pooled, summed, small = main(
        ring, deep, high, variant_pos, variant_shift, codes, near_codes, cot, near_cot, stem_weight, conv_weight
    )
    conv_grad, stem_grad = finish(summed, small)
    return features[None], d_pooled[None], conv_grad, stem_grad


def build(mesh, ring, deep, high):
    placed = (P("dp", "context"), P("dp", None), P("dp", None), P(), P(), P("dp", "context", None))
    return jax.shard_map(
        functools.partial(per_device, ring, deep, high),
        mesh=mesh,
        in_specs=placed,
        out_specs=(P("dp", "context", None), P("dp", "context", None), P(), P()),
        check_vma=False,
    )


def solution(mesh):
    return build(mesh, 4, 16, 2)
```

```python
import functools
import math

import jax
import jax.numpy as jnp
from jax import lax
from jax.experimental import pallas as pl
from jax.experimental.pallas import tpu as pltpu
from jax.sharding import PartitionSpec as P

MESH = pl.DeviceIdType.MESH
f32, bf16 = jnp.float32, jnp.bfloat16
root_scale = math.sqrt(2.0 / math.pi)
cubic = 0.044715

C = 384
ROWS = 512
LEAD = 16
TALL = ROWS + 2 * LEAD
LANES = 640
PAIRS = 44


def places(ring, deep, high):
    low = ring // high
    dp, ctx = lax.axis_index("dp"), lax.axis_index("context")
    y, xh = lax.div(dp, high), lax.rem(dp, high)
    core, z = lax.rem(ctx, 2), lax.rem(lax.div(ctx, 2), deep)
    x = xh * low + lax.div(ctx, 2 * deep)

    def device(x, y, z, core):
        return {
            "dp": y * high + lax.div(x, low),
            "context": (lax.rem(x, low) * deep + z) * 2 + core,
        }

    return x, y, z, core, device


def remote(src, dst, send, recv, to):
    return pltpu.make_async_remote_copy(
        src_ref=src, dst_ref=dst, send_sem=send, recv_sem=recv, device_id=to, device_id_type=MESH
    )


def halo_kernel(count, codes, cot, near_codes, near_cot, sends, recvs):
    ctx = lax.axis_index("context")
    left = {"context": lax.rem(ctx + count - 1, count)}
    right = {"context": lax.rem(ctx + 1, count)}
    barrier = pltpu.get_barrier_semaphore()
    for to in (left, right):
        pl.semaphore_signal(barrier, inc=1, device_id=to, device_id_type=MESH)
    pl.semaphore_wait(barrier, 2)
    copies = [
        remote(codes, near_codes.at[0], sends.at[0], recvs.at[0], right),
        remote(codes, near_codes.at[1], sends.at[1], recvs.at[1], left),
        remote(cot.at[ROWS - LEAD : ROWS], near_cot.at[0], sends.at[2], recvs.at[2], right),
        remote(cot.at[0:LEAD], near_cot.at[1], sends.at[3], recvs.at[3], left),
    ]
    for copy in copies:
        copy.start()
    for copy in copies:
        copy.wait()


def halo(count, codes, cot):
    return pl.pallas_call(
        functools.partial(halo_kernel, count),
        out_shape=(
            jax.ShapeDtypeStruct((2, 8, 128), jnp.int32),
            jax.ShapeDtypeStruct((2, LEAD, C), bf16),
        ),
        in_specs=[pl.BlockSpec(memory_space=pltpu.HBM)] * 2,
        out_specs=(pl.BlockSpec(memory_space=pltpu.VMEM),) * 2,
        scratch_shapes=[pltpu.SemaphoreType.DMA((4,)), pltpu.SemaphoreType.DMA((4,))],
        compiler_params=pltpu.CompilerParams(
            collective_id=0, has_side_effects=True, vmem_limit_bytes=2 * 1024 * 1024
        ),
        name="halo",
    )(codes, cot)


def main_kernel(
    ring, deep, high, count,
    vpos_in, vshift_in, codes_in, near_codes, cot_in, near_cot, stem_weight_in, weight,
    features, d_pooled, gathered, stem_all,
    vpos, vshift, codes, cot, stem_weight, insem,
    wt, wf, wsem, ws, stem, slopes, cotx, gx, pooled, pslope, shifted, spread, wins_t, gated_t, dstem,
    own, s0, r0, s1, r1, a2, s2, r2,
    t0, u0, tsum, t1, u1, t2, u2,
    v3, s3, r3, g3, w3,
    c0s, c0r, c1s, c1r, c2s, c2r, c3s, c3r, d3s, d3r, d2s, d2r, d1s, d1r, d0s, d0r,
    e0s, e0r, e1s, e1r, e2s, e2r, h0s, h0r,
):
    x, y, z, core, device = places(ring, deep, high)
    ctx = lax.axis_index("context")
    other = 1 - core
    per = 4 // ring
    rows1 = per * C
    rows2 = rows1 // ring

    def along(half, level, step):
        if (half == 0) == (level == 1):
            return device(lax.rem(x + step, ring), y, z, core)
        return device(x, lax.rem(y + step, ring), z, core)

    def mine(half, level):
        return x if (half == 0) == (level == 1) else y

    def deeper(step):
        return device(x, y, lax.rem(z + step, deep), core)

    sibling = device(x, y, z, other)
    order = sorted(range(1, ring), key=lambda d: -min(d, ring - d))
    near = order[::-1]

    feeds = [
        pltpu.make_async_copy(source, target, insem.at[i])
        for i, (source, target) in enumerate(
            [(vpos_in, vpos), (vshift_in, vshift), (codes_in, codes), (stem_weight_in, stem_weight), (cot_in, cot)]
        )
    ]
    for feed in feeds:
        feed.start()
    barrier = pltpu.get_barrier_semaphore()
    pl.semaphore_signal(barrier, inc=1, device_id=sibling, device_id_type=MESH)

    def greet(step, carry):
        pl.semaphore_signal(barrier, inc=1, device_id=deeper(step), device_id_type=MESH)
        return carry

    lax.fori_loop(1, deep, greet, 0)
    for step in range(1, ring):
        for half in range(2):
            pl.semaphore_signal(barrier, inc=1, device_id=along(half, 1, step), device_id_type=MESH)

    loads = [pltpu.make_async_copy(weight.at[t], wt.at[:, t * C : (t + 1) * C], wsem.at[t]) for t in range(5)]
    loads += [pltpu.make_async_copy(weight.at[t], wf.at[t * C : (t + 1) * C], wsem.at[5 + t]) for t in range(5)]
    for load in loads:
        load.start()

    for feed in feeds[:3]:
        feed.wait()
    bases = jnp.concatenate(
        [near_codes[0, 7:8], codes[...], near_codes[1, 0:1], jnp.zeros((6, 128), jnp.int32)], axis=0
    )
    spot = (
        ctx * (2 * ROWS) - 128
        + 128 * lax.broadcasted_iota(jnp.int32, (16, 128), 0)
        + lax.broadcasted_iota(jnp.int32, (16, 128), 1)
    )
    for v in range(vpos.shape[1]):
        bases = bases + jnp.where(spot == vpos[0, v], vshift[0, v], 0)
    bases = jnp.where((spot >= 0) & (spot < count * (2 * ROWS)), bases & 3, 4)
    lane_in = lax.broadcasted_iota(jnp.int32, (128, 128), 0)
    lane_out = lax.broadcasted_iota(jnp.int32, (128, 128), 1)
    pick = (lane_in == 2 * (lane_out & 63) + lax.shift_right_logical(lane_out, 6)).astype(f32).astype(bf16)
    split = jnp.dot(bases.astype(f32).astype(bf16), pick, preferred_element_type=f32)
    turned = pltpu.roll(split, 64, 1)
    first = lax.broadcasted_iota(jnp.int32, (1, 128), 1) < 64
    evens, odds = [], []
    for p in range(5):
        evens.append(jnp.where(first, split[2 * p : 2 * p + 1], turned[2 * p + 1 : 2 * p + 2]))
        odds.append(jnp.where(first, turned[2 * p : 2 * p + 1], split[2 * p + 1 : 2 * p + 2]))
    even = jnp.broadcast_to(jnp.concatenate(evens, axis=1), (8, LANES))
    odd = jnp.broadcast_to(jnp.concatenate(odds, axis=1), (8, LANES))
    line = lax.broadcasted_iota(jnp.int32, (8, LANES), 0)
    both = jnp.where(line < 4, odd, pltpu.roll(even, LANES - 1, 1))
    hot = (both == (line & 3).astype(f32)).astype(f32)
    wide = [pltpu.roll(hot, LANES - (PAIRS + q), 1) for q in range(8)]
    windows_t = jnp.concatenate(wide + wide, axis=0)
    windows = windows_t.T[:TALL].astype(bf16)
    kept = jnp.concatenate(
        [pltpu.roll(hot, LANES - (PAIRS + LEAD + q), 1)[:, :ROWS] for q in range(8)], axis=0
    )
    wins_t[...] = kept.astype(bf16)

    feeds[3].wait()
    ws[...] = jnp.zeros_like(ws)
    for k in range(15):
        ws[4 * k : 4 * k + 4, 0:C] = stem_weight[k]
        ws[4 * k + 4 : 4 * k + 8, C:] = stem_weight[k]
    taps = ws[...]
    upper = taps.astype(bf16)
    lower = (taps - upper.astype(f32)).astype(bf16)
    stem[...] = jnp.dot(windows, jnp.concatenate([upper, lower], axis=0), preferred_element_type=f32)

    def bend(value):
        square = value * value
        inner = jnp.tanh(value * (root_scale + (root_scale * cubic) * square))
        active = 0.5 * value * (1.0 + inner)
        slope = 0.5 * (1.0 + inner) + 0.5 * value * (1.0 - inner * inner) * (
            root_scale + (3.0 * root_scale * cubic) * square
        )
        return active, slope

    def activate(i, carry):
        rows = pl.ds(pl.multiple_of(i * 16, 16), 16)
        active_e, slope_e = bend(stem[rows, 0:C])
        active_o, slope_o = bend(stem[rows, C:])
        slopes[rows, 0:C] = 0.5 * slope_e
        slopes[rows, C:] = 0.5 * slope_o
        pool = (0.5 * (active_e + active_o)).astype(bf16).astype(f32)
        pooled[rows] = pool
        gate, slope = bend(pool)
        gx[rows] = gate.astype(bf16).astype(f32)
        pslope[rows] = slope
        return carry

    lax.fori_loop(0, TALL // 16, activate, 0)
    inside_left = jnp.where(ctx > 0, 1.0, 0.0)
    inside_right = jnp.where(ctx < count - 1, 1.0, 0.0)
    gx[0:LEAD] = gx[0:LEAD] * inside_left
    gx[LEAD + ROWS :] = gx[LEAD + ROWS :] * inside_right
    cotx[0:LEAD] = near_cot[0].astype(f32) * inside_left
    cotx[LEAD + ROWS :] = near_cot[1].astype(f32) * inside_right
    feeds[4].wait()
    cotx[LEAD : LEAD + ROWS] = cot[...].astype(f32)
    gated_t[...] = gx[LEAD : LEAD + ROWS].T.astype(bf16)
    for t in range(5):
        shifted[:, t * C : (t + 1) * C] = cotx[LEAD + 2 - t : LEAD + 2 - t + ROWS].astype(bf16)
    shifted[:, 5 * C :] = jnp.zeros((ROWS, 128), bf16)

    pl.semaphore_wait(barrier, 1 + 2 * (ring - 1) + deep - 1)

    def level0(half, piece):
        return remote(
            s0.at[half, piece], r0.at[half, piece], c0s.at[half, piece], c0r.at[half, piece], sibling
        )

    def product(owner, j):
        at = pl.multiple_of(owner * 1024 + 256 * j, 256)
        return jnp.dot(gated_t[...], shifted[:, pl.ds(at, 256)], preferred_element_type=f32)

    for j in range(4):
        block = product(other, j)
        for k in range(2):
            half, sub = divmod(2 * j + k, 4)
            piece, sub = divmod(sub, per)
            s0[half, piece, sub * C : (sub + 1) * C] = block[:, 128 * k : 128 * (k + 1)].astype(bf16)
            if sub == per - 1:
                level0(half, piece).start()
    for j in range(4):
        block = product(core, j)
        for k in range(2):
            half, sub = divmod(2 * j + k, 4)
            piece, sub = divmod(sub, per)
            own[half, piece, sub * C : (sub + 1) * C] = block[:, 128 * k : 128 * (k + 1)]

    def level1(half, step):
        return remote(
            s1.at[half, step - 1], r1.at[half, step - 1], c1s.at[half, step - 1], c1r.at[half, step - 1],
            along(half, 1, step),
        )

    for half in range(2):
        for piece in range(ring):
            level0(half, piece).wait_recv()
    for step in order:
        for half in range(2):
            piece = lax.rem(mine(half, 1) + step, ring)
            s1[half, step - 1] = (own[half, piece] + r0[half, piece].astype(f32)).astype(bf16)
            level1(half, step).start()

    for load in loads:
        load.wait()
    for block in range(2):
        at = block * (ROWS // 2)
        rows = slice(at, at + ROWS // 2)
        more = slice(LEAD + at, LEAD + at + ROWS // 2)
        back = lax.dot_general(
            shifted[rows, : 5 * C], wt[...], (((1,), (1,)), ((), ())), preferred_element_type=f32
        )
        dpool = cotx[more] + back * pslope[more]
        d_pooled[rows] = dpool.astype(bf16)
        dstem[rows, 0:C] = (dpool * slopes[more, 0:C]).astype(bf16)
        dstem[rows, C:] = (dpool * slopes[more, C:]).astype(bf16)
    grad = jnp.dot(wins_t[...], dstem[...], preferred_element_type=f32)
    for k in range(3):
        tsum[k * 64 : k * 64 + 64] = grad[:, 128 * k : 128 * (k + 1)]
    for k in range(3):
        tsum[k * 64 : k * 64 + 60] = tsum[k * 64 : k * 64 + 60] + grad[4:64, C + 128 * k : C + 128 * (k + 1)]

    def stem0():
        return remote(t0, u0, e0s, e0r, sibling)

    t0[...] = tsum[pl.ds(pl.multiple_of(other * 96, 96), 96)].astype(bf16)
    stem0().start()

    for t in range(5):
        spread[:, t * C : (t + 1) * C] = gx[LEAD - 2 + t : LEAD - 2 + t + ROWS].astype(bf16)
    for block in range(2):
        at = block * (ROWS // 2)
        rows = slice(at, at + ROWS // 2)
        conv = jnp.dot(spread[rows], wf[...], preferred_element_type=f32)
        features[rows] = (pooled[LEAD + at : LEAD + at + ROWS // 2] + conv).astype(bf16)

    def stem1(step):
        return remote(t1, u1.at[step - 1], e1s.at[step - 1], e1r.at[step - 1], along(0, 1, step))

    def stem2(step):
        return remote(t2, u2.at[step - 1], e2s.at[step - 1], e2r.at[step - 1], along(0, 2, step))

    stem0().wait_recv()
    small = tsum[pl.ds(pl.multiple_of(core * 96, 96), 96)] + u0[...].astype(f32)
    t1[...] = small.astype(bf16)
    for step in order:
        stem1(step).start()

    def level2(half, step):
        return remote(
            s2.at[half, lax.rem(mine(half, 2) + step, ring)], r2.at[half, step - 1],
            c2s.at[half, step - 1], c2r.at[half, step - 1], along(half, 2, step),
        )

    for half in range(2):
        piece = mine(half, 1)
        total = own[half, piece] + r0[half, piece].astype(f32)
        for step in range(1, ring):
            level1(half, step).wait_recv()
            total = total + r1[half, step - 1].astype(f32)
        total = total.reshape(a2.shape[1:])
        a2[half] = total
        s2[half] = total.astype(bf16)
        for step in order:
            level2(half, step).start()

    for step in range(1, ring):
        stem1(step).wait_recv()
        small = small + u1[step - 1].astype(f32)
    t2[...] = small.astype(bf16)
    for step in order:
        stem2(step).start()

    for half in range(2):
        total = a2[half, mine(half, 2)]
        for step in range(1, ring):
            level2(half, step).wait_recv()
            total = total + r2[half, step - 1].astype(f32)
        v3[half * rows2 : (half + 1) * rows2] = total
    for step in range(1, ring):
        stem2(step).wait_recv()
        small = small + u2[step - 1].astype(f32)
    v3[2 * rows2 : 2 * rows2 + 96] = small
    share = (2 * rows2 + 96) // deep
    tall = s3.shape[1]
    for piece in range(deep):
        s3[piece] = v3[piece * share : piece * share + tall].astype(bf16)

    def level3(step):
        return remote(
            s3.at[lax.rem(z + step, deep)], r3.at[step - 1], c3s.at[step - 1], c3r.at[step - 1], deeper(step)
        )

    def back3(step):
        return remote(g3.at[z], g3.at[z], d3s.at[step - 1], d3r.at[step - 1], deeper(step))

    def far(i):
        half_way = deep // 2 - lax.div(i + 1, 2)
        return jnp.where(lax.rem(i, 2) == 0, half_way, deep - half_way)

    def send3(i, carry):
        level3(far(i)).start()
        return carry

    lax.fori_loop(0, deep - 1, send3, 0)

    def take3(i, total):
        level3(i + 1).wait_recv()
        return total + r3[i].astype(f32)

    g3[z] = lax.fori_loop(0, deep - 1, take3, s3[z].astype(f32)).astype(bf16)

    def spread3(i, carry):
        back3(far(i)).start()
        return carry

    lax.fori_loop(0, deep - 1, spread3, 0)

    def got3(i, carry):
        back3(i + 1).wait_recv()
        return carry

    lax.fori_loop(0, deep - 1, got3, 0)
    for piece in range(deep):
        w3[piece * share : piece * share + tall] = g3[piece].astype(f32)

    def back2(half, step):
        spot = gathered.at[core, half, mine(half, 1), mine(half, 2)]
        return remote(spot, spot, d2s.at[half, step - 1], d2r.at[half, step - 1], along(half, 2, step))

    for half in range(2):
        gathered[core, half, mine(half, 1), mine(half, 2)] = w3[half * rows2 : (half + 1) * rows2].astype(bf16)
        for step in order:
            back2(half, step).start()

    def back_stem():
        return remote(stem_all.at[core], stem_all.at[core], h0s, h0r, sibling)

    stem_all[core] = w3[2 * rows2 : 2 * rows2 + 96].astype(bf16)
    back_stem().start()

    def back1(half, step):
        spot = gathered.at[core, half, mine(half, 1)]
        return remote(spot, spot, d1s.at[half, step - 1], d1r.at[half, step - 1], along(half, 1, step))

    def back0(half, step):
        spot = gathered.at[core, half, lax.rem(mine(half, 1) + ring - step, ring)]
        return remote(spot, spot, d0s.at[half, step], d0r.at[half, step], sibling)

    for half in range(2):
        for step in range(1, ring):
            back2(half, step).wait_recv()
        for step in order:
            back1(half, step).start()
        back0(half, 0).start()
    for step in near:
        for half in range(2):
            back1(half, step).wait_recv()
            back0(half, step).start()
    back_stem().wait()
    stem0().wait_send()
    for half in range(2):
        for step in range(ring):
            back0(half, step).wait()
            level0(half, step).wait_send()
        for step in range(1, ring):
            level1(half, step).wait_send()
            level2(half, step).wait_send()
            back2(half, step).wait_send()
            back1(half, step).wait_send()
    for step in range(1, ring):
        stem1(step).wait_send()
        stem2(step).wait_send()

    def sent3(i, carry):
        level3(i + 1).wait_send()
        back3(i + 1).wait_send()
        return carry

    lax.fori_loop(0, deep - 1, sent3, 0)


def main(ring, deep, high, vpos, vshift, codes, near_codes, cot, near_cot, stem_weight, weight):
    per = 4 // ring
    rows1 = per * C
    rows2 = rows1 // ring
    share = (2 * rows2 + 96) // deep
    tall = -(-share // 8) * 8
    count = 2 * (ring // high) * deep
    dma = pltpu.SemaphoreType.DMA
    halves = lambda *lead: pltpu.VMEM((2,) + lead, bf16)
    pair = lambda *dims: [dma(dims), dma(dims)]
    vmem = pl.BlockSpec(memory_space=pltpu.VMEM)
    hbm = pl.BlockSpec(memory_space=pltpu.HBM)
    return pl.pallas_call(
        functools.partial(main_kernel, ring, deep, high, count),
        out_shape=(
            jax.ShapeDtypeStruct((ROWS, C), bf16),
            jax.ShapeDtypeStruct((ROWS, C), bf16),
            jax.ShapeDtypeStruct((2, 2, ring, ring, rows2, 128), bf16),
            jax.ShapeDtypeStruct((2, 96, 128), bf16),
        ),
        in_specs=[hbm, hbm, hbm, vmem, hbm, vmem, hbm, hbm],
        out_specs=(vmem,) * 4,
        scratch_shapes=[
            pltpu.SMEM(vpos.shape, jnp.int32),
            pltpu.SMEM(vshift.shape, jnp.int32),
            pltpu.VMEM((8, 128), jnp.int32),
            pltpu.VMEM((ROWS, C), bf16),
            pltpu.VMEM((15, 4, C), f32),
            dma((5,)),
            pltpu.VMEM((C, 5 * C), bf16),
            pltpu.VMEM((5 * C, C), bf16),
            dma((10,)),
            pltpu.VMEM((64, 2 * C), f32),
            pltpu.VMEM((TALL, 2 * C), f32),
            pltpu.VMEM((TALL, 2 * C), f32),
            pltpu.VMEM((TALL, C), f32),
            pltpu.VMEM((TALL, C), f32),
            pltpu.VMEM((TALL, C), f32),
            pltpu.VMEM((TALL, C), f32),
            pltpu.VMEM((ROWS, 2048), bf16),
            pltpu.VMEM((ROWS, 5 * C), bf16),
            pltpu.VMEM((64, ROWS), bf16),
            pltpu.VMEM((C, ROWS), bf16),
            pltpu.VMEM((ROWS, 2 * C), bf16),
            pltpu.VMEM((2, ring, rows1, 128), f32),
            halves(ring, rows1, 128),
            halves(ring, rows1, 128),
            halves(ring - 1, rows1, 128),
            halves(ring - 1, rows1, 128),
            pltpu.VMEM((2, ring, rows2, 128), f32),
            halves(ring, rows2, 128),
            halves(ring - 1, rows2, 128),
            pltpu.VMEM((96, 128), bf16),
            pltpu.VMEM((96, 128), bf16),
            pltpu.VMEM((192, 128), f32),
            pltpu.VMEM((96, 128), bf16),
            pltpu.VMEM((ring - 1, 96, 128), bf16),
            pltpu.VMEM((96, 128), bf16),
            pltpu.VMEM((ring - 1, 96, 128), bf16),
            pltpu.VMEM((2 * rows2 + 96 + tall, 128), f32),
            pltpu.VMEM((deep, tall, 128), bf16),
            pltpu.VMEM((deep - 1, tall, 128), bf16),
            pltpu.VMEM((deep, tall, 128), bf16),
            pltpu.VMEM((2 * rows2 + 96 + tall, 128), f32),
            *pair(2, ring), *pair(2, ring - 1), *pair(2, ring - 1), *pair(deep - 1),
            *pair(deep - 1), *pair(2, ring - 1), *pair(2, ring - 1), *pair(2, ring),
            *pair(), *pair(ring - 1), *pair(ring - 1), *pair(),
        ],
        compiler_params=pltpu.CompilerParams(
            collective_id=1, has_side_effects=True, vmem_limit_bytes=36 * 1024 * 1024
        ),
        name="block",
    )(vpos, vshift, codes, near_codes, cot, near_cot, stem_weight, weight)


def finish_kernel(summed, small, features, d_pooled, conv, stem, features_out, d_pooled_out, widened, sems):
    copies = [
        pltpu.make_async_copy(features, features_out, sems.at[5]),
        pltpu.make_async_copy(d_pooled, d_pooled_out, sems.at[6]),
    ]
    for t in range(5):
        for k in range(3):
            widened[t, :, k * 128 : (k + 1) * 128] = summed[3 * t + k].astype(f32)
        copies.append(pltpu.make_async_copy(widened.at[t], conv.at[t], sems.at[t]))
        copies[-1].start()
    for copy in copies[:2]:
        copy.start()
    rows = jnp.concatenate([small[0], small[1]], axis=0).astype(f32)
    for k in range(3):
        for tap in range(15):
            stem[tap, :, k * 128 : (k + 1) * 128] = rows[k * 64 + 4 * tap : k * 64 + 4 * tap + 4]
    for copy in copies:
        copy.wait()


def finish(summed, small, features, d_pooled):
    vmem = pl.BlockSpec(memory_space=pltpu.VMEM)
    apart = pl.BlockSpec(memory_space=pl.ANY)
    return pl.pallas_call(
        finish_kernel,
        out_shape=(
            jax.ShapeDtypeStruct((5, C, C), f32),
            jax.ShapeDtypeStruct((15, 4, C), f32),
            jax.ShapeDtypeStruct((ROWS, C), bf16),
            jax.ShapeDtypeStruct((ROWS, C), bf16),
        ),
        in_specs=[vmem] * 4,
        out_specs=(apart, vmem, apart, apart),
        scratch_shapes=[pltpu.VMEM((5, C, C), f32), pltpu.SemaphoreType.DMA((7,))],
        compiler_params=pltpu.CompilerParams(vmem_limit_bytes=8 * 1024 * 1024),
        name="finish",
    )(summed.reshape(16, C, 128), small, features, d_pooled)


def per_device(ring, deep, high, codes, variant_pos, variant_shift, stem_weight, conv_weight, cotangent):
    codes = codes.reshape(8, 128)
    cot = cotangent.reshape(ROWS, C)
    codes, cot, variant_pos, variant_shift, stem_weight, conv_weight = (
        pltpu.with_memory_space_constraint(array, pltpu.HBM)
        for array in (codes, cot, variant_pos, variant_shift, stem_weight, conv_weight)
    )
    near_codes, near_cot = halo(2 * (ring // high) * deep, codes, cot)
    features, d_pooled, summed, small = main(
        ring, deep, high, variant_pos, variant_shift, codes, near_codes, cot, near_cot, stem_weight, conv_weight
    )
    conv_grad, stem_grad, features, d_pooled = finish(summed, small, features, d_pooled)
    return features[None], d_pooled[None], conv_grad, stem_grad


def build(mesh, ring, deep, high):
    placed = (P("dp", "context"), P("dp", None), P("dp", None), P(), P(), P("dp", "context", None))
    return jax.shard_map(
        functools.partial(per_device, ring, deep, high),
        mesh=mesh,
        in_specs=placed,
        out_specs=(P("dp", "context", None), P("dp", "context", None), P(), P()),
        check_vma=False,
    )


def solution(mesh):
    return build(mesh, 4, 16, 2)
```

```python
import functools
import math

import jax
import jax.numpy as jnp
from jax import lax
from jax.experimental import pallas as pl
from jax.experimental.pallas import tpu as pltpu
from jax.sharding import PartitionSpec as P

MESH = pl.DeviceIdType.MESH
f32, bf16 = jnp.float32, jnp.bfloat16
root_scale = math.sqrt(2.0 / math.pi)
cubic = 0.044715

C = 384
ROWS = 512
LEAD = 16
TALL = ROWS + 2 * LEAD
LANES = 640
PAIRS = 44


def places(ring, deep, high):
    low = ring // high
    dp, ctx = lax.axis_index("dp"), lax.axis_index("context")
    y, xh = lax.div(dp, high), lax.rem(dp, high)
    core, z = lax.rem(ctx, 2), lax.rem(lax.div(ctx, 2), deep)
    x = xh * low + lax.div(ctx, 2 * deep)

    def device(x, y, z, core):
        return {
            "dp": y * high + lax.div(x, low),
            "context": (lax.rem(x, low) * deep + z) * 2 + core,
        }

    return x, y, z, core, device


def remote(src, dst, send, recv, to):
    return pltpu.make_async_remote_copy(
        src_ref=src, dst_ref=dst, send_sem=send, recv_sem=recv, device_id=to, device_id_type=MESH
    )


def halo_kernel(count, codes, cot, near_codes, near_cot, sends, recvs):
    ctx = lax.axis_index("context")
    left = {"context": lax.rem(ctx + count - 1, count)}
    right = {"context": lax.rem(ctx + 1, count)}
    barrier = pltpu.get_barrier_semaphore()
    for to in (left, right):
        pl.semaphore_signal(barrier, inc=1, device_id=to, device_id_type=MESH)
    pl.semaphore_wait(barrier, 2)
    copies = [
        remote(codes, near_codes.at[0], sends.at[0], recvs.at[0], right),
        remote(codes, near_codes.at[1], sends.at[1], recvs.at[1], left),
        remote(cot.at[ROWS - LEAD : ROWS], near_cot.at[0], sends.at[2], recvs.at[2], right),
        remote(cot.at[0:LEAD], near_cot.at[1], sends.at[3], recvs.at[3], left),
    ]
    for copy in copies:
        copy.start()
    for copy in copies:
        copy.wait()


def halo(count, codes, cot):
    return pl.pallas_call(
        functools.partial(halo_kernel, count),
        out_shape=(
            jax.ShapeDtypeStruct((2, 8, 128), jnp.int32),
            jax.ShapeDtypeStruct((2, LEAD, C), bf16),
        ),
        in_specs=[pl.BlockSpec(memory_space=pltpu.HBM)] * 2,
        out_specs=(pl.BlockSpec(memory_space=pltpu.VMEM),) * 2,
        scratch_shapes=[pltpu.SemaphoreType.DMA((4,)), pltpu.SemaphoreType.DMA((4,))],
        compiler_params=pltpu.CompilerParams(
            collective_id=0, has_side_effects=True, vmem_limit_bytes=2 * 1024 * 1024
        ),
        name="halo",
    )(codes, cot)


def main_kernel(
    ring, deep, high, count,
    vpos_in, vshift_in, codes_in, near_codes, cot_in, near_cot, stem_weight_in, weight,
    features, d_pooled, gathered, stem_all,
    vpos, vshift, codes, cot, stem_weight, insem,
    wt, wf, wsem, ws, stem, slopes, cotx, gx, pooled, pslope, shifted, spread, wins_t, gated_t, dstem,
    own, s0, r0, s1, r1, s2, r2,
    t0, u0, tsum, t1, u1, t2, u2,
    v3, s3, r3, g3, w3, v4, s4, r4, g4, w4,
    c0s, c0r, c1s, c1r, c2s, c2r, c3s, c3r, d3s, d3r, d2s, d2r, d1s, d1r, d0s, d0r,
    e0s, e0r, e1s, e1r, e2s, e2r, h0s, h0r, c4s, c4r, d4s, d4r,
):
    x, y, z, core, device = places(ring, deep, high)
    ctx = lax.axis_index("context")
    other = 1 - core
    per = 4 // ring
    rows1 = per * C
    rows2 = rows1 // ring

    def along(half, level, step):
        if (half == 0) == (level == 1):
            return device(lax.rem(x + step, ring), y, z, core)
        return device(x, lax.rem(y + step, ring), z, core)

    def mine(half, level):
        return x if (half == 0) == (level == 1) else y

    def deeper(step):
        return device(x, y, lax.rem(z + step, deep), core)

    sibling = device(x, y, z, other)
    order = sorted(range(1, ring), key=lambda d: -min(d, ring - d))
    near = order[::-1]

    feeds = [
        pltpu.make_async_copy(source, target, insem.at[i])
        for i, (source, target) in enumerate(
            [(vpos_in, vpos), (vshift_in, vshift), (codes_in, codes), (stem_weight_in, stem_weight), (cot_in, cot)]
        )
    ]
    for feed in feeds:
        feed.start()
    barrier = pltpu.get_barrier_semaphore()
    pl.semaphore_signal(barrier, inc=1, device_id=sibling, device_id_type=MESH)

    def greet(step, carry):
        pl.semaphore_signal(barrier, inc=1, device_id=deeper(step), device_id_type=MESH)
        return carry

    lax.fori_loop(1, deep, greet, 0)
    for step in range(1, ring):
        for half in range(2):
            pl.semaphore_signal(barrier, inc=1, device_id=along(half, 1, step), device_id_type=MESH)

    loads = [pltpu.make_async_copy(weight.at[t], wt.at[:, t * C : (t + 1) * C], wsem.at[t]) for t in range(5)]
    loads += [pltpu.make_async_copy(weight.at[t], wf.at[t * C : (t + 1) * C], wsem.at[5 + t]) for t in range(5)]
    for load in loads:
        load.start()

    for feed in feeds[:3]:
        feed.wait()
    bases = jnp.concatenate(
        [near_codes[0, 7:8], codes[...], near_codes[1, 0:1], jnp.zeros((6, 128), jnp.int32)], axis=0
    )
    spot = (
        ctx * (2 * ROWS) - 128
        + 128 * lax.broadcasted_iota(jnp.int32, (16, 128), 0)
        + lax.broadcasted_iota(jnp.int32, (16, 128), 1)
    )
    for v in range(vpos.shape[1]):
        bases = bases + jnp.where(spot == vpos[0, v], vshift[0, v], 0)
    bases = jnp.where((spot >= 0) & (spot < count * (2 * ROWS)), bases & 3, 4)
    lane_in = lax.broadcasted_iota(jnp.int32, (128, 128), 0)
    lane_out = lax.broadcasted_iota(jnp.int32, (128, 128), 1)
    pick = (lane_in == 2 * (lane_out & 63) + lax.shift_right_logical(lane_out, 6)).astype(f32).astype(bf16)
    split = jnp.dot(bases.astype(f32).astype(bf16), pick, preferred_element_type=f32)
    turned = pltpu.roll(split, 64, 1)
    first = lax.broadcasted_iota(jnp.int32, (1, 128), 1) < 64
    evens, odds = [], []
    for p in range(5):
        evens.append(jnp.where(first, split[2 * p : 2 * p + 1], turned[2 * p + 1 : 2 * p + 2]))
        odds.append(jnp.where(first, turned[2 * p : 2 * p + 1], split[2 * p + 1 : 2 * p + 2]))
    even = jnp.broadcast_to(jnp.concatenate(evens, axis=1), (8, LANES))
    odd = jnp.broadcast_to(jnp.concatenate(odds, axis=1), (8, LANES))
    line = lax.broadcasted_iota(jnp.int32, (8, LANES), 0)
    both = jnp.where(line < 4, odd, pltpu.roll(even, LANES - 1, 1))
    hot = (both == (line & 3).astype(f32)).astype(f32)
    wide = [pltpu.roll(hot, LANES - (PAIRS + q), 1) for q in range(8)]
    windows_t = jnp.concatenate(wide + wide, axis=0)
    windows = windows_t.T[:TALL].astype(bf16)
    kept = jnp.concatenate(
        [pltpu.roll(hot, LANES - (PAIRS + LEAD + q), 1)[:, :ROWS] for q in range(8)], axis=0
    )
    wins_t[...] = kept.astype(bf16)

    feeds[3].wait()
    ws[...] = jnp.zeros_like(ws)
    for k in range(15):
        ws[4 * k : 4 * k + 4, 0:C] = stem_weight[k]
        ws[4 * k + 4 : 4 * k + 8, C:] = stem_weight[k]
    taps = ws[...]
    upper = taps.astype(bf16)
    lower = (taps - upper.astype(f32)).astype(bf16)
    stem[...] = jnp.dot(windows, jnp.concatenate([upper, lower], axis=0), preferred_element_type=f32)

    def bend(value):
        square = value * value
        inner = jnp.tanh(value * (root_scale + (root_scale * cubic) * square))
        active = 0.5 * value * (1.0 + inner)
        slope = 0.5 * (1.0 + inner) + 0.5 * value * (1.0 - inner * inner) * (
            root_scale + (3.0 * root_scale * cubic) * square
        )
        return active, slope

    def activate(i, carry):
        rows = pl.ds(pl.multiple_of(i * 16, 16), 16)
        active_e, slope_e = bend(stem[rows, 0:C])
        active_o, slope_o = bend(stem[rows, C:])
        slopes[rows, 0:C] = 0.5 * slope_e
        slopes[rows, C:] = 0.5 * slope_o
        pool = (0.5 * (active_e + active_o)).astype(bf16).astype(f32)
        pooled[rows] = pool
        gate, slope = bend(pool)
        gx[rows] = gate.astype(bf16).astype(f32)
        pslope[rows] = slope
        return carry

    lax.fori_loop(0, TALL // 16, activate, 0)
    inside_left = jnp.where(ctx > 0, 1.0, 0.0)
    inside_right = jnp.where(ctx < count - 1, 1.0, 0.0)
    gx[0:LEAD] = gx[0:LEAD] * inside_left
    gx[LEAD + ROWS :] = gx[LEAD + ROWS :] * inside_right
    cotx[0:LEAD] = near_cot[0].astype(f32) * inside_left
    cotx[LEAD + ROWS :] = near_cot[1].astype(f32) * inside_right
    feeds[4].wait()
    cotx[LEAD : LEAD + ROWS] = cot[...].astype(f32)
    gated_t[...] = gx[LEAD : LEAD + ROWS].T.astype(bf16)
    for t in range(5):
        shifted[:, t * C : (t + 1) * C] = cotx[LEAD + 2 - t : LEAD + 2 - t + ROWS].astype(bf16)
    shifted[:, 5 * C :] = jnp.zeros((ROWS, 128), bf16)

    pl.semaphore_wait(barrier, 1 + 2 * (ring - 1) + deep - 1)

    def level0(half, piece):
        return remote(
            s0.at[half, piece], r0.at[half, piece], c0s.at[half, piece], c0r.at[half, piece], sibling
        )

    def product(owner, j):
        at = pl.multiple_of(owner * 1024 + 256 * j, 256)
        return jnp.dot(gated_t[...], shifted[:, pl.ds(at, 256)], preferred_element_type=f32)

    parts = C // rows2
    for j in range(4):
        block = product(other, j)
        for k in range(2):
            half, sub = divmod(2 * j + k, 4)
            piece, sub = divmod(sub, per)
            some = block[:, 128 * k : 128 * (k + 1)].reshape(parts, rows2, 128)
            s0[half, piece, sub * parts : (sub + 1) * parts] = some.astype(bf16)
            if sub == per - 1:
                level0(half, piece).start()
    for j in range(4):
        block = product(core, j)
        for k in range(2):
            half, sub = divmod(2 * j + k, 4)
            piece, sub = divmod(sub, per)
            some = block[:, 128 * k : 128 * (k + 1)].reshape(parts, rows2, 128)
            own[half, piece, sub * parts : (sub + 1) * parts] = some

    def ahead(half, level, step):
        return lax.rem(mine(half, level) + step, ring)

    def behind(half, level, step):
        return lax.rem(mine(half, level) + ring - step, ring)

    def level1(half, step, chunk):
        return remote(
            s1.at[half, step - 1, chunk], r1.at[half, step - 1, chunk],
            c1s.at[half, step - 1, chunk], c1r.at[half, step - 1, chunk], along(half, 1, step),
        )

    for half in range(2):
        for piece in range(ring):
            level0(half, piece).wait_recv()
    for chunk in order + [0]:
        for step in order:
            for half in range(2):
                at = ahead(half, 1, step), ahead(half, 2, chunk)
                s1[half, step - 1, chunk] = (own[half, at[0], at[1]] + r0[half, at[0], at[1]].astype(f32)).astype(bf16)
                level1(half, step, chunk).start()

    for load in loads:
        load.wait()
    for block in range(2):
        at = block * (ROWS // 2)
        rows = slice(at, at + ROWS // 2)
        more = slice(LEAD + at, LEAD + at + ROWS // 2)
        back = lax.dot_general(
            shifted[rows, : 5 * C], wt[...], (((1,), (1,)), ((), ())), preferred_element_type=f32
        )
        dpool = cotx[more] + back * pslope[more]
        d_pooled[rows] = dpool.astype(bf16)
        dstem[rows, 0:C] = (dpool * slopes[more, 0:C]).astype(bf16)
        dstem[rows, C:] = (dpool * slopes[more, C:]).astype(bf16)
    grad = jnp.dot(wins_t[...], dstem[...], preferred_element_type=f32)
    for k in range(3):
        tsum[k * 64 : k * 64 + 64] = grad[:, 128 * k : 128 * (k + 1)]
    for k in range(3):
        tsum[k * 64 : k * 64 + 60] = tsum[k * 64 : k * 64 + 60] + grad[4:64, C + 128 * k : C + 128 * (k + 1)]

    def stem0():
        return remote(t0, u0, e0s, e0r, sibling)

    t0[...] = tsum[pl.ds(pl.multiple_of(other * 96, 96), 96)].astype(bf16)
    stem0().start()

    for t in range(5):
        spread[:, t * C : (t + 1) * C] = gx[LEAD - 2 + t : LEAD - 2 + t + ROWS].astype(bf16)
    for block in range(2):
        at = block * (ROWS // 2)
        rows = slice(at, at + ROWS // 2)
        conv = jnp.dot(spread[rows], wf[...], preferred_element_type=f32)
        features[rows] = (pooled[LEAD + at : LEAD + at + ROWS // 2] + conv).astype(bf16)

    def stem1(step):
        return remote(t1, u1.at[step - 1], e1s.at[step - 1], e1r.at[step - 1], along(0, 1, step))

    def stem2(step):
        return remote(t2, u2.at[step - 1], e2s.at[step - 1], e2r.at[step - 1], along(0, 2, step))

    stem0().wait_recv()
    small = tsum[pl.ds(pl.multiple_of(core * 96, 96), 96)] + u0[...].astype(f32)
    t1[...] = small.astype(bf16)
    for step in order:
        stem1(step).start()

    def level2(half, step):
        return remote(
            s2.at[half, step - 1], r2.at[half, step - 1], c2s.at[half, step - 1], c2r.at[half, step - 1],
            along(half, 2, step),
        )

    for chunk in order + [0]:
        for half in range(2):
            at = mine(half, 1), ahead(half, 2, chunk)
            total = own[half, at[0], at[1]] + r0[half, at[0], at[1]].astype(f32)
            for step in range(1, ring):
                level1(half, step, chunk).wait_recv()
                total = total + r1[half, step - 1, chunk].astype(f32)
            if chunk:
                s2[half, chunk - 1] = total.astype(bf16)
                level2(half, chunk).start()
            else:
                v3[half * rows2 : (half + 1) * rows2] = total

    for step in range(1, ring):
        stem1(step).wait_recv()
        small = small + u1[step - 1].astype(f32)
    t2[...] = small.astype(bf16)
    for step in order:
        stem2(step).start()

    def far(i):
        half_way = deep // 2 - lax.div(i + 1, 2)
        return jnp.where(lax.rem(i, 2) == 0, half_way, deep - half_way)

    def down(send, land, sends, recvs):
        return lambda step: remote(
            send.at[lax.rem(z + step, deep)], land.at[step - 1], sends.at[step - 1], recvs.at[step - 1], deeper(step)
        )

    def up(all_of, sends, recvs):
        return lambda step: remote(all_of.at[z], all_of.at[z], sends.at[step - 1], recvs.at[step - 1], deeper(step))

    def start_all(copy):
        def one(i, carry):
            copy(far(i)).start()
            return carry

        lax.fori_loop(0, deep - 1, one, 0)

    def each(method, *copies):
        def one(i, carry):
            for copy in copies:
                getattr(copy(i + 1), method)()
            return carry

        lax.fori_loop(0, deep - 1, one, 0)

    def cut(source, send, share):
        for piece in range(deep):
            send[piece] = source[piece * share : piece * share + send.shape[1]].astype(bf16)

    def join(all_of, target, share):
        for piece in range(deep):
            target[piece * share : piece * share + all_of.shape[1]] = all_of[piece].astype(f32)

    def summed(copy, send, land):
        def one(i, total):
            copy(i + 1).wait_recv()
            return total + land[i].astype(f32)

        return lax.fori_loop(0, deep - 1, one, send[z].astype(f32)).astype(bf16)

    for half in range(2):
        total = v3[half * rows2 : (half + 1) * rows2]
        for step in near:
            level2(half, step).wait_recv()
            total = total + r2[half, step - 1].astype(f32)
        v3[half * rows2 : (half + 1) * rows2] = total
    conv_down, conv_up = down(s3, r3, c3s, c3r), up(g3, d3s, d3r)
    stem_down, stem_up = down(s4, r4, c4s, c4r), up(g4, d4s, d4r)
    cut(v3, s3, 2 * rows2 // deep)
    start_all(conv_down)
    for step in range(1, ring):
        stem2(step).wait_recv()
        small = small + u2[step - 1].astype(f32)
    v4[0:96] = small
    cut(v4, s4, 96 // deep)
    start_all(stem_down)
    g3[z] = summed(conv_down, s3, r3)
    start_all(conv_up)
    g4[z] = summed(stem_down, s4, r4)
    start_all(stem_up)
    each("wait_recv", conv_up)
    join(g3, w3, 2 * rows2 // deep)

    def back2(half, step):
        spot = gathered.at[core, half, mine(half, 1), mine(half, 2)]
        return remote(spot, spot, d2s.at[half, step - 1], d2r.at[half, step - 1], along(half, 2, step))

    def back1(half, step, chunk):
        spot = gathered.at[core, half, mine(half, 1), behind(half, 2, chunk)]
        return remote(spot, spot, d1s.at[half, step - 1, chunk], d1r.at[half, step - 1, chunk], along(half, 1, step))

    def back0(half, step, chunk):
        spot = gathered.at[core, half, behind(half, 1, step), behind(half, 2, chunk)]
        return remote(spot, spot, d0s.at[half, step, chunk], d0r.at[half, step, chunk], sibling)

    for half in range(2):
        gathered[core, half, mine(half, 1), mine(half, 2)] = w3[half * rows2 : (half + 1) * rows2].astype(bf16)
        for step in order:
            back2(half, step).start()
    for chunk in [0] + near:
        for half in range(2):
            if chunk:
                back2(half, chunk).wait_recv()
            for step in order:
                back1(half, step, chunk).start()
            back0(half, 0, chunk).start()

    each("wait_recv", stem_up)
    join(g4, w4, 96 // deep)

    def back_stem():
        return remote(stem_all.at[core], stem_all.at[core], h0s, h0r, sibling)

    stem_all[core] = w4[0:96].astype(bf16)
    back_stem().start()
    for chunk in [0] + near:
        for step in near:
            for half in range(2):
                back1(half, step, chunk).wait_recv()
                back0(half, step, chunk).start()
    back_stem().wait()
    stem0().wait_send()
    for half in range(2):
        for step in range(ring):
            level0(half, step).wait_send()
            for chunk in range(ring):
                back0(half, step, chunk).wait()
        for step in range(1, ring):
            level2(half, step).wait_send()
            back2(half, step).wait_send()
            for chunk in range(ring):
                level1(half, step, chunk).wait_send()
                back1(half, step, chunk).wait_send()
    for step in range(1, ring):
        stem1(step).wait_send()
        stem2(step).wait_send()
    each("wait_send", conv_down, conv_up, stem_down, stem_up)


def main(ring, deep, high, vpos, vshift, codes, near_codes, cot, near_cot, stem_weight, weight):
    per = 4 // ring
    rows1 = per * C
    rows2 = rows1 // ring
    talls = [-(-total // (8 * deep)) * 8 for total in (2 * rows2, 96)]
    count = 2 * (ring // high) * deep
    dma = pltpu.SemaphoreType.DMA
    halves = lambda *lead: pltpu.VMEM((2,) + lead, bf16)
    pair = lambda *dims: [dma(dims), dma(dims)]
    vmem = pl.BlockSpec(memory_space=pltpu.VMEM)
    hbm = pl.BlockSpec(memory_space=pltpu.HBM)
    return pl.pallas_call(
        functools.partial(main_kernel, ring, deep, high, count),
        out_shape=(
            jax.ShapeDtypeStruct((ROWS, C), bf16),
            jax.ShapeDtypeStruct((ROWS, C), bf16),
            jax.ShapeDtypeStruct((2, 2, ring, ring, rows2, 128), bf16),
            jax.ShapeDtypeStruct((2, 96, 128), bf16),
        ),
        in_specs=[hbm, hbm, hbm, vmem, hbm, vmem, hbm, hbm],
        out_specs=(vmem,) * 4,
        scratch_shapes=[
            pltpu.SMEM(vpos.shape, jnp.int32),
            pltpu.SMEM(vshift.shape, jnp.int32),
            pltpu.VMEM((8, 128), jnp.int32),
            pltpu.VMEM((ROWS, C), bf16),
            pltpu.VMEM((15, 4, C), f32),
            dma((5,)),
            pltpu.VMEM((C, 5 * C), bf16),
            pltpu.VMEM((5 * C, C), bf16),
            dma((10,)),
            pltpu.VMEM((64, 2 * C), f32),
            pltpu.VMEM((TALL, 2 * C), f32),
            pltpu.VMEM((TALL, 2 * C), f32),
            pltpu.VMEM((TALL, C), f32),
            pltpu.VMEM((TALL, C), f32),
            pltpu.VMEM((TALL, C), f32),
            pltpu.VMEM((TALL, C), f32),
            pltpu.VMEM((ROWS, 2048), bf16),
            pltpu.VMEM((ROWS, 5 * C), bf16),
            pltpu.VMEM((64, ROWS), bf16),
            pltpu.VMEM((C, ROWS), bf16),
            pltpu.VMEM((ROWS, 2 * C), bf16),
            pltpu.VMEM((2, ring, ring, rows2, 128), f32),
            halves(ring, ring, rows2, 128),
            halves(ring, ring, rows2, 128),
            halves(ring - 1, ring, rows2, 128),
            halves(ring - 1, ring, rows2, 128),
            halves(ring - 1, rows2, 128),
            halves(ring - 1, rows2, 128),
            pltpu.VMEM((96, 128), bf16),
            pltpu.VMEM((96, 128), bf16),
            pltpu.VMEM((192, 128), f32),
            pltpu.VMEM((96, 128), bf16),
            pltpu.VMEM((ring - 1, 96, 128), bf16),
            pltpu.VMEM((96, 128), bf16),
            pltpu.VMEM((ring - 1, 96, 128), bf16),
            *[
                scratch
                for tall, total in zip(talls, (2 * rows2, 96))
                for scratch in (
                    pltpu.VMEM((total + tall, 128), f32),
                    pltpu.VMEM((deep, tall, 128), bf16),
                    pltpu.VMEM((deep - 1, tall, 128), bf16),
                    pltpu.VMEM((deep, tall, 128), bf16),
                    pltpu.VMEM((total + tall, 128), f32),
                )
            ],
            *pair(2, ring), *pair(2, ring - 1, ring), *pair(2, ring - 1), *pair(deep - 1),
            *pair(deep - 1), *pair(2, ring - 1), *pair(2, ring - 1, ring), *pair(2, ring, ring),
            *pair(), *pair(ring - 1), *pair(ring - 1), *pair(),
            *pair(deep - 1), *pair(deep - 1),
        ],
        compiler_params=pltpu.CompilerParams(
            collective_id=1, has_side_effects=True, vmem_limit_bytes=36 * 1024 * 1024
        ),
        name="block",
    )(vpos, vshift, codes, near_codes, cot, near_cot, stem_weight, weight)


def finish_kernel(summed, small, features, d_pooled, conv, stem, features_out, d_pooled_out, widened, sems):
    copies = [
        pltpu.make_async_copy(features, features_out, sems.at[5]),
        pltpu.make_async_copy(d_pooled, d_pooled_out, sems.at[6]),
    ]
    for t in range(5):
        for k in range(3):
            widened[t, :, k * 128 : (k + 1) * 128] = summed[3 * t + k].astype(f32)
        copies.append(pltpu.make_async_copy(widened.at[t], conv.at[t], sems.at[t]))
        copies[-1].start()
    for copy in copies[:2]:
        copy.start()
    rows = jnp.concatenate([small[0], small[1]], axis=0).astype(f32)
    for k in range(3):
        for tap in range(15):
            stem[tap, :, k * 128 : (k + 1) * 128] = rows[k * 64 + 4 * tap : k * 64 + 4 * tap + 4]
    for copy in copies:
        copy.wait()


def finish(summed, small, features, d_pooled):
    vmem = pl.BlockSpec(memory_space=pltpu.VMEM)
    apart = pl.BlockSpec(memory_space=pl.ANY)
    return pl.pallas_call(
        finish_kernel,
        out_shape=(
            jax.ShapeDtypeStruct((5, C, C), f32),
            jax.ShapeDtypeStruct((15, 4, C), f32),
            jax.ShapeDtypeStruct((ROWS, C), bf16),
            jax.ShapeDtypeStruct((ROWS, C), bf16),
        ),
        in_specs=[vmem] * 4,
        out_specs=(apart, vmem, apart, apart),
        scratch_shapes=[pltpu.VMEM((5, C, C), f32), pltpu.SemaphoreType.DMA((7,))],
        compiler_params=pltpu.CompilerParams(vmem_limit_bytes=8 * 1024 * 1024),
        name="finish",
    )(summed.reshape(16, C, 128), small, features, d_pooled)


def per_device(ring, deep, high, codes, variant_pos, variant_shift, stem_weight, conv_weight, cotangent):
    codes = codes.reshape(8, 128)
    cot = cotangent.reshape(ROWS, C)
    codes, cot, variant_pos, variant_shift, stem_weight, conv_weight = (
        pltpu.with_memory_space_constraint(array, pltpu.HBM)
        for array in (codes, cot, variant_pos, variant_shift, stem_weight, conv_weight)
    )
    near_codes, near_cot = halo(2 * (ring // high) * deep, codes, cot)
    features, d_pooled, summed, small = main(
        ring, deep, high, variant_pos, variant_shift, codes, near_codes, cot, near_cot, stem_weight, conv_weight
    )
    conv_grad, stem_grad, features, d_pooled = finish(summed, small, features, d_pooled)
    return features[None], d_pooled[None], conv_grad, stem_grad


def build(mesh, ring, deep, high):
    placed = (P("dp", "context"), P("dp", None), P("dp", None), P(), P(), P("dp", "context", None))
    return jax.shard_map(
        functools.partial(per_device, ring, deep, high),
        mesh=mesh,
        in_specs=placed,
        out_specs=(P("dp", "context", None), P("dp", "context", None), P(), P()),
        check_vma=False,
    )


def solution(mesh):
    return build(mesh, 4, 16, 2)
```

```python
import functools
import math

import jax
import jax.numpy as jnp
from jax import lax
from jax.experimental import pallas as pl
from jax.experimental.pallas import tpu as pltpu
from jax.sharding import PartitionSpec as P

MESH = pl.DeviceIdType.MESH
f32, bf16 = jnp.float32, jnp.bfloat16
root_scale = math.sqrt(2.0 / math.pi)
cubic = 0.044715

C = 384
ROWS = 512
LEAD = 16
TALL = ROWS + 2 * LEAD
LANES = 640
PAIRS = 44


def places(ring, deep, high):
    low = ring // high
    dp, ctx = lax.axis_index("dp"), lax.axis_index("context")
    y, xh = lax.div(dp, high), lax.rem(dp, high)
    core, z = lax.rem(ctx, 2), lax.rem(lax.div(ctx, 2), deep)
    x = xh * low + lax.div(ctx, 2 * deep)

    def device(x, y, z, core):
        return {
            "dp": y * high + lax.div(x, low),
            "context": (lax.rem(x, low) * deep + z) * 2 + core,
        }

    return x, y, z, core, device


def remote(src, dst, send, recv, to):
    return pltpu.make_async_remote_copy(
        src_ref=src, dst_ref=dst, send_sem=send, recv_sem=recv, device_id=to, device_id_type=MESH
    )


def main_kernel(
    ring, deep, high, count,
    vpos_in, vshift_in, codes_in, cot_in, stem_weight_in, weight,
    features, d_pooled, gathered, stem_all,
    vpos, vshift, codes, cot, stem_weight, insem, near_codes, near_cot, hs, hr, known, wcat,
    wt, wf, wsem, ws, stem, slopes, cotx, gx, pooled, pslope, shifted, spread, wins_t, gated_t, dstem,
    own, s0, r0, s1, r1, s2, r2,
    t0, u0, tsum, t1, u1, t2, u2,
    v3, s3, r3, g3, w3, v4, s4, r4, g4, w4,
    c0s, c0r, c1s, c1r, c2s, c2r, c3s, c3r, d3s, d3r, d2s, d2r, d1s, d1r, d0s, d0r,
    e0s, e0r, e1s, e1r, e2s, e2r, h0s, h0r, c4s, c4r, d4s, d4r,
):
    x, y, z, core, device = places(ring, deep, high)
    ctx = lax.axis_index("context")
    other = 1 - core
    per = 4 // ring
    rows1 = per * C
    rows2 = rows1 // ring

    def along(half, level, step):
        if (half == 0) == (level == 1):
            return device(lax.rem(x + step, ring), y, z, core)
        return device(x, lax.rem(y + step, ring), z, core)

    def mine(half, level):
        return x if (half == 0) == (level == 1) else y

    def deeper(step):
        return device(x, y, lax.rem(z + step, deep), core)

    sibling = device(x, y, z, other)
    order = sorted(range(1, ring), key=lambda d: -min(d, ring - d))
    near = order[::-1]

    feeds = [
        pltpu.make_async_copy(source, target, insem.at[i])
        for i, (source, target) in enumerate(
            [(vpos_in, vpos), (vshift_in, vshift), (codes_in, codes), (stem_weight_in, stem_weight), (cot_in, cot)]
        )
    ]
    for feed in feeds:
        feed.start()
    loads = [pltpu.make_async_copy(weight.at[t], wt.at[:, t * C : (t + 1) * C], wsem.at[t]) for t in range(5)]
    loads += [pltpu.make_async_copy(weight.at[t], wf.at[t * C : (t + 1) * C], wsem.at[5 + t]) for t in range(5)]
    for load in loads:
        load.start()

    left = {"context": lax.rem(ctx + count - 1, count)}
    right = {"context": lax.rem(ctx + 1, count)}
    barrier = pltpu.get_barrier_semaphore()
    greeted = [left, right, deeper(1), deeper(deep - 1)]
    greeted += [along(half, 1, step) for step in range(1, ring) for half in range(2)]
    for to in greeted:
        pl.semaphore_signal(barrier, inc=1, device_id=to, device_id_type=MESH)

    ws[...] = jnp.zeros_like(ws)
    feeds[3].wait()
    for k in range(15):
        ws[4 * k : 4 * k + 4, 0:C] = stem_weight[k]
        ws[4 * k + 4 : 4 * k + 8, C:] = stem_weight[k]
    taps = ws[...]
    upper = taps.astype(bf16)
    wcat[0:64] = upper
    wcat[64:128] = (taps - upper.astype(f32)).astype(bf16)
    for i in (0, 1, 2, 4):
        feeds[i].wait()

    pl.semaphore_wait(barrier, len(greeted))
    halos = [
        remote(codes, near_codes.at[0], hs.at[0], hr.at[0], right),
        remote(codes, near_codes.at[1], hs.at[1], hr.at[1], left),
        remote(cot.at[ROWS - LEAD : ROWS], near_cot.at[0], hs.at[2], hr.at[2], right),
        remote(cot.at[0:LEAD], near_cot.at[1], hs.at[3], hr.at[3], left),
    ]
    for copy in halos:
        copy.start()
    reach = [1 << m for m in range(8) if (1 << m) < deep // 2]

    def tell(m):
        for step in (reach[m], deep - reach[m]):
            pl.semaphore_signal(known.at[m], inc=1, device_id=deeper(step), device_id_type=MESH)

    def learn(m):
        if m < len(reach):
            pl.semaphore_wait(known.at[m], 2)
            if m + 1 < len(reach):
                tell(m + 1)

    if reach:
        tell(0)

    cotx[LEAD : LEAD + ROWS] = cot[...].astype(f32)

    def shift_in(first, size):
        for t in range(5):
            at = LEAD + 2 - t + first
            shifted[first : first + size, t * C : (t + 1) * C] = cotx[at : at + size].astype(bf16)

    shift_in(LEAD, ROWS - 2 * LEAD)
    shifted[:, 5 * C :] = jnp.zeros((ROWS, 128), bf16)
    spot = (
        ctx * (2 * ROWS) - 128
        + 128 * lax.broadcasted_iota(jnp.int32, (16, 128), 0)
        + lax.broadcasted_iota(jnp.int32, (16, 128), 1)
    )
    moved = jnp.zeros((16, 128), jnp.int32)
    for v in range(vpos.shape[1]):
        moved = moved + jnp.where(spot == vpos[0, v], vshift[0, v], 0)

    for copy in halos:
        copy.wait_recv()
    learn(0)
    bases = moved + jnp.concatenate(
        [near_codes[0, 7:8], codes[...], near_codes[1, 0:1], jnp.zeros((6, 128), jnp.int32)], axis=0
    )
    bases = jnp.where((spot >= 0) & (spot < count * (2 * ROWS)), bases & 3, 4)
    lane_in = lax.broadcasted_iota(jnp.int32, (128, 128), 0)
    lane_out = lax.broadcasted_iota(jnp.int32, (128, 128), 1)
    pick = (lane_in == 2 * (lane_out & 63) + lax.shift_right_logical(lane_out, 6)).astype(f32).astype(bf16)
    split = jnp.dot(bases.astype(f32).astype(bf16), pick, preferred_element_type=f32)
    turned = pltpu.roll(split, 64, 1)
    first = lax.broadcasted_iota(jnp.int32, (1, 128), 1) < 64
    evens, odds = [], []
    for p in range(5):
        evens.append(jnp.where(first, split[2 * p : 2 * p + 1], turned[2 * p + 1 : 2 * p + 2]))
        odds.append(jnp.where(first, turned[2 * p : 2 * p + 1], split[2 * p + 1 : 2 * p + 2]))
    even = jnp.broadcast_to(jnp.concatenate(evens, axis=1), (8, LANES))
    odd = jnp.broadcast_to(jnp.concatenate(odds, axis=1), (8, LANES))
    line = lax.broadcasted_iota(jnp.int32, (8, LANES), 0)
    both = jnp.where(line < 4, odd, pltpu.roll(even, LANES - 1, 1))
    hot = (both == (line & 3).astype(f32)).astype(f32)
    wide = [pltpu.roll(hot, LANES - (PAIRS + q), 1) for q in range(8)]
    windows_t = jnp.concatenate(wide + wide, axis=0)
    windows = windows_t.T[:TALL].astype(bf16)
    kept = jnp.concatenate(
        [pltpu.roll(hot, LANES - (PAIRS + LEAD + q), 1)[:, :ROWS] for q in range(8)], axis=0
    )
    wins_t[...] = kept.astype(bf16)

    stem[...] = jnp.dot(windows, wcat[...], preferred_element_type=f32)

    def bend(value):
        square = value * value
        inner = jnp.tanh(value * (root_scale + (root_scale * cubic) * square))
        active = 0.5 * value * (1.0 + inner)
        slope = 0.5 * (1.0 + inner) + 0.5 * value * (1.0 - inner * inner) * (
            root_scale + (3.0 * root_scale * cubic) * square
        )
        return active, slope

    def activate(i, carry):
        rows = pl.ds(pl.multiple_of(i * 16, 16), 16)
        active_e, slope_e = bend(stem[rows, 0:C])
        active_o, slope_o = bend(stem[rows, C:])
        slopes[rows, 0:C] = 0.5 * slope_e
        slopes[rows, C:] = 0.5 * slope_o
        pool = (0.5 * (active_e + active_o)).astype(bf16).astype(f32)
        pooled[rows] = pool
        gate, slope = bend(pool)
        gx[rows] = gate.astype(bf16).astype(f32)
        pslope[rows] = slope
        return carry

    lax.fori_loop(0, TALL // 16, activate, 0)
    inside_left = jnp.where(ctx > 0, 1.0, 0.0)
    inside_right = jnp.where(ctx < count - 1, 1.0, 0.0)
    gx[0:LEAD] = gx[0:LEAD] * inside_left
    gx[LEAD + ROWS :] = gx[LEAD + ROWS :] * inside_right
    cotx[0:LEAD] = near_cot[0].astype(f32) * inside_left
    cotx[LEAD + ROWS :] = near_cot[1].astype(f32) * inside_right
    shift_in(0, LEAD)
    shift_in(ROWS - LEAD, LEAD)
    gated_t[...] = gx[LEAD : LEAD + ROWS].T.astype(bf16)

    def level0(half, piece):
        return remote(
            s0.at[half, piece], r0.at[half, piece], c0s.at[half, piece], c0r.at[half, piece], sibling
        )

    def product(owner, j):
        at = pl.multiple_of(owner * 1024 + 256 * j, 256)
        return jnp.dot(gated_t[...], shifted[:, pl.ds(at, 256)], preferred_element_type=f32)

    parts = C // rows2
    for j in range(4):
        block = product(other, j)
        for k in range(2):
            half, sub = divmod(2 * j + k, 4)
            piece, sub = divmod(sub, per)
            some = block[:, 128 * k : 128 * (k + 1)].reshape(parts, rows2, 128)
            s0[half, piece, sub * parts : (sub + 1) * parts] = some.astype(bf16)
            if sub == per - 1:
                level0(half, piece).start()
    for j in range(4):
        block = product(core, j)
        for k in range(2):
            half, sub = divmod(2 * j + k, 4)
            piece, sub = divmod(sub, per)
            some = block[:, 128 * k : 128 * (k + 1)].reshape(parts, rows2, 128)
            own[half, piece, sub * parts : (sub + 1) * parts] = some

    def ahead(half, level, step):
        return lax.rem(mine(half, level) + step, ring)

    def behind(half, level, step):
        return lax.rem(mine(half, level) + ring - step, ring)

    def level1(half, step, chunk):
        return remote(
            s1.at[half, step - 1, chunk], r1.at[half, step - 1, chunk],
            c1s.at[half, step - 1, chunk], c1r.at[half, step - 1, chunk], along(half, 1, step),
        )

    for half in range(2):
        for piece in range(ring):
            level0(half, piece).wait_recv()
    for chunk in order + [0]:
        for step in order:
            for half in range(2):
                at = ahead(half, 1, step), ahead(half, 2, chunk)
                s1[half, step - 1, chunk] = (own[half, at[0], at[1]] + r0[half, at[0], at[1]].astype(f32)).astype(bf16)
                level1(half, step, chunk).start()

    learn(1)
    for load in loads:
        load.wait()
    for block in range(2):
        at = block * (ROWS // 2)
        rows = slice(at, at + ROWS // 2)
        more = slice(LEAD + at, LEAD + at + ROWS // 2)
        back = lax.dot_general(
            shifted[rows, : 5 * C], wt[...], (((1,), (1,)), ((), ())), preferred_element_type=f32
        )
        dpool = cotx[more] + back * pslope[more]
        d_pooled[rows] = dpool.astype(bf16)
        dstem[rows, 0:C] = (dpool * slopes[more, 0:C]).astype(bf16)
        dstem[rows, C:] = (dpool * slopes[more, C:]).astype(bf16)
    grad = jnp.dot(wins_t[...], dstem[...], preferred_element_type=f32)
    for k in range(3):
        tsum[k * 64 : k * 64 + 64] = grad[:, 128 * k : 128 * (k + 1)]
    for k in range(3):
        tsum[k * 64 : k * 64 + 60] = tsum[k * 64 : k * 64 + 60] + grad[4:64, C + 128 * k : C + 128 * (k + 1)]

    def stem0():
        return remote(t0, u0, e0s, e0r, sibling)

    t0[...] = tsum[pl.ds(pl.multiple_of(other * 96, 96), 96)].astype(bf16)
    stem0().start()

    for t in range(5):
        spread[:, t * C : (t + 1) * C] = gx[LEAD - 2 + t : LEAD - 2 + t + ROWS].astype(bf16)
    for block in range(2):
        at = block * (ROWS // 2)
        rows = slice(at, at + ROWS // 2)
        conv = jnp.dot(spread[rows], wf[...], preferred_element_type=f32)
        features[rows] = (pooled[LEAD + at : LEAD + at + ROWS // 2] + conv).astype(bf16)

    def stem1(step):
        return remote(t1, u1.at[step - 1], e1s.at[step - 1], e1r.at[step - 1], along(0, 1, step))

    def stem2(step):
        return remote(t2, u2.at[step - 1], e2s.at[step - 1], e2r.at[step - 1], along(0, 2, step))

    stem0().wait_recv()
    small = tsum[pl.ds(pl.multiple_of(core * 96, 96), 96)] + u0[...].astype(f32)
    t1[...] = small.astype(bf16)
    for step in order:
        stem1(step).start()

    def level2(half, step):
        return remote(
            s2.at[half, step - 1], r2.at[half, step - 1], c2s.at[half, step - 1], c2r.at[half, step - 1],
            along(half, 2, step),
        )

    for chunk in order + [0]:
        for half in range(2):
            at = mine(half, 1), ahead(half, 2, chunk)
            total = own[half, at[0], at[1]] + r0[half, at[0], at[1]].astype(f32)
            for step in range(1, ring):
                level1(half, step, chunk).wait_recv()
                total = total + r1[half, step - 1, chunk].astype(f32)
            if chunk:
                s2[half, chunk - 1] = total.astype(bf16)
                level2(half, chunk).start()
            else:
                v3[half * rows2 : (half + 1) * rows2] = total

    for step in range(1, ring):
        stem1(step).wait_recv()
        small = small + u1[step - 1].astype(f32)
    t2[...] = small.astype(bf16)
    for step in order:
        stem2(step).start()

    def far(i):
        half_way = deep // 2 - lax.div(i + 1, 2)
        return jnp.where(lax.rem(i, 2) == 0, half_way, deep - half_way)

    def down(send, land, sends, recvs):
        return lambda step: remote(
            send.at[lax.rem(z + step, deep)], land.at[step - 1], sends.at[step - 1], recvs.at[step - 1], deeper(step)
        )

    def up(all_of, sends, recvs):
        return lambda step: remote(all_of.at[z], all_of.at[z], sends.at[step - 1], recvs.at[step - 1], deeper(step))

    def start_all(copy):
        def one(i, carry):
            copy(far(i)).start()
            return carry

        lax.fori_loop(0, deep - 1, one, 0)

    def each(method, *copies):
        def one(i, carry):
            for copy in copies:
                getattr(copy(i + 1), method)()
            return carry

        lax.fori_loop(0, deep - 1, one, 0)

    def cut(source, send, share):
        for piece in range(deep):
            send[piece] = source[piece * share : piece * share + send.shape[1]].astype(bf16)

    def join(all_of, target, share):
        for piece in range(deep):
            target[piece * share : piece * share + all_of.shape[1]] = all_of[piece].astype(f32)

    def summed(copy, send, land):
        def one(i, total):
            copy(i + 1).wait_recv()
            return total + land[i].astype(f32)

        return lax.fori_loop(0, deep - 1, one, send[z].astype(f32)).astype(bf16)

    for half in range(2):
        total = v3[half * rows2 : (half + 1) * rows2]
        for step in near:
            level2(half, step).wait_recv()
            total = total + r2[half, step - 1].astype(f32)
        v3[half * rows2 : (half + 1) * rows2] = total
    conv_down, conv_up = down(s3, r3, c3s, c3r), up(g3, d3s, d3r)
    stem_down, stem_up = down(s4, r4, c4s, c4r), up(g4, d4s, d4r)
    for m in range(2, len(reach)):
        learn(m)
    cut(v3, s3, 2 * rows2 // deep)
    start_all(conv_down)
    for step in range(1, ring):
        stem2(step).wait_recv()
        small = small + u2[step - 1].astype(f32)
    v4[0:96] = small
    cut(v4, s4, 96 // deep)
    start_all(stem_down)
    g3[z] = summed(conv_down, s3, r3)
    start_all(conv_up)
    g4[z] = summed(stem_down, s4, r4)
    start_all(stem_up)
    each("wait_recv", conv_up)
    join(g3, w3, 2 * rows2 // deep)

    def back2(half, step):
        spot = gathered.at[core, half, mine(half, 1), mine(half, 2)]
        return remote(spot, spot, d2s.at[half, step - 1], d2r.at[half, step - 1], along(half, 2, step))

    def back1(half, step, chunk):
        spot = gathered.at[core, half, mine(half, 1), behind(half, 2, chunk)]
        return remote(spot, spot, d1s.at[half, step - 1, chunk], d1r.at[half, step - 1, chunk], along(half, 1, step))

    def back0(half, step, chunk):
        spot = gathered.at[core, half, behind(half, 1, step), behind(half, 2, chunk)]
        return remote(spot, spot, d0s.at[half, step, chunk], d0r.at[half, step, chunk], sibling)

    for half in range(2):
        gathered[core, half, mine(half, 1), mine(half, 2)] = w3[half * rows2 : (half + 1) * rows2].astype(bf16)
        for step in order:
            back2(half, step).start()
    for chunk in [0] + near:
        for half in range(2):
            if chunk:
                back2(half, chunk).wait_recv()
            for step in order:
                back1(half, step, chunk).start()
            back0(half, 0, chunk).start()

    each("wait_recv", stem_up)
    join(g4, w4, 96 // deep)

    def back_stem():
        return remote(stem_all.at[core], stem_all.at[core], h0s, h0r, sibling)

    stem_all[core] = w4[0:96].astype(bf16)
    back_stem().start()
    for chunk in [0] + near:
        for step in near:
            for half in range(2):
                back1(half, step, chunk).wait_recv()
                back0(half, step, chunk).start()
    back_stem().wait()
    for copy in halos:
        copy.wait_send()
    stem0().wait_send()
    for half in range(2):
        for step in range(ring):
            level0(half, step).wait_send()
            for chunk in range(ring):
                back0(half, step, chunk).wait()
        for step in range(1, ring):
            level2(half, step).wait_send()
            back2(half, step).wait_send()
            for chunk in range(ring):
                level1(half, step, chunk).wait_send()
                back1(half, step, chunk).wait_send()
    for step in range(1, ring):
        stem1(step).wait_send()
        stem2(step).wait_send()
    each("wait_send", conv_down, conv_up, stem_down, stem_up)


def main(ring, deep, high, vpos, vshift, codes, cot, stem_weight, weight):
    per = 4 // ring
    rows1 = per * C
    rows2 = rows1 // ring
    talls = [-(-total // (8 * deep)) * 8 for total in (2 * rows2, 96)]
    count = 2 * (ring // high) * deep
    dma = pltpu.SemaphoreType.DMA
    halves = lambda *lead: pltpu.VMEM((2,) + lead, bf16)
    pair = lambda *dims: [dma(dims), dma(dims)]
    vmem = pl.BlockSpec(memory_space=pltpu.VMEM)
    hbm = pl.BlockSpec(memory_space=pltpu.HBM)
    return pl.pallas_call(
        functools.partial(main_kernel, ring, deep, high, count),
        out_shape=(
            jax.ShapeDtypeStruct((ROWS, C), bf16),
            jax.ShapeDtypeStruct((ROWS, C), bf16),
            jax.ShapeDtypeStruct((2, 2, ring, ring, rows2, 128), bf16),
            jax.ShapeDtypeStruct((2, 96, 128), bf16),
        ),
        in_specs=[hbm] * 6,
        out_specs=(vmem,) * 4,
        scratch_shapes=[
            pltpu.SMEM(vpos.shape, jnp.int32),
            pltpu.SMEM(vshift.shape, jnp.int32),
            pltpu.VMEM((8, 128), jnp.int32),
            pltpu.VMEM((ROWS, C), bf16),
            pltpu.VMEM((15, 4, C), f32),
            dma((5,)),
            pltpu.VMEM((2, 8, 128), jnp.int32),
            pltpu.VMEM((2, LEAD, C), bf16),
            *pair(4),
            pltpu.SemaphoreType.REGULAR((3,)),
            pltpu.VMEM((128, 2 * C), bf16),
            pltpu.VMEM((C, 5 * C), bf16),
            pltpu.VMEM((5 * C, C), bf16),
            dma((10,)),
            pltpu.VMEM((64, 2 * C), f32),
            pltpu.VMEM((TALL, 2 * C), f32),
            pltpu.VMEM((TALL, 2 * C), f32),
            pltpu.VMEM((TALL, C), f32),
            pltpu.VMEM((TALL, C), f32),
            pltpu.VMEM((TALL, C), f32),
            pltpu.VMEM((TALL, C), f32),
            pltpu.VMEM((ROWS, 2048), bf16),
            pltpu.VMEM((ROWS, 5 * C), bf16),
            pltpu.VMEM((64, ROWS), bf16),
            pltpu.VMEM((C, ROWS), bf16),
            pltpu.VMEM((ROWS, 2 * C), bf16),
            pltpu.VMEM((2, ring, ring, rows2, 128), f32),
            halves(ring, ring, rows2, 128),
            halves(ring, ring, rows2, 128),
            halves(ring - 1, ring, rows2, 128),
            halves(ring - 1, ring, rows2, 128),
            halves(ring - 1, rows2, 128),
            halves(ring - 1, rows2, 128),
            pltpu.VMEM((96, 128), bf16),
            pltpu.VMEM((96, 128), bf16),
            pltpu.VMEM((192, 128), f32),
            pltpu.VMEM((96, 128), bf16),
            pltpu.VMEM((ring - 1, 96, 128), bf16),
            pltpu.VMEM((96, 128), bf16),
            pltpu.VMEM((ring - 1, 96, 128), bf16),
            *[
                scratch
                for tall, total in zip(talls, (2 * rows2, 96))
                for scratch in (
                    pltpu.VMEM((total + tall, 128), f32),
                    pltpu.VMEM((deep, tall, 128), bf16),
                    pltpu.VMEM((deep - 1, tall, 128), bf16),
                    pltpu.VMEM((deep, tall, 128), bf16),
                    pltpu.VMEM((total + tall, 128), f32),
                )
            ],
            *pair(2, ring), *pair(2, ring - 1, ring), *pair(2, ring - 1), *pair(deep - 1),
            *pair(deep - 1), *pair(2, ring - 1), *pair(2, ring - 1, ring), *pair(2, ring, ring),
            *pair(), *pair(ring - 1), *pair(ring - 1), *pair(),
            *pair(deep - 1), *pair(deep - 1),
        ],
        compiler_params=pltpu.CompilerParams(
            collective_id=0, has_side_effects=True, vmem_limit_bytes=36 * 1024 * 1024
        ),
        name="block",
    )(vpos, vshift, codes, cot, stem_weight, weight)


def finish_kernel(summed, small, features, d_pooled, conv, stem, features_out, d_pooled_out, widened, sems):
    copies = [
        pltpu.make_async_copy(features, features_out, sems.at[5]),
        pltpu.make_async_copy(d_pooled, d_pooled_out, sems.at[6]),
    ]
    for t in range(5):
        for k in range(3):
            widened[t, :, k * 128 : (k + 1) * 128] = summed[3 * t + k].astype(f32)
        copies.append(pltpu.make_async_copy(widened.at[t], conv.at[t], sems.at[t]))
        copies[-1].start()
    for copy in copies[:2]:
        copy.start()
    rows = jnp.concatenate([small[0], small[1]], axis=0).astype(f32)
    for k in range(3):
        for tap in range(15):
            stem[tap, :, k * 128 : (k + 1) * 128] = rows[k * 64 + 4 * tap : k * 64 + 4 * tap + 4]
    for copy in copies:
        copy.wait()


def finish(summed, small, features, d_pooled):
    vmem = pl.BlockSpec(memory_space=pltpu.VMEM)
    apart = pl.BlockSpec(memory_space=pl.ANY)
    return pl.pallas_call(
        finish_kernel,
        out_shape=(
            jax.ShapeDtypeStruct((5, C, C), f32),
            jax.ShapeDtypeStruct((15, 4, C), f32),
            jax.ShapeDtypeStruct((ROWS, C), bf16),
            jax.ShapeDtypeStruct((ROWS, C), bf16),
        ),
        in_specs=[vmem] * 4,
        out_specs=(apart, vmem, apart, apart),
        scratch_shapes=[pltpu.VMEM((5, C, C), f32), pltpu.SemaphoreType.DMA((7,))],
        compiler_params=pltpu.CompilerParams(vmem_limit_bytes=8 * 1024 * 1024),
        name="finish",
    )(summed.reshape(16, C, 128), small, features, d_pooled)


def per_device(ring, deep, high, codes, variant_pos, variant_shift, stem_weight, conv_weight, cotangent):
    codes = codes.reshape(8, 128)
    cot = cotangent.reshape(ROWS, C)
    codes, cot, variant_pos, variant_shift, stem_weight, conv_weight = (
        pltpu.with_memory_space_constraint(array, pltpu.HBM)
        for array in (codes, cot, variant_pos, variant_shift, stem_weight, conv_weight)
    )
    features, d_pooled, summed, small = main(
        ring, deep, high, variant_pos, variant_shift, codes, cot, stem_weight, conv_weight
    )
    conv_grad, stem_grad, features, d_pooled = finish(summed, small, features, d_pooled)
    return features[None], d_pooled[None], conv_grad, stem_grad


def build(mesh, ring, deep, high):
    placed = (P("dp", "context"), P("dp", None), P("dp", None), P(), P(), P("dp", "context", None))
    return jax.shard_map(
        functools.partial(per_device, ring, deep, high),
        mesh=mesh,
        in_specs=placed,
        out_specs=(P("dp", "context", None), P("dp", "context", None), P(), P()),
        check_vma=False,
    )


def solution(mesh):
    return build(mesh, 4, 16, 2)
```

```python
import functools
import math

import jax
import jax.numpy as jnp
from jax import lax
from jax.experimental import pallas as pl
from jax.experimental.pallas import tpu as pltpu
from jax.sharding import PartitionSpec as P

MESH = pl.DeviceIdType.MESH
f32, bf16 = jnp.float32, jnp.bfloat16
root_scale = math.sqrt(2.0 / math.pi)
cubic = 0.044715

C = 384
ROWS = 512
LEAD = 16
TALL = ROWS + 2 * LEAD
LANES = 640
PAIRS = 44


def places(ring, deep, high):
    low = ring // high
    dp, ctx = lax.axis_index("dp"), lax.axis_index("context")
    y, xh = lax.div(dp, high), lax.rem(dp, high)
    core, z = lax.rem(ctx, 2), lax.rem(lax.div(ctx, 2), deep)
    x = xh * low + lax.div(ctx, 2 * deep)

    def device(x, y, z, core):
        return {
            "dp": y * high + lax.div(x, low),
            "context": (lax.rem(x, low) * deep + z) * 2 + core,
        }

    return x, y, z, core, device


def remote(src, dst, send, recv, to):
    return pltpu.make_async_remote_copy(
        src_ref=src, dst_ref=dst, send_sem=send, recv_sem=recv, device_id=to, device_id_type=MESH
    )


def main_kernel(
    ring, deep, high, count,
    vpos_in, vshift_in, codes_in, cot_in, stem_weight_in, weight,
    features, d_pooled, gathered, stem_all,
    vpos, vshift, codes, cot, stem_weight, insem, near_codes, near_cot, hs, hr, known, wcat,
    wt, wf, wsem, ws, stem, slopes, cotx, gx, pooled, pslope, shifted, spread, wins_t, gated_t, dstem,
    own, s0, r0, s1, r1, s2, r2,
    t0, u0, tsum, t1, u1, t2, u2,
    v3, s3, r3, g3, w3, v4, s4, r4, g4, w4,
    c0s, c0r, c1s, c1r, c2s, c2r, c3s, c3r, d3s, d3r, d2s, d2r, d1s, d1r, d0s, d0r,
    e0s, e0r, e1s, e1r, e2s, e2r, h0s, h0r, c4s, c4r, d4s, d4r,
):
    x, y, z, core, device = places(ring, deep, high)
    ctx = lax.axis_index("context")
    other = 1 - core
    per = 4 // ring
    rows1 = per * C
    rows2 = rows1 // ring

    def along(half, level, step):
        if (half == 0) == (level == 1):
            return device(lax.rem(x + step, ring), y, z, core)
        return device(x, lax.rem(y + step, ring), z, core)

    def mine(half, level):
        return x if (half == 0) == (level == 1) else y

    def deeper(step):
        return device(x, y, lax.rem(z + step, deep), core)

    sibling = device(x, y, z, other)
    order = sorted(range(1, ring), key=lambda d: -min(d, ring - d))
    near = order[::-1]

    feeds = [
        pltpu.make_async_copy(source, target, insem.at[i])
        for i, (source, target) in enumerate(
            [(vpos_in, vpos), (vshift_in, vshift), (codes_in, codes), (stem_weight_in, stem_weight), (cot_in, cot)]
        )
    ]
    for feed in feeds:
        feed.start()
    loads = [pltpu.make_async_copy(weight.at[t], wt.at[:, t * C : (t + 1) * C], wsem.at[t]) for t in range(5)]
    loads += [pltpu.make_async_copy(weight.at[t], wf.at[t * C : (t + 1) * C], wsem.at[5 + t]) for t in range(5)]
    left = {"context": lax.rem(ctx + count - 1, count)}
    right = {"context": lax.rem(ctx + 1, count)}
    barrier = pltpu.get_barrier_semaphore()
    greeted = [left, right, deeper(1), deeper(deep - 1)]
    greeted += [along(half, 1, step) for step in range(1, ring) for half in range(2)]
    for to in greeted:
        pl.semaphore_signal(barrier, inc=1, device_id=to, device_id_type=MESH)

    ws[...] = jnp.zeros_like(ws)
    feeds[3].wait()
    for k in range(15):
        ws[4 * k : 4 * k + 4, 0:C] = stem_weight[k]
        ws[4 * k + 4 : 4 * k + 8, C:] = stem_weight[k]
    taps = ws[...]
    upper = taps.astype(bf16)
    wcat[0:64] = upper
    wcat[64:128] = (taps - upper.astype(f32)).astype(bf16)
    for i in (0, 1, 2, 4):
        feeds[i].wait()

    pl.semaphore_wait(barrier, len(greeted))
    halos = [
        remote(codes, near_codes.at[0], hs.at[0], hr.at[0], right),
        remote(codes, near_codes.at[1], hs.at[1], hr.at[1], left),
        remote(cot.at[ROWS - LEAD : ROWS], near_cot.at[0], hs.at[2], hr.at[2], right),
        remote(cot.at[0:LEAD], near_cot.at[1], hs.at[3], hr.at[3], left),
    ]
    for copy in halos:
        copy.start()
    for load in loads:
        load.start()
    reach = [1 << m for m in range(8) if (1 << m) < deep // 2]

    def tell(m):
        for step in (reach[m], deep - reach[m]):
            pl.semaphore_signal(known.at[m], inc=1, device_id=deeper(step), device_id_type=MESH)

    def learn(m):
        if m < len(reach):
            pl.semaphore_wait(known.at[m], 2)
            if m + 1 < len(reach):
                tell(m + 1)

    if reach:
        tell(0)

    cotx[LEAD : LEAD + ROWS] = cot[...].astype(f32)

    def shift_in(first, size):
        for t in range(5):
            at = LEAD + 2 - t + first
            shifted[first : first + size, t * C : (t + 1) * C] = cotx[at : at + size].astype(bf16)

    shift_in(LEAD, ROWS - 2 * LEAD)
    shifted[:, 5 * C :] = jnp.zeros((ROWS, 128), bf16)
    spot = (
        ctx * (2 * ROWS) - 128
        + 128 * lax.broadcasted_iota(jnp.int32, (16, 128), 0)
        + lax.broadcasted_iota(jnp.int32, (16, 128), 1)
    )
    moved = jnp.zeros((16, 128), jnp.int32)
    for v in range(vpos.shape[1]):
        moved = moved + jnp.where(spot == vpos[0, v], vshift[0, v], 0)

    inside = (spot >= 0) & (spot < count * (2 * ROWS))
    lane_in = lax.broadcasted_iota(jnp.int32, (128, 128), 0)
    lane_out = lax.broadcasted_iota(jnp.int32, (128, 128), 1)
    pick = (lane_in == 2 * (lane_out & 63) + lax.shift_right_logical(lane_out, 6)).astype(f32).astype(bf16)
    first = lax.broadcasted_iota(jnp.int32, (1, 128), 1) < 64
    line = lax.broadcasted_iota(jnp.int32, (8, LANES), 0)

    def one_hot(before, after):
        bases = moved + jnp.concatenate([before, codes[...], after, jnp.zeros((6, 128), jnp.int32)], axis=0)
        bases = jnp.where(inside, bases & 3, 4)
        split = jnp.dot(bases.astype(f32).astype(bf16), pick, preferred_element_type=f32)
        turned = pltpu.roll(split, 64, 1)
        evens, odds = [], []
        for p in range(5):
            evens.append(jnp.where(first, split[2 * p : 2 * p + 1], turned[2 * p + 1 : 2 * p + 2]))
            odds.append(jnp.where(first, turned[2 * p : 2 * p + 1], split[2 * p + 1 : 2 * p + 2]))
        even = jnp.broadcast_to(jnp.concatenate(evens, axis=1), (8, LANES))
        odd = jnp.broadcast_to(jnp.concatenate(odds, axis=1), (8, LANES))
        both = jnp.where(line < 4, odd, pltpu.roll(even, LANES - 1, 1))
        return (both == (line & 3).astype(f32)).astype(f32)

    def windows_of(hot):
        wide = [pltpu.roll(hot, LANES - (PAIRS + q), 1) for q in range(8)]
        return jnp.concatenate(wide + wide, axis=0)

    def bend(value):
        square = value * value
        inner = jnp.tanh(value * (root_scale + (root_scale * cubic) * square))
        active = 0.5 * value * (1.0 + inner)
        slope = 0.5 * (1.0 + inner) + 0.5 * value * (1.0 - inner * inner) * (
            root_scale + (3.0 * root_scale * cubic) * square
        )
        return active, slope

    def activate(i, carry):
        rows = pl.ds(pl.multiple_of(i * 16, 16), 16)
        active_e, slope_e = bend(stem[rows, 0:C])
        active_o, slope_o = bend(stem[rows, C:])
        slopes[rows, 0:C] = 0.5 * slope_e
        slopes[rows, C:] = 0.5 * slope_o
        pool = (0.5 * (active_e + active_o)).astype(bf16).astype(f32)
        pooled[rows] = pool
        gate, slope = bend(pool)
        gx[rows] = gate.astype(bf16).astype(f32)
        pslope[rows] = slope
        return carry

    edge = 2 * LEAD
    blank = jnp.zeros((1, 128), jnp.int32)
    windows = windows_of(one_hot(blank, blank)).T[edge : TALL - edge].astype(bf16)
    stem[edge : TALL - edge] = jnp.dot(windows, wcat[...], preferred_element_type=f32)
    lax.fori_loop(edge // 16, (TALL - edge) // 16, activate, 0)

    for copy in halos:
        copy.wait_recv()
    learn(0)
    hot = one_hot(near_codes[0, 7:8], near_codes[1, 0:1])
    windows_t = windows_of(hot)
    ends = jnp.concatenate(
        [windows_t[:, 0:128].T[0:edge], windows_t[:, ROWS : ROWS + 128].T[0:edge]], axis=0
    ).astype(bf16)
    ends = jnp.dot(ends, wcat[...], preferred_element_type=f32)
    stem[0:edge] = ends[0:edge]
    stem[TALL - edge :] = ends[edge:]
    for i in (0, 1, TALL // 16 - 2, TALL // 16 - 1):
        activate(i, 0)
    inside_left = jnp.where(ctx > 0, 1.0, 0.0)
    inside_right = jnp.where(ctx < count - 1, 1.0, 0.0)
    gx[0:LEAD] = gx[0:LEAD] * inside_left
    gx[LEAD + ROWS :] = gx[LEAD + ROWS :] * inside_right
    cotx[0:LEAD] = near_cot[0].astype(f32) * inside_left
    cotx[LEAD + ROWS :] = near_cot[1].astype(f32) * inside_right
    shift_in(0, LEAD)
    shift_in(ROWS - LEAD, LEAD)
    gated_t[...] = gx[LEAD : LEAD + ROWS].T.astype(bf16)

    def level0(half, piece):
        return remote(
            s0.at[half, piece], r0.at[half, piece], c0s.at[half, piece], c0r.at[half, piece], sibling
        )

    def product(owner, j):
        at = pl.multiple_of(owner * 1024 + 256 * j, 256)
        return jnp.dot(gated_t[...], shifted[:, pl.ds(at, 256)], preferred_element_type=f32)

    parts = C // rows2
    for j in range(4):
        block = product(other, j)
        for k in range(2):
            half, sub = divmod(2 * j + k, 4)
            piece, sub = divmod(sub, per)
            some = block[:, 128 * k : 128 * (k + 1)].reshape(parts, rows2, 128)
            s0[half, piece, sub * parts : (sub + 1) * parts] = some.astype(bf16)
            if sub == per - 1:
                level0(half, piece).start()
    for j in range(4):
        block = product(core, j)
        for k in range(2):
            half, sub = divmod(2 * j + k, 4)
            piece, sub = divmod(sub, per)
            some = block[:, 128 * k : 128 * (k + 1)].reshape(parts, rows2, 128)
            own[half, piece, sub * parts : (sub + 1) * parts] = some

    def ahead(half, level, step):
        return lax.rem(mine(half, level) + step, ring)

    def behind(half, level, step):
        return lax.rem(mine(half, level) + ring - step, ring)

    def level1(half, step, chunk):
        return remote(
            s1.at[half, step - 1, chunk], r1.at[half, step - 1, chunk],
            c1s.at[half, step - 1, chunk], c1r.at[half, step - 1, chunk], along(half, 1, step),
        )

    for half in range(2):
        for piece in range(ring):
            level0(half, piece).wait_recv()
    for chunk in order + [0]:
        for step in order:
            for half in range(2):
                at = ahead(half, 1, step), ahead(half, 2, chunk)
                s1[half, step - 1, chunk] = (own[half, at[0], at[1]] + r0[half, at[0], at[1]].astype(f32)).astype(bf16)
                level1(half, step, chunk).start()

    learn(1)
    for load in loads:
        load.wait()
    for block in range(2):
        at = block * (ROWS // 2)
        rows = slice(at, at + ROWS // 2)
        more = slice(LEAD + at, LEAD + at + ROWS // 2)
        back = lax.dot_general(
            shifted[rows, : 5 * C], wt[...], (((1,), (1,)), ((), ())), preferred_element_type=f32
        )
        dpool = cotx[more] + back * pslope[more]
        d_pooled[rows] = dpool.astype(bf16)
        dstem[rows, 0:C] = (dpool * slopes[more, 0:C]).astype(bf16)
        dstem[rows, C:] = (dpool * slopes[more, C:]).astype(bf16)
    wins_t[...] = jnp.concatenate(
        [pltpu.roll(hot, LANES - (PAIRS + LEAD + q), 1)[:, :ROWS] for q in range(8)], axis=0
    ).astype(bf16)
    grad = jnp.dot(wins_t[...], dstem[...], preferred_element_type=f32)
    for k in range(3):
        tsum[k * 64 : k * 64 + 64] = grad[:, 128 * k : 128 * (k + 1)]
    for k in range(3):
        tsum[k * 64 : k * 64 + 60] = tsum[k * 64 : k * 64 + 60] + grad[4:64, C + 128 * k : C + 128 * (k + 1)]

    def stem0():
        return remote(t0, u0, e0s, e0r, sibling)

    t0[...] = tsum[pl.ds(pl.multiple_of(other * 96, 96), 96)].astype(bf16)
    stem0().start()

    for t in range(5):
        spread[:, t * C : (t + 1) * C] = gx[LEAD - 2 + t : LEAD - 2 + t + ROWS].astype(bf16)
    for block in range(2):
        at = block * (ROWS // 2)
        rows = slice(at, at + ROWS // 2)
        conv = jnp.dot(spread[rows], wf[...], preferred_element_type=f32)
        features[rows] = (pooled[LEAD + at : LEAD + at + ROWS // 2] + conv).astype(bf16)

    def stem1(step):
        return remote(t1, u1.at[step - 1], e1s.at[step - 1], e1r.at[step - 1], along(0, 1, step))

    def stem2(step):
        return remote(t2, u2.at[step - 1], e2s.at[step - 1], e2r.at[step - 1], along(0, 2, step))

    stem0().wait_recv()
    small = tsum[pl.ds(pl.multiple_of(core * 96, 96), 96)] + u0[...].astype(f32)
    t1[...] = small.astype(bf16)
    for step in order:
        stem1(step).start()

    def level2(half, step):
        return remote(
            s2.at[half, step - 1], r2.at[half, step - 1], c2s.at[half, step - 1], c2r.at[half, step - 1],
            along(half, 2, step),
        )

    for chunk in order + [0]:
        for half in range(2):
            at = mine(half, 1), ahead(half, 2, chunk)
            total = own[half, at[0], at[1]] + r0[half, at[0], at[1]].astype(f32)
            for step in range(1, ring):
                level1(half, step, chunk).wait_recv()
                total = total + r1[half, step - 1, chunk].astype(f32)
            if chunk:
                s2[half, chunk - 1] = total.astype(bf16)
                level2(half, chunk).start()
            else:
                v3[half * rows2 : (half + 1) * rows2] = total

    for step in range(1, ring):
        stem1(step).wait_recv()
        small = small + u1[step - 1].astype(f32)
    t2[...] = small.astype(bf16)
    for step in order:
        stem2(step).start()

    def far(i):
        half_way = deep // 2 - lax.div(i + 1, 2)
        return jnp.where(lax.rem(i, 2) == 0, half_way, deep - half_way)

    def down(send, land, sends, recvs):
        return lambda step: remote(
            send.at[lax.rem(z + step, deep)], land.at[step - 1], sends.at[step - 1], recvs.at[step - 1], deeper(step)
        )

    def up(all_of, sends, recvs):
        return lambda step: remote(all_of.at[z], all_of.at[z], sends.at[step - 1], recvs.at[step - 1], deeper(step))

    def start_all(copy):
        def one(i, carry):
            copy(far(i)).start()
            return carry

        lax.fori_loop(0, deep - 1, one, 0)

    def each(method, *copies):
        def one(i, carry):
            for copy in copies:
                getattr(copy(i + 1), method)()
            return carry

        lax.fori_loop(0, deep - 1, one, 0)

    def cut(source, send, share):
        for piece in range(deep):
            send[piece] = source[piece * share : piece * share + send.shape[1]].astype(bf16)

    def join(all_of, target, share):
        for piece in range(deep):
            target[piece * share : piece * share + all_of.shape[1]] = all_of[piece].astype(f32)

    def summed(copy, send, land):
        def one(i, total):
            copy(i + 1).wait_recv()
            return total + land[i].astype(f32)

        return lax.fori_loop(0, deep - 1, one, send[z].astype(f32)).astype(bf16)

    for half in range(2):
        total = v3[half * rows2 : (half + 1) * rows2]
        for step in near:
            level2(half, step).wait_recv()
            total = total + r2[half, step - 1].astype(f32)
        v3[half * rows2 : (half + 1) * rows2] = total
    conv_down, conv_up = down(s3, r3, c3s, c3r), up(g3, d3s, d3r)
    stem_down, stem_up = down(s4, r4, c4s, c4r), up(g4, d4s, d4r)
    for m in range(2, len(reach)):
        learn(m)
    cut(v3, s3, 2 * rows2 // deep)
    start_all(conv_down)
    for step in range(1, ring):
        stem2(step).wait_recv()
        small = small + u2[step - 1].astype(f32)
    v4[0:96] = small
    cut(v4, s4, 96 // deep)
    start_all(stem_down)
    g3[z] = summed(conv_down, s3, r3)
    start_all(conv_up)
    g4[z] = summed(stem_down, s4, r4)
    start_all(stem_up)
    each("wait_recv", conv_up)
    join(g3, w3, 2 * rows2 // deep)

    def back2(half, step):
        spot = gathered.at[core, half, mine(half, 1), mine(half, 2)]
        return remote(spot, spot, d2s.at[half, step - 1], d2r.at[half, step - 1], along(half, 2, step))

    def back1(half, step, chunk):
        spot = gathered.at[core, half, mine(half, 1), behind(half, 2, chunk)]
        return remote(spot, spot, d1s.at[half, step - 1, chunk], d1r.at[half, step - 1, chunk], along(half, 1, step))

    def back0(half, step, chunk):
        spot = gathered.at[core, half, behind(half, 1, step), behind(half, 2, chunk)]
        return remote(spot, spot, d0s.at[half, step, chunk], d0r.at[half, step, chunk], sibling)

    for half in range(2):
        gathered[core, half, mine(half, 1), mine(half, 2)] = w3[half * rows2 : (half + 1) * rows2].astype(bf16)
        for step in order:
            back2(half, step).start()
    for chunk in [0] + near:
        for half in range(2):
            if chunk:
                back2(half, chunk).wait_recv()
            for step in order:
                back1(half, step, chunk).start()
            back0(half, 0, chunk).start()

    each("wait_recv", stem_up)
    join(g4, w4, 96 // deep)

    def back_stem():
        return remote(stem_all.at[core], stem_all.at[core], h0s, h0r, sibling)

    stem_all[core] = w4[0:96].astype(bf16)
    back_stem().start()
    for chunk in [0] + near:
        for step in near:
            for half in range(2):
                back1(half, step, chunk).wait_recv()
                back0(half, step, chunk).start()
    back_stem().wait()
    for copy in halos:
        copy.wait_send()
    stem0().wait_send()
    for half in range(2):
        for step in range(ring):
            level0(half, step).wait_send()
            for chunk in range(ring):
                back0(half, step, chunk).wait()
        for step in range(1, ring):
            level2(half, step).wait_send()
            back2(half, step).wait_send()
            for chunk in range(ring):
                level1(half, step, chunk).wait_send()
                back1(half, step, chunk).wait_send()
    for step in range(1, ring):
        stem1(step).wait_send()
        stem2(step).wait_send()
    each("wait_send", conv_down, conv_up, stem_down, stem_up)


def main(ring, deep, high, vpos, vshift, codes, cot, stem_weight, weight):
    per = 4 // ring
    rows1 = per * C
    rows2 = rows1 // ring
    talls = [-(-total // (8 * deep)) * 8 for total in (2 * rows2, 96)]
    count = 2 * (ring // high) * deep
    dma = pltpu.SemaphoreType.DMA
    halves = lambda *lead: pltpu.VMEM((2,) + lead, bf16)
    pair = lambda *dims: [dma(dims), dma(dims)]
    vmem = pl.BlockSpec(memory_space=pltpu.VMEM)
    hbm = pl.BlockSpec(memory_space=pltpu.HBM)
    return pl.pallas_call(
        functools.partial(main_kernel, ring, deep, high, count),
        out_shape=(
            jax.ShapeDtypeStruct((ROWS, C), bf16),
            jax.ShapeDtypeStruct((ROWS, C), bf16),
            jax.ShapeDtypeStruct((2, 2, ring, ring, rows2, 128), bf16),
            jax.ShapeDtypeStruct((2, 96, 128), bf16),
        ),
        in_specs=[hbm] * 6,
        out_specs=(vmem,) * 4,
        scratch_shapes=[
            pltpu.SMEM(vpos.shape, jnp.int32),
            pltpu.SMEM(vshift.shape, jnp.int32),
            pltpu.VMEM((8, 128), jnp.int32),
            pltpu.VMEM((ROWS, C), bf16),
            pltpu.VMEM((15, 4, C), f32),
            dma((5,)),
            pltpu.VMEM((2, 8, 128), jnp.int32),
            pltpu.VMEM((2, LEAD, C), bf16),
            *pair(4),
            pltpu.SemaphoreType.REGULAR((3,)),
            pltpu.VMEM((128, 2 * C), bf16),
            pltpu.VMEM((C, 5 * C), bf16),
            pltpu.VMEM((5 * C, C), bf16),
            dma((10,)),
            pltpu.VMEM((64, 2 * C), f32),
            pltpu.VMEM((TALL, 2 * C), f32),
            pltpu.VMEM((TALL, 2 * C), f32),
            pltpu.VMEM((TALL, C), f32),
            pltpu.VMEM((TALL, C), f32),
            pltpu.VMEM((TALL, C), f32),
            pltpu.VMEM((TALL, C), f32),
            pltpu.VMEM((ROWS, 2048), bf16),
            pltpu.VMEM((ROWS, 5 * C), bf16),
            pltpu.VMEM((64, ROWS), bf16),
            pltpu.VMEM((C, ROWS), bf16),
            pltpu.VMEM((ROWS, 2 * C), bf16),
            pltpu.VMEM((2, ring, ring, rows2, 128), f32),
            halves(ring, ring, rows2, 128),
            halves(ring, ring, rows2, 128),
            halves(ring - 1, ring, rows2, 128),
            halves(ring - 1, ring, rows2, 128),
            halves(ring - 1, rows2, 128),
            halves(ring - 1, rows2, 128),
            pltpu.VMEM((96, 128), bf16),
            pltpu.VMEM((96, 128), bf16),
            pltpu.VMEM((192, 128), f32),
            pltpu.VMEM((96, 128), bf16),
            pltpu.VMEM((ring - 1, 96, 128), bf16),
            pltpu.VMEM((96, 128), bf16),
            pltpu.VMEM((ring - 1, 96, 128), bf16),
            *[
                scratch
                for tall, total in zip(talls, (2 * rows2, 96))
                for scratch in (
                    pltpu.VMEM((total + tall, 128), f32),
                    pltpu.VMEM((deep, tall, 128), bf16),
                    pltpu.VMEM((deep - 1, tall, 128), bf16),
                    pltpu.VMEM((deep, tall, 128), bf16),
                    pltpu.VMEM((total + tall, 128), f32),
                )
            ],
            *pair(2, ring), *pair(2, ring - 1, ring), *pair(2, ring - 1), *pair(deep - 1),
            *pair(deep - 1), *pair(2, ring - 1), *pair(2, ring - 1, ring), *pair(2, ring, ring),
            *pair(), *pair(ring - 1), *pair(ring - 1), *pair(),
            *pair(deep - 1), *pair(deep - 1),
        ],
        compiler_params=pltpu.CompilerParams(
            collective_id=0, has_side_effects=True, vmem_limit_bytes=36 * 1024 * 1024
        ),
        name="block",
    )(vpos, vshift, codes, cot, stem_weight, weight)


def finish_kernel(summed, small, features, d_pooled, conv, stem, features_out, d_pooled_out, widened, sems):
    copies = [
        pltpu.make_async_copy(features, features_out, sems.at[5]),
        pltpu.make_async_copy(d_pooled, d_pooled_out, sems.at[6]),
    ]
    for t in range(5):
        for k in range(3):
            widened[t, :, k * 128 : (k + 1) * 128] = summed[3 * t + k].astype(f32)
        copies.append(pltpu.make_async_copy(widened.at[t], conv.at[t], sems.at[t]))
        copies[-1].start()
    for copy in copies[:2]:
        copy.start()
    rows = jnp.concatenate([small[0], small[1]], axis=0).astype(f32)
    for k in range(3):
        for tap in range(15):
            stem[tap, :, k * 128 : (k + 1) * 128] = rows[k * 64 + 4 * tap : k * 64 + 4 * tap + 4]
    for copy in copies:
        copy.wait()


def finish(summed, small, features, d_pooled):
    vmem = pl.BlockSpec(memory_space=pltpu.VMEM)
    apart = pl.BlockSpec(memory_space=pl.ANY)
    return pl.pallas_call(
        finish_kernel,
        out_shape=(
            jax.ShapeDtypeStruct((5, C, C), f32),
            jax.ShapeDtypeStruct((15, 4, C), f32),
            jax.ShapeDtypeStruct((ROWS, C), bf16),
            jax.ShapeDtypeStruct((ROWS, C), bf16),
        ),
        in_specs=[vmem] * 4,
        out_specs=(apart, vmem, apart, apart),
        scratch_shapes=[pltpu.VMEM((5, C, C), f32), pltpu.SemaphoreType.DMA((7,))],
        compiler_params=pltpu.CompilerParams(vmem_limit_bytes=8 * 1024 * 1024),
        name="finish",
    )(summed.reshape(16, C, 128), small, features, d_pooled)


def per_device(ring, deep, high, codes, variant_pos, variant_shift, stem_weight, conv_weight, cotangent):
    codes = codes.reshape(8, 128)
    cot = cotangent.reshape(ROWS, C)
    codes, cot, variant_pos, variant_shift, stem_weight, conv_weight = (
        pltpu.with_memory_space_constraint(array, pltpu.HBM)
        for array in (codes, cot, variant_pos, variant_shift, stem_weight, conv_weight)
    )
    features, d_pooled, summed, small = main(
        ring, deep, high, variant_pos, variant_shift, codes, cot, stem_weight, conv_weight
    )
    conv_grad, stem_grad, features, d_pooled = finish(summed, small, features, d_pooled)
    return features[None], d_pooled[None], conv_grad, stem_grad


def build(mesh, ring, deep, high):
    placed = (P("dp", "context"), P("dp", None), P("dp", None), P(), P(), P("dp", "context", None))
    return jax.shard_map(
        functools.partial(per_device, ring, deep, high),
        mesh=mesh,
        in_specs=placed,
        out_specs=(P("dp", "context", None), P("dp", "context", None), P(), P()),
        check_vma=False,
    )


def solution(mesh):
    return build(mesh, 4, 16, 2)
```

```python
import functools
import math

import jax
import jax.numpy as jnp
from jax import lax
from jax.experimental import pallas as pl
from jax.experimental.pallas import tpu as pltpu
from jax.sharding import PartitionSpec as P

MESH = pl.DeviceIdType.MESH
f32, bf16 = jnp.float32, jnp.bfloat16
root_scale = math.sqrt(2.0 / math.pi)
cubic = 0.044715

C = 384
ROWS = 512
LEAD = 16
TALL = ROWS + 2 * LEAD
LANES = 640
PAIRS = 44


def places(ring, deep, high):
    low = ring // high
    dp, ctx = lax.axis_index("dp"), lax.axis_index("context")
    y, xh = lax.div(dp, high), lax.rem(dp, high)
    core, z = lax.rem(ctx, 2), lax.rem(lax.div(ctx, 2), deep)
    x = xh * low + lax.div(ctx, 2 * deep)

    def device(x, y, z, core):
        return {
            "dp": y * high + lax.div(x, low),
            "context": (lax.rem(x, low) * deep + z) * 2 + core,
        }

    return x, y, z, core, device


def remote(src, dst, send, recv, to):
    return pltpu.make_async_remote_copy(
        src_ref=src, dst_ref=dst, send_sem=send, recv_sem=recv, device_id=to, device_id_type=MESH
    )


def main_kernel(
    ring, deep, high, count,
    vpos_in, vshift_in, codes_in, cot_in, stem_weight_in, weight,
    features, d_pooled, gathered, stem_all,
    vpos, vshift, codes, cot, stem_weight, insem, near_codes, near_cot, hs, hr, known, wcat,
    wt, wf, wsem, ws, stem, slopes, cotx, gx, pooled, pslope, shifted, spread, wins_t, gated_t, dstem,
    own, s0, r0, s1, r1, s2, r2,
    t0, u0, tsum, t1, u1, t2, u2,
    v3a, s3a, r3a, g3a, w3a, v3b, s3b, r3b, g3b, w3b, v4, s4, r4, g4, w4,
    c0s, c0r, c1s, c1r, c2s, c2r, c3sa, c3ra, d3sa, d3ra, d2s, d2r, d1s, d1r, d0s, d0r,
    e0s, e0r, e1s, e1r, e2s, e2r, h0s, h0r, c4s, c4r, d4s, d4r, c3sb, c3rb, d3sb, d3rb,
):
    x, y, z, core, device = places(ring, deep, high)
    v3, s3, r3, g3, w3 = (v3a, v3b), (s3a, s3b), (r3a, r3b), (g3a, g3b), (w3a, w3b)
    c3s, c3r, d3s, d3r = (c3sa, c3sb), (c3ra, c3rb), (d3sa, d3sb), (d3ra, d3rb)
    ctx = lax.axis_index("context")
    other = 1 - core
    per = 4 // ring
    rows1 = per * C
    rows2 = rows1 // ring
    rows3 = rows2 // 2

    def along(half, level, step):
        if (half == 0) == (level == 1):
            return device(lax.rem(x + step, ring), y, z, core)
        return device(x, lax.rem(y + step, ring), z, core)

    def mine(half, level):
        return x if (half == 0) == (level == 1) else y

    def deeper(step):
        return device(x, y, lax.rem(z + step, deep), core)

    sibling = device(x, y, z, other)
    order = sorted(range(1, ring), key=lambda d: -min(d, ring - d))
    near = order[::-1]

    feeds = [
        pltpu.make_async_copy(source, target, insem.at[i])
        for i, (source, target) in enumerate(
            [(vpos_in, vpos), (vshift_in, vshift), (codes_in, codes), (stem_weight_in, stem_weight), (cot_in, cot)]
        )
    ]
    for feed in feeds:
        feed.start()
    loads = [pltpu.make_async_copy(weight.at[t], wt.at[:, t * C : (t + 1) * C], wsem.at[t]) for t in range(5)]
    loads += [pltpu.make_async_copy(weight.at[t], wf.at[t * C : (t + 1) * C], wsem.at[5 + t]) for t in range(5)]
    left = {"context": lax.rem(ctx + count - 1, count)}
    right = {"context": lax.rem(ctx + 1, count)}
    barrier = pltpu.get_barrier_semaphore()
    greeted = [left, right, deeper(1), deeper(deep - 1)]
    greeted += [along(half, 1, step) for step in range(1, ring) for half in range(2)]
    for to in greeted:
        pl.semaphore_signal(barrier, inc=1, device_id=to, device_id_type=MESH)

    ws[...] = jnp.zeros_like(ws)
    feeds[3].wait()
    for k in range(15):
        ws[4 * k : 4 * k + 4, 0:C] = stem_weight[k]
        ws[4 * k + 4 : 4 * k + 8, C:] = stem_weight[k]
    taps = ws[...]
    upper = taps.astype(bf16)
    wcat[0:64] = upper
    wcat[64:128] = (taps - upper.astype(f32)).astype(bf16)
    for i in (0, 1, 2, 4):
        feeds[i].wait()

    pl.semaphore_wait(barrier, len(greeted))
    halos = [
        remote(codes, near_codes.at[0], hs.at[0], hr.at[0], right),
        remote(codes, near_codes.at[1], hs.at[1], hr.at[1], left),
        remote(cot.at[ROWS - LEAD : ROWS], near_cot.at[0], hs.at[2], hr.at[2], right),
        remote(cot.at[0:LEAD], near_cot.at[1], hs.at[3], hr.at[3], left),
    ]
    for copy in halos:
        copy.start()
    for load in loads:
        load.start()
    reach = [1 << m for m in range(8) if (1 << m) < deep // 2]

    def tell(m):
        for step in (reach[m], deep - reach[m]):
            pl.semaphore_signal(known.at[m], inc=1, device_id=deeper(step), device_id_type=MESH)

    def learn(m):
        if m < len(reach):
            pl.semaphore_wait(known.at[m], 2)
            if m + 1 < len(reach):
                tell(m + 1)

    if reach:
        tell(0)

    cotx[LEAD : LEAD + ROWS] = cot[...].astype(f32)

    def shift_in(first, size):
        for t in range(5):
            at = LEAD + 2 - t + first
            shifted[first : first + size, t * C : (t + 1) * C] = cotx[at : at + size].astype(bf16)

    shift_in(LEAD, ROWS - 2 * LEAD)
    shifted[:, 5 * C :] = jnp.zeros((ROWS, 128), bf16)
    spot = (
        ctx * (2 * ROWS) - 128
        + 128 * lax.broadcasted_iota(jnp.int32, (16, 128), 0)
        + lax.broadcasted_iota(jnp.int32, (16, 128), 1)
    )
    moved = jnp.zeros((16, 128), jnp.int32)
    for v in range(vpos.shape[1]):
        moved = moved + jnp.where(spot == vpos[0, v], vshift[0, v], 0)

    inside = (spot >= 0) & (spot < count * (2 * ROWS))
    lane_in = lax.broadcasted_iota(jnp.int32, (128, 128), 0)
    lane_out = lax.broadcasted_iota(jnp.int32, (128, 128), 1)
    pick = (lane_in == 2 * (lane_out & 63) + lax.shift_right_logical(lane_out, 6)).astype(f32).astype(bf16)
    first = lax.broadcasted_iota(jnp.int32, (1, 128), 1) < 64
    line = lax.broadcasted_iota(jnp.int32, (8, LANES), 0)

    def one_hot(before, after):
        bases = moved + jnp.concatenate([before, codes[...], after, jnp.zeros((6, 128), jnp.int32)], axis=0)
        bases = jnp.where(inside, bases & 3, 4)
        split = jnp.dot(bases.astype(f32).astype(bf16), pick, preferred_element_type=f32)
        turned = pltpu.roll(split, 64, 1)
        evens, odds = [], []
        for p in range(5):
            evens.append(jnp.where(first, split[2 * p : 2 * p + 1], turned[2 * p + 1 : 2 * p + 2]))
            odds.append(jnp.where(first, turned[2 * p : 2 * p + 1], split[2 * p + 1 : 2 * p + 2]))
        even = jnp.broadcast_to(jnp.concatenate(evens, axis=1), (8, LANES))
        odd = jnp.broadcast_to(jnp.concatenate(odds, axis=1), (8, LANES))
        both = jnp.where(line < 4, odd, pltpu.roll(even, LANES - 1, 1))
        return (both == (line & 3).astype(f32)).astype(f32)

    def windows_of(hot):
        wide = [pltpu.roll(hot, LANES - (PAIRS + q), 1) for q in range(8)]
        return jnp.concatenate(wide + wide, axis=0)

    def bend(value):
        square = value * value
        inner = jnp.tanh(value * (root_scale + (root_scale * cubic) * square))
        active = 0.5 * value * (1.0 + inner)
        slope = 0.5 * (1.0 + inner) + 0.5 * value * (1.0 - inner * inner) * (
            root_scale + (3.0 * root_scale * cubic) * square
        )
        return active, slope

    def activate(i, carry):
        rows = pl.ds(pl.multiple_of(i * 16, 16), 16)
        active_e, slope_e = bend(stem[rows, 0:C])
        active_o, slope_o = bend(stem[rows, C:])
        slopes[rows, 0:C] = 0.5 * slope_e
        slopes[rows, C:] = 0.5 * slope_o
        pool = (0.5 * (active_e + active_o)).astype(bf16).astype(f32)
        pooled[rows] = pool
        gate, slope = bend(pool)
        gx[rows] = gate.astype(bf16).astype(f32)
        pslope[rows] = slope
        return carry

    edge = 2 * LEAD
    blank = jnp.zeros((1, 128), jnp.int32)
    windows = windows_of(one_hot(blank, blank)).T[edge : TALL - edge].astype(bf16)
    stem[edge : TALL - edge] = jnp.dot(windows, wcat[...], preferred_element_type=f32)
    lax.fori_loop(edge // 16, (TALL - edge) // 16, activate, 0)

    for copy in halos:
        copy.wait_recv()
    learn(0)
    hot = one_hot(near_codes[0, 7:8], near_codes[1, 0:1])
    windows_t = windows_of(hot)
    ends = jnp.concatenate(
        [windows_t[:, 0:128].T[0:edge], windows_t[:, ROWS : ROWS + 128].T[0:edge]], axis=0
    ).astype(bf16)
    ends = jnp.dot(ends, wcat[...], preferred_element_type=f32)
    stem[0:edge] = ends[0:edge]
    stem[TALL - edge :] = ends[edge:]
    for i in (0, 1, TALL // 16 - 2, TALL // 16 - 1):
        activate(i, 0)
    inside_left = jnp.where(ctx > 0, 1.0, 0.0)
    inside_right = jnp.where(ctx < count - 1, 1.0, 0.0)
    gx[0:LEAD] = gx[0:LEAD] * inside_left
    gx[LEAD + ROWS :] = gx[LEAD + ROWS :] * inside_right
    cotx[0:LEAD] = near_cot[0].astype(f32) * inside_left
    cotx[LEAD + ROWS :] = near_cot[1].astype(f32) * inside_right
    shift_in(0, LEAD)
    shift_in(ROWS - LEAD, LEAD)
    gated_t[...] = gx[LEAD : LEAD + ROWS].T.astype(bf16)

    def level0(half, piece):
        return remote(
            s0.at[half, piece], r0.at[half, piece], c0s.at[half, piece], c0r.at[half, piece], sibling
        )

    def product(owner, j):
        at = pl.multiple_of(owner * 1024 + 256 * j, 256)
        return jnp.dot(gated_t[...], shifted[:, pl.ds(at, 256)], preferred_element_type=f32)

    parts = C // rows2
    for j in range(4):
        block = product(other, j)
        for k in range(2):
            half, sub = divmod(2 * j + k, 4)
            piece, sub = divmod(sub, per)
            some = block[:, 128 * k : 128 * (k + 1)].reshape(parts, 2, rows3, 128)
            s0[half, piece, sub * parts : (sub + 1) * parts] = some.astype(bf16)
            if sub == per - 1:
                level0(half, piece).start()
    for j in range(4):
        block = product(core, j)
        for k in range(2):
            half, sub = divmod(2 * j + k, 4)
            piece, sub = divmod(sub, per)
            some = block[:, 128 * k : 128 * (k + 1)].reshape(parts, 2, rows3, 128)
            own[half, piece, sub * parts : (sub + 1) * parts] = some

    def ahead(half, level, step):
        return lax.rem(mine(half, level) + step, ring)

    def behind(half, level, step):
        return lax.rem(mine(half, level) + ring - step, ring)

    def level1(half, step, chunk, q):
        return remote(
            s1.at[half, step - 1, chunk, q], r1.at[half, step - 1, chunk, q],
            c1s.at[half, step - 1, chunk, q], c1r.at[half, step - 1, chunk, q], along(half, 1, step),
        )

    for half in range(2):
        for piece in range(ring):
            level0(half, piece).wait_recv()
    for q in range(2):
        for chunk in order + [0]:
            for step in order:
                for half in range(2):
                    at = ahead(half, 1, step), ahead(half, 2, chunk), q
                    s1[half, step - 1, chunk, q] = (own[(half, *at)] + r0[(half, *at)].astype(f32)).astype(bf16)
                    level1(half, step, chunk, q).start()

    learn(1)
    for load in loads:
        load.wait()
    for block in range(2):
        at = block * (ROWS // 2)
        rows = slice(at, at + ROWS // 2)
        more = slice(LEAD + at, LEAD + at + ROWS // 2)
        back = lax.dot_general(
            shifted[rows, : 5 * C], wt[...], (((1,), (1,)), ((), ())), preferred_element_type=f32
        )
        dpool = cotx[more] + back * pslope[more]
        d_pooled[rows] = dpool.astype(bf16)
        dstem[rows, 0:C] = (dpool * slopes[more, 0:C]).astype(bf16)
        dstem[rows, C:] = (dpool * slopes[more, C:]).astype(bf16)
    wins_t[...] = jnp.concatenate(
        [pltpu.roll(hot, LANES - (PAIRS + LEAD + q), 1)[:, :ROWS] for q in range(8)], axis=0
    ).astype(bf16)
    grad = jnp.dot(wins_t[...], dstem[...], preferred_element_type=f32)
    for k in range(3):
        tsum[k * 64 : k * 64 + 64] = grad[:, 128 * k : 128 * (k + 1)]
    for k in range(3):
        tsum[k * 64 : k * 64 + 60] = tsum[k * 64 : k * 64 + 60] + grad[4:64, C + 128 * k : C + 128 * (k + 1)]

    def stem0():
        return remote(t0, u0, e0s, e0r, sibling)

    t0[...] = tsum[pl.ds(pl.multiple_of(other * 96, 96), 96)].astype(bf16)
    stem0().start()

    for t in range(5):
        spread[:, t * C : (t + 1) * C] = gx[LEAD - 2 + t : LEAD - 2 + t + ROWS].astype(bf16)
    for block in range(2):
        at = block * (ROWS // 2)
        rows = slice(at, at + ROWS // 2)
        conv = jnp.dot(spread[rows], wf[...], preferred_element_type=f32)
        features[rows] = (pooled[LEAD + at : LEAD + at + ROWS // 2] + conv).astype(bf16)

    def stem1(step):
        return remote(t1, u1.at[step - 1], e1s.at[step - 1], e1r.at[step - 1], along(0, 1, step))

    def stem2(step):
        return remote(t2, u2.at[step - 1], e2s.at[step - 1], e2r.at[step - 1], along(0, 2, step))

    stem0().wait_recv()
    small = tsum[pl.ds(pl.multiple_of(core * 96, 96), 96)] + u0[...].astype(f32)
    t1[...] = small.astype(bf16)
    for step in order:
        stem1(step).start()

    def level2(half, step, q):
        return remote(
            s2.at[half, step - 1, q], r2.at[half, step - 1, q], c2s.at[half, step - 1, q], c2r.at[half, step - 1, q],
            along(half, 2, step),
        )

    def second(q):
        for chunk in order + [0]:
            for half in range(2):
                at = mine(half, 1), ahead(half, 2, chunk), q
                total = own[(half, *at)] + r0[(half, *at)].astype(f32)
                for step in range(1, ring):
                    level1(half, step, chunk, q).wait_recv()
                    total = total + r1[half, step - 1, chunk, q].astype(f32)
                if chunk:
                    s2[half, chunk - 1, q] = total.astype(bf16)
                    level2(half, chunk, q).start()
                else:
                    v3[q][half * rows3 : (half + 1) * rows3] = total

    def far(i):
        half_way = deep // 2 - lax.div(i + 1, 2)
        return jnp.where(lax.rem(i, 2) == 0, half_way, deep - half_way)

    def down(send, land, sends, recvs):
        return lambda step: remote(
            send.at[lax.rem(z + step, deep)], land.at[step - 1], sends.at[step - 1], recvs.at[step - 1], deeper(step)
        )

    def up(all_of, sends, recvs):
        return lambda step: remote(all_of.at[z], all_of.at[z], sends.at[step - 1], recvs.at[step - 1], deeper(step))

    def start_all(copy):
        def one(i, carry):
            copy(far(i)).start()
            return carry

        lax.fori_loop(0, deep - 1, one, 0)

    def each(method, *copies):
        def one(i, carry):
            for copy in copies:
                getattr(copy(i + 1), method)()
            return carry

        lax.fori_loop(0, deep - 1, one, 0)

    def cut(source, send, share):
        for piece in range(deep):
            send[piece] = source[piece * share : piece * share + send.shape[1]].astype(bf16)

    def join(all_of, target, share):
        for piece in range(deep):
            target[piece * share : piece * share + all_of.shape[1]] = all_of[piece].astype(f32)

    def summed(copy, send, land):
        def one(i, total):
            copy(i + 1).wait_recv()
            return total + land[i].astype(f32)

        return lax.fori_loop(0, deep - 1, one, send[z].astype(f32)).astype(bf16)

    share3 = 2 * rows3 // deep
    conv_down = [down(s3[q], r3[q], c3s[q], c3r[q]) for q in range(2)]
    conv_up = [up(g3[q], d3s[q], d3r[q]) for q in range(2)]
    stem_down, stem_up = down(s4, r4, c4s, c4r), up(g4, d4s, d4r)

    for q in range(2):
        second(q)
        if q == 0:
            for m in range(2, len(reach)):
                learn(m)
        else:
            for step in range(1, ring):
                stem1(step).wait_recv()
                small = small + u1[step - 1].astype(f32)
            t2[...] = small.astype(bf16)
            for step in order:
                stem2(step).start()
        for half in range(2):
            total = v3[q][half * rows3 : (half + 1) * rows3]
            for step in near:
                level2(half, step, q).wait_recv()
                total = total + r2[half, step - 1, q].astype(f32)
            v3[q][half * rows3 : (half + 1) * rows3] = total
        cut(v3[q], s3[q], share3)
        start_all(conv_down[q])
    for step in range(1, ring):
        stem2(step).wait_recv()
        small = small + u2[step - 1].astype(f32)
    v4[0:96] = small
    cut(v4, s4, 96 // deep)
    start_all(stem_down)
    for q in range(2):
        g3[q][z] = summed(conv_down[q], s3[q], r3[q])
        start_all(conv_up[q])
    g4[z] = summed(stem_down, s4, r4)
    start_all(stem_up)

    def back2(half, step, q):
        spot = gathered.at[core, half, mine(half, 1), mine(half, 2), q]
        return remote(spot, spot, d2s.at[half, step - 1, q], d2r.at[half, step - 1, q], along(half, 2, step))

    def back1(half, step, chunk, q):
        spot = gathered.at[core, half, mine(half, 1), behind(half, 2, chunk), q]
        return remote(
            spot, spot, d1s.at[half, step - 1, chunk, q], d1r.at[half, step - 1, chunk, q], along(half, 1, step)
        )

    def back0(half, step, chunk, q):
        spot = gathered.at[core, half, behind(half, 1, step), behind(half, 2, chunk), q]
        return remote(spot, spot, d0s.at[half, step, chunk, q], d0r.at[half, step, chunk, q], sibling)

    for q in range(2):
        each("wait_recv", conv_up[q])
        join(g3[q], w3[q], share3)
        for half in range(2):
            gathered[core, half, mine(half, 1), mine(half, 2), q] = w3[q][
                half * rows3 : (half + 1) * rows3
            ].astype(bf16)
            for step in order:
                back2(half, step, q).start()
        for chunk in [0] + near:
            for half in range(2):
                if chunk:
                    back2(half, chunk, q).wait_recv()
                for step in order:
                    back1(half, step, chunk, q).start()
                back0(half, 0, chunk, q).start()

    each("wait_recv", stem_up)
    join(g4, w4, 96 // deep)

    def back_stem():
        return remote(stem_all.at[core], stem_all.at[core], h0s, h0r, sibling)

    stem_all[core] = w4[0:96].astype(bf16)
    back_stem().start()
    for q in range(2):
        for chunk in [0] + near:
            for step in near:
                for half in range(2):
                    back1(half, step, chunk, q).wait_recv()
                    back0(half, step, chunk, q).start()
    back_stem().wait()
    for copy in halos:
        copy.wait_send()
    stem0().wait_send()
    for half in range(2):
        for step in range(ring):
            level0(half, step).wait_send()
            for chunk in range(ring):
                for q in range(2):
                    back0(half, step, chunk, q).wait()
        for step in range(1, ring):
            for q in range(2):
                level2(half, step, q).wait_send()
                back2(half, step, q).wait_send()
                for chunk in range(ring):
                    level1(half, step, chunk, q).wait_send()
                    back1(half, step, chunk, q).wait_send()
    for step in range(1, ring):
        stem1(step).wait_send()
        stem2(step).wait_send()
    each("wait_send", *conv_down, *conv_up, stem_down, stem_up)


def main(ring, deep, high, vpos, vshift, codes, cot, stem_weight, weight):
    per = 4 // ring
    rows1 = per * C
    rows2 = rows1 // ring
    rows3 = rows2 // 2
    totals = (2 * rows3, 2 * rows3, 96)
    talls = [-(-total // (8 * deep)) * 8 for total in totals]
    count = 2 * (ring // high) * deep
    dma = pltpu.SemaphoreType.DMA
    halves = lambda *lead: pltpu.VMEM((2,) + lead, bf16)
    pair = lambda *dims: [dma(dims), dma(dims)]
    vmem = pl.BlockSpec(memory_space=pltpu.VMEM)
    hbm = pl.BlockSpec(memory_space=pltpu.HBM)
    return pl.pallas_call(
        functools.partial(main_kernel, ring, deep, high, count),
        out_shape=(
            jax.ShapeDtypeStruct((ROWS, C), bf16),
            jax.ShapeDtypeStruct((ROWS, C), bf16),
            jax.ShapeDtypeStruct((2, 2, ring, ring, 2, rows3, 128), bf16),
            jax.ShapeDtypeStruct((2, 96, 128), bf16),
        ),
        in_specs=[hbm] * 6,
        out_specs=(vmem,) * 4,
        scratch_shapes=[
            pltpu.SMEM(vpos.shape, jnp.int32),
            pltpu.SMEM(vshift.shape, jnp.int32),
            pltpu.VMEM((8, 128), jnp.int32),
            pltpu.VMEM((ROWS, C), bf16),
            pltpu.VMEM((15, 4, C), f32),
            dma((5,)),
            pltpu.VMEM((2, 8, 128), jnp.int32),
            pltpu.VMEM((2, LEAD, C), bf16),
            *pair(4),
            pltpu.SemaphoreType.REGULAR((3,)),
            pltpu.VMEM((128, 2 * C), bf16),
            pltpu.VMEM((C, 5 * C), bf16),
            pltpu.VMEM((5 * C, C), bf16),
            dma((10,)),
            pltpu.VMEM((64, 2 * C), f32),
            pltpu.VMEM((TALL, 2 * C), f32),
            pltpu.VMEM((TALL, 2 * C), f32),
            pltpu.VMEM((TALL, C), f32),
            pltpu.VMEM((TALL, C), f32),
            pltpu.VMEM((TALL, C), f32),
            pltpu.VMEM((TALL, C), f32),
            pltpu.VMEM((ROWS, 2048), bf16),
            pltpu.VMEM((ROWS, 5 * C), bf16),
            pltpu.VMEM((64, ROWS), bf16),
            pltpu.VMEM((C, ROWS), bf16),
            pltpu.VMEM((ROWS, 2 * C), bf16),
            pltpu.VMEM((2, ring, ring, 2, rows3, 128), f32),
            halves(ring, ring, 2, rows3, 128),
            halves(ring, ring, 2, rows3, 128),
            halves(ring - 1, ring, 2, rows3, 128),
            halves(ring - 1, ring, 2, rows3, 128),
            halves(ring - 1, 2, rows3, 128),
            halves(ring - 1, 2, rows3, 128),
            pltpu.VMEM((96, 128), bf16),
            pltpu.VMEM((96, 128), bf16),
            pltpu.VMEM((192, 128), f32),
            pltpu.VMEM((96, 128), bf16),
            pltpu.VMEM((ring - 1, 96, 128), bf16),
            pltpu.VMEM((96, 128), bf16),
            pltpu.VMEM((ring - 1, 96, 128), bf16),
            *[
                scratch
                for tall, total in zip(talls, totals)
                for scratch in (
                    pltpu.VMEM((total + tall, 128), f32),
                    pltpu.VMEM((deep, tall, 128), bf16),
                    pltpu.VMEM((deep - 1, tall, 128), bf16),
                    pltpu.VMEM((deep, tall, 128), bf16),
                    pltpu.VMEM((total + tall, 128), f32),
                )
            ],
            *pair(2, ring), *pair(2, ring - 1, ring, 2), *pair(2, ring - 1, 2), *pair(deep - 1),
            *pair(deep - 1), *pair(2, ring - 1, 2), *pair(2, ring - 1, ring, 2), *pair(2, ring, ring, 2),
            *pair(), *pair(ring - 1), *pair(ring - 1), *pair(),
            *pair(deep - 1), *pair(deep - 1), *pair(deep - 1), *pair(deep - 1),
        ],
        compiler_params=pltpu.CompilerParams(
            collective_id=0, has_side_effects=True, vmem_limit_bytes=36 * 1024 * 1024
        ),
        name="block",
    )(vpos, vshift, codes, cot, stem_weight, weight)


def finish_kernel(summed, small, features, d_pooled, conv, stem, features_out, d_pooled_out, widened, sems):
    copies = [
        pltpu.make_async_copy(features, features_out, sems.at[5]),
        pltpu.make_async_copy(d_pooled, d_pooled_out, sems.at[6]),
    ]
    for t in range(5):
        for k in range(3):
            widened[t, :, k * 128 : (k + 1) * 128] = summed[3 * t + k].astype(f32)
        copies.append(pltpu.make_async_copy(widened.at[t], conv.at[t], sems.at[t]))
        copies[-1].start()
    for copy in copies[:2]:
        copy.start()
    rows = jnp.concatenate([small[0], small[1]], axis=0).astype(f32)
    for k in range(3):
        for tap in range(15):
            stem[tap, :, k * 128 : (k + 1) * 128] = rows[k * 64 + 4 * tap : k * 64 + 4 * tap + 4]
    for copy in copies:
        copy.wait()


def finish(summed, small, features, d_pooled):
    vmem = pl.BlockSpec(memory_space=pltpu.VMEM)
    apart = pl.BlockSpec(memory_space=pl.ANY)
    return pl.pallas_call(
        finish_kernel,
        out_shape=(
            jax.ShapeDtypeStruct((5, C, C), f32),
            jax.ShapeDtypeStruct((15, 4, C), f32),
            jax.ShapeDtypeStruct((ROWS, C), bf16),
            jax.ShapeDtypeStruct((ROWS, C), bf16),
        ),
        in_specs=[vmem] * 4,
        out_specs=(apart, vmem, apart, apart),
        scratch_shapes=[pltpu.VMEM((5, C, C), f32), pltpu.SemaphoreType.DMA((7,))],
        compiler_params=pltpu.CompilerParams(vmem_limit_bytes=8 * 1024 * 1024),
        name="finish",
    )(summed.reshape(16, C, 128), small, features, d_pooled)


def per_device(ring, deep, high, codes, variant_pos, variant_shift, stem_weight, conv_weight, cotangent):
    codes = codes.reshape(8, 128)
    cot = cotangent.reshape(ROWS, C)
    codes, cot, variant_pos, variant_shift, stem_weight, conv_weight = (
        pltpu.with_memory_space_constraint(array, pltpu.HBM)
        for array in (codes, cot, variant_pos, variant_shift, stem_weight, conv_weight)
    )
    features, d_pooled, summed, small = main(
        ring, deep, high, variant_pos, variant_shift, codes, cot, stem_weight, conv_weight
    )
    conv_grad, stem_grad, features, d_pooled = finish(summed, small, features, d_pooled)
    return features[None], d_pooled[None], conv_grad, stem_grad


def build(mesh, ring, deep, high):
    placed = (P("dp", "context"), P("dp", None), P("dp", None), P(), P(), P("dp", "context", None))
    return jax.shard_map(
        functools.partial(per_device, ring, deep, high),
        mesh=mesh,
        in_specs=placed,
        out_specs=(P("dp", "context", None), P("dp", "context", None), P(), P()),
        check_vma=False,
    )


def solution(mesh):
    return build(mesh, 4, 16, 2)
```

```python
import functools
import math

import jax
import jax.numpy as jnp
from jax import lax
from jax.experimental import pallas as pl
from jax.experimental.pallas import tpu as pltpu
from jax.sharding import PartitionSpec as P

MESH = pl.DeviceIdType.MESH
f32, bf16 = jnp.float32, jnp.bfloat16
root_scale = math.sqrt(2.0 / math.pi)
cubic = 0.044715

C = 384
ROWS = 512
LEAD = 16
TALL = ROWS + 2 * LEAD
LANES = 640
PAIRS = 44


def places(ring, deep, high):
    low = ring // high
    dp, ctx = lax.axis_index("dp"), lax.axis_index("context")
    y, xh = lax.div(dp, high), lax.rem(dp, high)
    core, z = lax.rem(ctx, 2), lax.rem(lax.div(ctx, 2), deep)
    x = xh * low + lax.div(ctx, 2 * deep)

    def device(x, y, z, core):
        return {
            "dp": y * high + lax.div(x, low),
            "context": (lax.rem(x, low) * deep + z) * 2 + core,
        }

    return x, y, z, core, device


def remote(src, dst, send, recv, to):
    return pltpu.make_async_remote_copy(
        src_ref=src, dst_ref=dst, send_sem=send, recv_sem=recv, device_id=to, device_id_type=MESH
    )


def main_kernel(
    ring, deep, high, count,
    vpos_in, vshift_in, codes_in, cot_in, stem_weight_in, weight,
    features, d_pooled, gathered, stem_all,
    vpos, vshift, codes, cot, stem_weight, insem, near_codes, near_cot, hs, hr, known, wcat,
    wt, wf, wsem, ws, stem, slopes, cotx, gx, pooled, pslope, shifted, spread, wins_t, gated_t, dstem,
    own, s0, r0, s1, r1, s2, r2,
    t0, u0, tsum, t1, u1, t2, u2,
    v3, s3, r3, g3, w3, v4, s4, r4, g4, w4,
    c0s, c0r, c1s, c1r, c2s, c2r, c3s, c3r, d3s, d3r, d2s, d2r, d1s, d1r, d0s, d0r,
    e0s, e0r, e1s, e1r, e2s, e2r, h0s, h0r, c4s, c4r, d4s, d4r,
):
    x, y, z, core, device = places(ring, deep, high)
    ctx = lax.axis_index("context")
    other = 1 - core
    per = 4 // ring
    rows1 = per * C
    rows2 = rows1 // ring

    def along(half, level, step):
        if (half == 0) == (level == 1):
            return device(lax.rem(x + step, ring), y, z, core)
        return device(x, lax.rem(y + step, ring), z, core)

    def mine(half, level):
        return x if (half == 0) == (level == 1) else y

    def deeper(step):
        return device(x, y, lax.rem(z + step, deep), core)

    sibling = device(x, y, z, other)
    order = sorted(range(1, ring), key=lambda d: -min(d, ring - d))
    near = order[::-1]

    feeds = [
        pltpu.make_async_copy(source, target, insem.at[i])
        for i, (source, target) in enumerate(
            [(vpos_in, vpos), (vshift_in, vshift), (codes_in, codes), (stem_weight_in, stem_weight), (cot_in, cot)]
        )
    ]
    for feed in feeds:
        feed.start()
    loads = [pltpu.make_async_copy(weight.at[t], wt.at[:, t * C : (t + 1) * C], wsem.at[t]) for t in range(5)]
    loads += [pltpu.make_async_copy(weight.at[t], wf.at[t * C : (t + 1) * C], wsem.at[5 + t]) for t in range(5)]
    left = {"context": lax.rem(ctx + count - 1, count)}
    right = {"context": lax.rem(ctx + 1, count)}
    barrier = pltpu.get_barrier_semaphore()
    greeted = [left, right, deeper(1), deeper(deep - 1)]
    greeted += [along(half, 1, step) for step in range(1, ring) for half in range(2)]
    for to in greeted:
        pl.semaphore_signal(barrier, inc=1, device_id=to, device_id_type=MESH)

    ws[...] = jnp.zeros_like(ws)
    feeds[3].wait()
    for k in range(15):
        ws[4 * k : 4 * k + 4, 0:C] = stem_weight[k]
        ws[4 * k + 4 : 4 * k + 8, C:] = stem_weight[k]
    taps = ws[...]
    upper = taps.astype(bf16)
    wcat[0:64] = upper
    wcat[64:128] = (taps - upper.astype(f32)).astype(bf16)
    for i in (0, 1, 2, 4):
        feeds[i].wait()

    pl.semaphore_wait(barrier, len(greeted))
    halos = [
        remote(codes, near_codes.at[0], hs.at[0], hr.at[0], right),
        remote(codes, near_codes.at[1], hs.at[1], hr.at[1], left),
        remote(cot.at[ROWS - LEAD : ROWS], near_cot.at[0], hs.at[2], hr.at[2], right),
        remote(cot.at[0:LEAD], near_cot.at[1], hs.at[3], hr.at[3], left),
    ]
    for copy in halos:
        copy.start()
    for load in loads:
        load.start()
    reach = [1 << m for m in range(8) if (1 << m) < deep // 2]

    def tell(m):
        for step in (reach[m], deep - reach[m]):
            pl.semaphore_signal(known.at[m], inc=1, device_id=deeper(step), device_id_type=MESH)

    def learn(m):
        if m < len(reach):
            pl.semaphore_wait(known.at[m], 2)
            if m + 1 < len(reach):
                tell(m + 1)

    if reach:
        tell(0)

    cotx[LEAD : LEAD + ROWS] = cot[...].astype(f32)

    def shift_in(first, size):
        for t in range(5):
            at = LEAD + 2 - t + first
            shifted[first : first + size, t * C : (t + 1) * C] = cotx[at : at + size].astype(bf16)

    shift_in(LEAD, ROWS - 2 * LEAD)
    shifted[:, 5 * C :] = jnp.zeros((ROWS, 128), bf16)
    spot = (
        ctx * (2 * ROWS) - 128
        + 128 * lax.broadcasted_iota(jnp.int32, (16, 128), 0)
        + lax.broadcasted_iota(jnp.int32, (16, 128), 1)
    )
    moved = jnp.zeros((16, 128), jnp.int32)
    for v in range(vpos.shape[1]):
        moved = moved + jnp.where(spot == vpos[0, v], vshift[0, v], 0)

    inside = (spot >= 0) & (spot < count * (2 * ROWS))
    lane_in = lax.broadcasted_iota(jnp.int32, (128, 128), 0)
    lane_out = lax.broadcasted_iota(jnp.int32, (128, 128), 1)
    pick = (lane_in == 2 * (lane_out & 63) + lax.shift_right_logical(lane_out, 6)).astype(f32).astype(bf16)
    first = lax.broadcasted_iota(jnp.int32, (1, 128), 1) < 64
    line = lax.broadcasted_iota(jnp.int32, (8, LANES), 0)

    def one_hot(before, after):
        bases = moved + jnp.concatenate([before, codes[...], after, jnp.zeros((6, 128), jnp.int32)], axis=0)
        bases = jnp.where(inside, bases & 3, 4)
        split = jnp.dot(bases.astype(f32).astype(bf16), pick, preferred_element_type=f32)
        turned = pltpu.roll(split, 64, 1)
        evens, odds = [], []
        for p in range(5):
            evens.append(jnp.where(first, split[2 * p : 2 * p + 1], turned[2 * p + 1 : 2 * p + 2]))
            odds.append(jnp.where(first, turned[2 * p : 2 * p + 1], split[2 * p + 1 : 2 * p + 2]))
        even = jnp.broadcast_to(jnp.concatenate(evens, axis=1), (8, LANES))
        odd = jnp.broadcast_to(jnp.concatenate(odds, axis=1), (8, LANES))
        both = jnp.where(line < 4, odd, pltpu.roll(even, LANES - 1, 1))
        return (both == (line & 3).astype(f32)).astype(f32)

    def windows_of(hot):
        wide = [pltpu.roll(hot, LANES - (PAIRS + q), 1) for q in range(8)]
        return jnp.concatenate(wide + wide, axis=0)

    def bend(value):
        square = value * value
        inner = jnp.tanh(value * (root_scale + (root_scale * cubic) * square))
        active = 0.5 * value * (1.0 + inner)
        slope = 0.5 * (1.0 + inner) + 0.5 * value * (1.0 - inner * inner) * (
            root_scale + (3.0 * root_scale * cubic) * square
        )
        return active, slope

    def activate(i, carry):
        rows = pl.ds(pl.multiple_of(i * 16, 16), 16)
        active_e, slope_e = bend(stem[rows, 0:C])
        active_o, slope_o = bend(stem[rows, C:])
        slopes[rows, 0:C] = 0.5 * slope_e
        slopes[rows, C:] = 0.5 * slope_o
        pool = (0.5 * (active_e + active_o)).astype(bf16).astype(f32)
        pooled[rows] = pool
        gate, slope = bend(pool)
        gx[rows] = gate.astype(bf16).astype(f32)
        pslope[rows] = slope
        return carry

    edge = 2 * LEAD
    blank = jnp.zeros((1, 128), jnp.int32)
    windows = windows_of(one_hot(blank, blank)).T[edge : TALL - edge].astype(bf16)
    stem[edge : TALL - edge] = jnp.dot(windows, wcat[...], preferred_element_type=f32)
    lax.fori_loop(edge // 16, (TALL - edge) // 16, activate, 0)

    for copy in halos:
        copy.wait_recv()
    learn(0)
    hot = one_hot(near_codes[0, 7:8], near_codes[1, 0:1])
    windows_t = windows_of(hot)
    ends = jnp.concatenate(
        [windows_t[:, 0:128].T[0:edge], windows_t[:, ROWS : ROWS + 128].T[0:edge]], axis=0
    ).astype(bf16)
    ends = jnp.dot(ends, wcat[...], preferred_element_type=f32)
    stem[0:edge] = ends[0:edge]
    stem[TALL - edge :] = ends[edge:]
    for i in (0, 1, TALL // 16 - 2, TALL // 16 - 1):
        activate(i, 0)
    inside_left = jnp.where(ctx > 0, 1.0, 0.0)
    inside_right = jnp.where(ctx < count - 1, 1.0, 0.0)
    gx[0:LEAD] = gx[0:LEAD] * inside_left
    gx[LEAD + ROWS :] = gx[LEAD + ROWS :] * inside_right
    cotx[0:LEAD] = near_cot[0].astype(f32) * inside_left
    cotx[LEAD + ROWS :] = near_cot[1].astype(f32) * inside_right
    shift_in(0, LEAD)
    shift_in(ROWS - LEAD, LEAD)
    gated_t[...] = gx[LEAD : LEAD + ROWS].T.astype(bf16)

    def level0(half, piece):
        return remote(
            s0.at[half, piece], r0.at[half, piece], c0s.at[half, piece], c0r.at[half, piece], sibling
        )

    def product(owner, j):
        at = pl.multiple_of(owner * 1024 + 256 * j, 256)
        return jnp.dot(gated_t[...], shifted[:, pl.ds(at, 256)], preferred_element_type=f32)

    parts = C // rows2
    for j in range(4):
        block = product(other, j)
        for k in range(2):
            half, sub = divmod(2 * j + k, 4)
            piece, sub = divmod(sub, per)
            some = block[:, 128 * k : 128 * (k + 1)].reshape(parts, rows2, 128)
            s0[half, piece, sub * parts : (sub + 1) * parts] = some.astype(bf16)
            if sub == per - 1:
                level0(half, piece).start()
    for j in range(4):
        block = product(core, j)
        for k in range(2):
            half, sub = divmod(2 * j + k, 4)
            piece, sub = divmod(sub, per)
            some = block[:, 128 * k : 128 * (k + 1)].reshape(parts, rows2, 128)
            own[half, piece, sub * parts : (sub + 1) * parts] = some

    def ahead(half, level, step):
        return lax.rem(mine(half, level) + step, ring)

    def behind(half, level, step):
        return lax.rem(mine(half, level) + ring - step, ring)

    def level1(half, step, chunk):
        return remote(
            s1.at[half, step - 1, chunk], r1.at[half, step - 1, chunk],
            c1s.at[half, step - 1, chunk], c1r.at[half, step - 1, chunk], along(half, 1, step),
        )

    for half in range(2):
        for piece in range(ring):
            level0(half, piece).wait_recv()
    for chunk in order + [0]:
        for step in order:
            for half in range(2):
                at = ahead(half, 1, step), ahead(half, 2, chunk)
                s1[half, step - 1, chunk] = (own[half, at[0], at[1]] + r0[half, at[0], at[1]].astype(f32)).astype(bf16)
                level1(half, step, chunk).start()

    learn(1)
    for load in loads:
        load.wait()
    for block in range(2):
        at = block * (ROWS // 2)
        rows = slice(at, at + ROWS // 2)
        more = slice(LEAD + at, LEAD + at + ROWS // 2)
        back = lax.dot_general(
            shifted[rows, : 5 * C], wt[...], (((1,), (1,)), ((), ())), preferred_element_type=f32
        )
        dpool = cotx[more] + back * pslope[more]
        d_pooled[rows] = dpool.astype(bf16)
        dstem[rows, 0:C] = (dpool * slopes[more, 0:C]).astype(bf16)
        dstem[rows, C:] = (dpool * slopes[more, C:]).astype(bf16)
    wins_t[...] = jnp.concatenate(
        [pltpu.roll(hot, LANES - (PAIRS + LEAD + q), 1)[:, :ROWS] for q in range(8)], axis=0
    ).astype(bf16)
    grad = jnp.dot(wins_t[...], dstem[...], preferred_element_type=f32)
    for k in range(3):
        tsum[k * 64 : k * 64 + 64] = grad[:, 128 * k : 128 * (k + 1)]
    for k in range(3):
        tsum[k * 64 : k * 64 + 60] = tsum[k * 64 : k * 64 + 60] + grad[4:64, C + 128 * k : C + 128 * (k + 1)]

    def stem0():
        return remote(t0, u0, e0s, e0r, sibling)

    t0[...] = tsum[pl.ds(pl.multiple_of(other * 96, 96), 96)].astype(bf16)
    stem0().start()

    for t in range(5):
        spread[:, t * C : (t + 1) * C] = gx[LEAD - 2 + t : LEAD - 2 + t + ROWS].astype(bf16)
    for block in range(2):
        at = block * (ROWS // 2)
        rows = slice(at, at + ROWS // 2)
        conv = jnp.dot(spread[rows], wf[...], preferred_element_type=f32)
        features[rows] = (pooled[LEAD + at : LEAD + at + ROWS // 2] + conv).astype(bf16)

    def stem1(step):
        return remote(t1, u1.at[step - 1], e1s.at[step - 1], e1r.at[step - 1], along(0, 1, step))

    def stem2(step):
        return remote(t2, u2.at[step - 1], e2s.at[step - 1], e2r.at[step - 1], along(0, 2, step))

    stem0().wait_recv()
    small = tsum[pl.ds(pl.multiple_of(core * 96, 96), 96)] + u0[...].astype(f32)
    t1[...] = small.astype(bf16)
    for step in order:
        stem1(step).start()

    def level2(half, step):
        return remote(
            s2.at[half, step - 1], r2.at[half, step - 1], c2s.at[half, step - 1], c2r.at[half, step - 1],
            along(half, 2, step),
        )

    for chunk in order + [0]:
        for half in range(2):
            at = mine(half, 1), ahead(half, 2, chunk)
            total = own[half, at[0], at[1]] + r0[half, at[0], at[1]].astype(f32)
            for step in range(1, ring):
                level1(half, step, chunk).wait_recv()
                total = total + r1[half, step - 1, chunk].astype(f32)
            if chunk:
                s2[half, chunk - 1] = total.astype(bf16)
                level2(half, chunk).start()
            else:
                v3[half * rows2 : (half + 1) * rows2] = total

    for step in range(1, ring):
        stem1(step).wait_recv()
        small = small + u1[step - 1].astype(f32)
    t2[...] = small.astype(bf16)
    for step in order:
        stem2(step).start()

    def far(i):
        half_way = deep // 2 - lax.div(i + 1, 2)
        return jnp.where(lax.rem(i, 2) == 0, half_way, deep - half_way)

    def down(send, land, sends, recvs):
        return lambda step: remote(
            send.at[lax.rem(z + step, deep)], land.at[step - 1], sends.at[step - 1], recvs.at[step - 1], deeper(step)
        )

    def up(all_of, sends, recvs):
        return lambda step: remote(all_of.at[z], all_of.at[z], sends.at[step - 1], recvs.at[step - 1], deeper(step))

    def start_all(copy):
        def one(i, carry):
            copy(far(i)).start()
            return carry

        lax.fori_loop(0, deep - 1, one, 0)

    def each(method, *copies):
        def one(i, carry):
            for copy in copies:
                getattr(copy(i + 1), method)()
            return carry

        lax.fori_loop(0, deep - 1, one, 0)

    def cut(source, send, share):
        for piece in range(deep):
            send[piece] = source[piece * share : piece * share + send.shape[1]].astype(bf16)

    def join(all_of, target, share):
        for piece in range(deep):
            target[piece * share : piece * share + all_of.shape[1]] = all_of[piece].astype(f32)

    def summed(copy, send, land):
        def one(i, total):
            step = far(deep - 2 - i)
            copy(step).wait_recv()
            return total + land[step - 1].astype(f32)

        return lax.fori_loop(0, deep - 1, one, send[z].astype(f32)).astype(bf16)

    for half in range(2):
        total = v3[half * rows2 : (half + 1) * rows2]
        for step in near:
            level2(half, step).wait_recv()
            total = total + r2[half, step - 1].astype(f32)
        v3[half * rows2 : (half + 1) * rows2] = total
    conv_down, conv_up = down(s3, r3, c3s, c3r), up(g3, d3s, d3r)
    stem_down, stem_up = down(s4, r4, c4s, c4r), up(g4, d4s, d4r)
    for m in range(2, len(reach)):
        learn(m)
    cut(v3, s3, 2 * rows2 // deep)
    start_all(conv_down)
    for step in range(1, ring):
        stem2(step).wait_recv()
        small = small + u2[step - 1].astype(f32)
    v4[0:96] = small
    cut(v4, s4, 96 // deep)
    start_all(stem_down)
    for half in range(2):
        for step in range(ring):
            level0(half, step).wait_send()
        for step in range(1, ring):
            level2(half, step).wait_send()
            for chunk in range(ring):
                level1(half, step, chunk).wait_send()
    stem0().wait_send()
    for step in range(1, ring):
        stem1(step).wait_send()
        stem2(step).wait_send()
    for copy in halos:
        copy.wait_send()
    g3[z] = summed(conv_down, s3, r3)
    start_all(conv_up)
    g4[z] = summed(stem_down, s4, r4)
    start_all(stem_up)
    each("wait_send", conv_down, stem_down)
    each("wait_recv", conv_up)
    join(g3, w3, 2 * rows2 // deep)

    def back2(half, step):
        spot = gathered.at[core, half, mine(half, 1), mine(half, 2)]
        return remote(spot, spot, d2s.at[half, step - 1], d2r.at[half, step - 1], along(half, 2, step))

    def back1(half, step, chunk):
        spot = gathered.at[core, half, mine(half, 1), behind(half, 2, chunk)]
        return remote(spot, spot, d1s.at[half, step - 1, chunk], d1r.at[half, step - 1, chunk], along(half, 1, step))

    def back0(half, step, chunk):
        spot = gathered.at[core, half, behind(half, 1, step), behind(half, 2, chunk)]
        return remote(spot, spot, d0s.at[half, step, chunk], d0r.at[half, step, chunk], sibling)

    for half in range(2):
        gathered[core, half, mine(half, 1), mine(half, 2)] = w3[half * rows2 : (half + 1) * rows2].astype(bf16)
        for step in order:
            back2(half, step).start()
    for chunk in [0] + near:
        for half in range(2):
            if chunk:
                back2(half, chunk).wait_recv()
            for step in order:
                back1(half, step, chunk).start()
            back0(half, 0, chunk).start()

    each("wait_recv", stem_up)
    join(g4, w4, 96 // deep)

    def back_stem():
        return remote(stem_all.at[core], stem_all.at[core], h0s, h0r, sibling)

    stem_all[core] = w4[0:96].astype(bf16)
    back_stem().start()
    each("wait_send", conv_up, stem_up)
    last = []
    for chunk in [0] + near:
        fresh = [(half, 0, chunk) for half in range(2)]
        for step in near:
            for half in range(2):
                back1(half, step, chunk).wait_recv()
                back0(half, step, chunk).start()
                fresh.append((half, step, chunk))
        for spot in last:
            back0(*spot).wait()
        last = fresh
    for half in range(2):
        for step in range(1, ring):
            back2(half, step).wait_send()
            for chunk in range(ring):
                back1(half, step, chunk).wait_send()
    back_stem().wait()
    for spot in last:
        back0(*spot).wait()


def main(ring, deep, high, vpos, vshift, codes, cot, stem_weight, weight):
    per = 4 // ring
    rows1 = per * C
    rows2 = rows1 // ring
    talls = [-(-total // (8 * deep)) * 8 for total in (2 * rows2, 96)]
    count = 2 * (ring // high) * deep
    dma = pltpu.SemaphoreType.DMA
    halves = lambda *lead: pltpu.VMEM((2,) + lead, bf16)
    pair = lambda *dims: [dma(dims), dma(dims)]
    vmem = pl.BlockSpec(memory_space=pltpu.VMEM)
    hbm = pl.BlockSpec(memory_space=pltpu.HBM)
    return pl.pallas_call(
        functools.partial(main_kernel, ring, deep, high, count),
        out_shape=(
            jax.ShapeDtypeStruct((ROWS, C), bf16),
            jax.ShapeDtypeStruct((ROWS, C), bf16),
            jax.ShapeDtypeStruct((2, 2, ring, ring, rows2, 128), bf16),
            jax.ShapeDtypeStruct((2, 96, 128), bf16),
        ),
        in_specs=[hbm] * 6,
        out_specs=(vmem,) * 4,
        scratch_shapes=[
            pltpu.SMEM(vpos.shape, jnp.int32),
            pltpu.SMEM(vshift.shape, jnp.int32),
            pltpu.VMEM((8, 128), jnp.int32),
            pltpu.VMEM((ROWS, C), bf16),
            pltpu.VMEM((15, 4, C), f32),
            dma((5,)),
            pltpu.VMEM((2, 8, 128), jnp.int32),
            pltpu.VMEM((2, LEAD, C), bf16),
            *pair(4),
            pltpu.SemaphoreType.REGULAR((3,)),
            pltpu.VMEM((128, 2 * C), bf16),
            pltpu.VMEM((C, 5 * C), bf16),
            pltpu.VMEM((5 * C, C), bf16),
            dma((10,)),
            pltpu.VMEM((64, 2 * C), f32),
            pltpu.VMEM((TALL, 2 * C), f32),
            pltpu.VMEM((TALL, 2 * C), f32),
            pltpu.VMEM((TALL, C), f32),
            pltpu.VMEM((TALL, C), f32),
            pltpu.VMEM((TALL, C), f32),
            pltpu.VMEM((TALL, C), f32),
            pltpu.VMEM((ROWS, 2048), bf16),
            pltpu.VMEM((ROWS, 5 * C), bf16),
            pltpu.VMEM((64, ROWS), bf16),
            pltpu.VMEM((C, ROWS), bf16),
            pltpu.VMEM((ROWS, 2 * C), bf16),
            pltpu.VMEM((2, ring, ring, rows2, 128), f32),
            halves(ring, ring, rows2, 128),
            halves(ring, ring, rows2, 128),
            halves(ring - 1, ring, rows2, 128),
            halves(ring - 1, ring, rows2, 128),
            halves(ring - 1, rows2, 128),
            halves(ring - 1, rows2, 128),
            pltpu.VMEM((96, 128), bf16),
            pltpu.VMEM((96, 128), bf16),
            pltpu.VMEM((192, 128), f32),
            pltpu.VMEM((96, 128), bf16),
            pltpu.VMEM((ring - 1, 96, 128), bf16),
            pltpu.VMEM((96, 128), bf16),
            pltpu.VMEM((ring - 1, 96, 128), bf16),
            *[
                scratch
                for tall, total in zip(talls, (2 * rows2, 96))
                for scratch in (
                    pltpu.VMEM((total + tall, 128), f32),
                    pltpu.VMEM((deep, tall, 128), bf16),
                    pltpu.VMEM((deep - 1, tall, 128), bf16),
                    pltpu.VMEM((deep, tall, 128), bf16),
                    pltpu.VMEM((total + tall, 128), f32),
                )
            ],
            *pair(2, ring), *pair(2, ring - 1, ring), *pair(2, ring - 1), *pair(deep - 1),
            *pair(deep - 1), *pair(2, ring - 1), *pair(2, ring - 1, ring), *pair(2, ring, ring),
            *pair(), *pair(ring - 1), *pair(ring - 1), *pair(),
            *pair(deep - 1), *pair(deep - 1),
        ],
        compiler_params=pltpu.CompilerParams(
            collective_id=0, has_side_effects=True, vmem_limit_bytes=36 * 1024 * 1024
        ),
        name="block",
    )(vpos, vshift, codes, cot, stem_weight, weight)


def finish_kernel(summed, small, features, d_pooled, conv, stem, features_out, d_pooled_out, widened, sems):
    copies = [
        pltpu.make_async_copy(features, features_out, sems.at[5]),
        pltpu.make_async_copy(d_pooled, d_pooled_out, sems.at[6]),
    ]
    for t in range(5):
        for k in range(3):
            widened[t, :, k * 128 : (k + 1) * 128] = summed[3 * t + k].astype(f32)
        copies.append(pltpu.make_async_copy(widened.at[t], conv.at[t], sems.at[t]))
        copies[-1].start()
    for copy in copies[:2]:
        copy.start()
    rows = jnp.concatenate([small[0], small[1]], axis=0).astype(f32)
    for k in range(3):
        for tap in range(15):
            stem[tap, :, k * 128 : (k + 1) * 128] = rows[k * 64 + 4 * tap : k * 64 + 4 * tap + 4]
    for copy in copies:
        copy.wait()


def finish(summed, small, features, d_pooled):
    vmem = pl.BlockSpec(memory_space=pltpu.VMEM)
    apart = pl.BlockSpec(memory_space=pl.ANY)
    return pl.pallas_call(
        finish_kernel,
        out_shape=(
            jax.ShapeDtypeStruct((5, C, C), f32),
            jax.ShapeDtypeStruct((15, 4, C), f32),
            jax.ShapeDtypeStruct((ROWS, C), bf16),
            jax.ShapeDtypeStruct((ROWS, C), bf16),
        ),
        in_specs=[vmem] * 4,
        out_specs=(apart, vmem, apart, apart),
        scratch_shapes=[pltpu.VMEM((5, C, C), f32), pltpu.SemaphoreType.DMA((7,))],
        compiler_params=pltpu.CompilerParams(vmem_limit_bytes=8 * 1024 * 1024),
        name="finish",
    )(summed.reshape(16, C, 128), small, features, d_pooled)


def per_device(ring, deep, high, codes, variant_pos, variant_shift, stem_weight, conv_weight, cotangent):
    codes = codes.reshape(8, 128)
    cot = cotangent.reshape(ROWS, C)
    codes, cot, variant_pos, variant_shift, stem_weight, conv_weight = (
        pltpu.with_memory_space_constraint(array, pltpu.HBM)
        for array in (codes, cot, variant_pos, variant_shift, stem_weight, conv_weight)
    )
    features, d_pooled, summed, small = main(
        ring, deep, high, variant_pos, variant_shift, codes, cot, stem_weight, conv_weight
    )
    conv_grad, stem_grad, features, d_pooled = finish(summed, small, features, d_pooled)
    return features[None], d_pooled[None], conv_grad, stem_grad


def build(mesh, ring, deep, high):
    placed = (P("dp", "context"), P("dp", None), P("dp", None), P(), P(), P("dp", "context", None))
    return jax.shard_map(
        functools.partial(per_device, ring, deep, high),
        mesh=mesh,
        in_specs=placed,
        out_specs=(P("dp", "context", None), P("dp", "context", None), P(), P()),
        check_vma=False,
    )


def solution(mesh):
    return build(mesh, 4, 16, 2)
```

```python
import functools
import math

import jax
import jax.numpy as jnp
from jax import lax
from jax.experimental import pallas as pl
from jax.experimental.pallas import tpu as pltpu
from jax.sharding import PartitionSpec as P

MESH = pl.DeviceIdType.MESH
f32, bf16 = jnp.float32, jnp.bfloat16
root_scale = math.sqrt(2.0 / math.pi)
cubic = 0.044715

C = 384
ROWS = 512
LEAD = 16
TALL = ROWS + 2 * LEAD
LANES = 640
PAIRS = 44


def places(ring, deep, high):
    low = ring // high
    dp, ctx = lax.axis_index("dp"), lax.axis_index("context")
    y, xh = lax.div(dp, high), lax.rem(dp, high)
    core, z = lax.rem(ctx, 2), lax.rem(lax.div(ctx, 2), deep)
    x = xh * low + lax.div(ctx, 2 * deep)

    def device(x, y, z, core):
        return {
            "dp": y * high + lax.div(x, low),
            "context": (lax.rem(x, low) * deep + z) * 2 + core,
        }

    return x, y, z, core, device


def remote(src, dst, send, recv, to):
    return pltpu.make_async_remote_copy(
        src_ref=src, dst_ref=dst, send_sem=send, recv_sem=recv, device_id=to, device_id_type=MESH
    )


def main_kernel(
    ring, deep, high, count,
    vpos_in, vshift_in, codes_in, cot_in, stem_weight_in, weight,
    features, d_pooled, gathered, stem_all,
    vpos, vshift, codes, cot, stem_weight, insem, near_codes, near_cot, hs, hr, known, wcat,
    wt, wf, wsem, ws, stem, slopes, cotx, gx, pooled, pslope, shifted, spread, wins_t, gated_t, dstem,
    own, s0, r0, s1, r1, s2, r2,
    t0, u0, tsum, t1, u1, t2, u2,
    v3, s3, r3, g3, w3, v4, s4, r4, g4, w4,
    c0s, c0r, c1s, c1r, c2s, c2r, c3s, c3r, d3s, d3r, d2s, d2r, d1s, d1r, d0s, d0r,
    e0s, e0r, e1s, e1r, e2s, e2r, h0s, h0r, c4s, c4r, d4s, d4r,
):
    x, y, z, core, device = places(ring, deep, high)
    ctx = lax.axis_index("context")
    other = 1 - core
    per = 4 // ring
    rows1 = per * C
    rows2 = rows1 // ring

    def along(half, level, step):
        if (half == 0) == (level == 1):
            return device(lax.rem(x + step, ring), y, z, core)
        return device(x, lax.rem(y + step, ring), z, core)

    def mine(half, level):
        return x if (half == 0) == (level == 1) else y

    def deeper(step):
        return device(x, y, lax.rem(z + step, deep), core)

    sibling = device(x, y, z, other)
    order = sorted(range(1, ring), key=lambda d: -min(d, ring - d))
    near = order[::-1]

    feeds = [
        pltpu.make_async_copy(source, target, insem.at[i])
        for i, (source, target) in enumerate(
            [(vpos_in, vpos), (vshift_in, vshift), (codes_in, codes), (stem_weight_in, stem_weight), (cot_in, cot)]
        )
    ]
    for feed in feeds:
        feed.start()
    loads = [pltpu.make_async_copy(weight.at[t], wt.at[:, t * C : (t + 1) * C], wsem.at[t]) for t in range(5)]
    loads += [pltpu.make_async_copy(weight.at[t], wf.at[t * C : (t + 1) * C], wsem.at[5 + t]) for t in range(5)]
    left = {"context": lax.rem(ctx + count - 1, count)}
    right = {"context": lax.rem(ctx + 1, count)}
    barrier = pltpu.get_barrier_semaphore()
    greeted = [left, right, deeper(1), deeper(deep - 1)]
    greeted += [along(half, 1, step) for step in range(1, ring) for half in range(2)]
    for to in greeted:
        pl.semaphore_signal(barrier, inc=1, device_id=to, device_id_type=MESH)

    ws[...] = jnp.zeros_like(ws)
    feeds[3].wait()
    for k in range(15):
        ws[4 * k : 4 * k + 4, 0:C] = stem_weight[k]
        ws[4 * k + 4 : 4 * k + 8, C:] = stem_weight[k]
    taps = ws[...]
    upper = taps.astype(bf16)
    wcat[0:64] = upper
    wcat[64:128] = (taps - upper.astype(f32)).astype(bf16)
    for i in (0, 1, 2, 4):
        feeds[i].wait()

    pl.semaphore_wait(barrier, len(greeted))
    halos = [
        remote(codes, near_codes.at[0], hs.at[0], hr.at[0], right),
        remote(codes, near_codes.at[1], hs.at[1], hr.at[1], left),
        remote(cot.at[ROWS - LEAD : ROWS], near_cot.at[0], hs.at[2], hr.at[2], right),
        remote(cot.at[0:LEAD], near_cot.at[1], hs.at[3], hr.at[3], left),
    ]
    for copy in halos:
        copy.start()
    for load in loads:
        load.start()
    reach = [1 << m for m in range(8) if (1 << m) < deep // 2]

    def tell(m):
        for step in (reach[m], deep - reach[m]):
            pl.semaphore_signal(known.at[m], inc=1, device_id=deeper(step), device_id_type=MESH)

    def learn(m):
        if m < len(reach):
            pl.semaphore_wait(known.at[m], 2)
            if m + 1 < len(reach):
                tell(m + 1)

    if reach:
        tell(0)

    cotx[LEAD : LEAD + ROWS] = cot[...].astype(f32)

    def shift_in(first, size):
        for t in range(5):
            at = LEAD + 2 - t + first
            shifted[first : first + size, t * C : (t + 1) * C] = cotx[at : at + size].astype(bf16)

    shift_in(LEAD, ROWS - 2 * LEAD)
    shifted[:, 5 * C :] = jnp.zeros((ROWS, 128), bf16)
    spot = (
        ctx * (2 * ROWS) - 128
        + 128 * lax.broadcasted_iota(jnp.int32, (16, 128), 0)
        + lax.broadcasted_iota(jnp.int32, (16, 128), 1)
    )
    moved = jnp.zeros((16, 128), jnp.int32)
    for v in range(vpos.shape[1]):
        moved = moved + jnp.where(spot == vpos[0, v], vshift[0, v], 0)

    inside = (spot >= 0) & (spot < count * (2 * ROWS))
    lane_in = lax.broadcasted_iota(jnp.int32, (128, 128), 0)
    lane_out = lax.broadcasted_iota(jnp.int32, (128, 128), 1)
    pick = (lane_in == 2 * (lane_out & 63) + lax.shift_right_logical(lane_out, 6)).astype(f32).astype(bf16)
    first = lax.broadcasted_iota(jnp.int32, (1, 128), 1) < 64
    line = lax.broadcasted_iota(jnp.int32, (8, LANES), 0)

    def one_hot(before, after):
        bases = moved + jnp.concatenate([before, codes[...], after, jnp.zeros((6, 128), jnp.int32)], axis=0)
        bases = jnp.where(inside, bases & 3, 4)
        split = jnp.dot(bases.astype(f32).astype(bf16), pick, preferred_element_type=f32)
        turned = pltpu.roll(split, 64, 1)
        evens, odds = [], []
        for p in range(5):
            evens.append(jnp.where(first, split[2 * p : 2 * p + 1], turned[2 * p + 1 : 2 * p + 2]))
            odds.append(jnp.where(first, turned[2 * p : 2 * p + 1], split[2 * p + 1 : 2 * p + 2]))
        even = jnp.broadcast_to(jnp.concatenate(evens, axis=1), (8, LANES))
        odd = jnp.broadcast_to(jnp.concatenate(odds, axis=1), (8, LANES))
        both = jnp.where(line < 4, odd, pltpu.roll(even, LANES - 1, 1))
        return (both == (line & 3).astype(f32)).astype(f32)

    def windows_of(hot):
        wide = [pltpu.roll(hot, LANES - (PAIRS + q), 1) for q in range(8)]
        return jnp.concatenate(wide + wide, axis=0)

    def bend(value):
        square = value * value
        inner = jnp.tanh(value * (root_scale + (root_scale * cubic) * square))
        active = 0.5 * value * (1.0 + inner)
        slope = 0.5 * (1.0 + inner) + 0.5 * value * (1.0 - inner * inner) * (
            root_scale + (3.0 * root_scale * cubic) * square
        )
        return active, slope

    def activate(i, carry):
        rows = pl.ds(pl.multiple_of(i * 16, 16), 16)
        active_e, slope_e = bend(stem[rows, 0:C])
        active_o, slope_o = bend(stem[rows, C:])
        slopes[rows, 0:C] = 0.5 * slope_e
        slopes[rows, C:] = 0.5 * slope_o
        pool = (0.5 * (active_e + active_o)).astype(bf16).astype(f32)
        pooled[rows] = pool
        gate, slope = bend(pool)
        gx[rows] = gate.astype(bf16).astype(f32)
        pslope[rows] = slope
        return carry

    edge = 2 * LEAD
    blank = jnp.zeros((1, 128), jnp.int32)
    windows = windows_of(one_hot(blank, blank)).T[edge : TALL - edge].astype(bf16)
    stem[edge : TALL - edge] = jnp.dot(windows, wcat[...], preferred_element_type=f32)
    lax.fori_loop(edge // 16, (TALL - edge) // 16, activate, 0)

    for copy in halos:
        copy.wait_recv()
    learn(0)
    hot = one_hot(near_codes[0, 7:8], near_codes[1, 0:1])
    windows_t = windows_of(hot)
    ends = jnp.concatenate(
        [windows_t[:, 0:128].T[0:edge], windows_t[:, ROWS : ROWS + 128].T[0:edge]], axis=0
    ).astype(bf16)
    ends = jnp.dot(ends, wcat[...], preferred_element_type=f32)
    stem[0:edge] = ends[0:edge]
    stem[TALL - edge :] = ends[edge:]
    for i in (0, 1, TALL // 16 - 2, TALL // 16 - 1):
        activate(i, 0)
    inside_left = jnp.where(ctx > 0, 1.0, 0.0)
    inside_right = jnp.where(ctx < count - 1, 1.0, 0.0)
    gx[0:LEAD] = gx[0:LEAD] * inside_left
    gx[LEAD + ROWS :] = gx[LEAD + ROWS :] * inside_right
    cotx[0:LEAD] = near_cot[0].astype(f32) * inside_left
    cotx[LEAD + ROWS :] = near_cot[1].astype(f32) * inside_right
    shift_in(0, LEAD)
    shift_in(ROWS - LEAD, LEAD)
    gated_t[...] = gx[LEAD : LEAD + ROWS].T.astype(bf16)

    def level0(half, piece):
        return remote(
            s0.at[half, piece], r0.at[half, piece], c0s.at[half, piece], c0r.at[half, piece], sibling
        )

    def product(owner, j):
        at = pl.multiple_of(owner * 1024 + 256 * j, 256)
        return jnp.dot(gated_t[...], shifted[:, pl.ds(at, 256)], preferred_element_type=f32)

    parts = C // rows2
    for j in range(4):
        block = product(other, j)
        for k in range(2):
            half, sub = divmod(2 * j + k, 4)
            piece, sub = divmod(sub, per)
            some = block[:, 128 * k : 128 * (k + 1)].reshape(parts, rows2, 128)
            s0[half, piece, sub * parts : (sub + 1) * parts] = some.astype(bf16)
            if sub == per - 1:
                level0(half, piece).start()
    for j in range(4):
        block = product(core, j)
        for k in range(2):
            half, sub = divmod(2 * j + k, 4)
            piece, sub = divmod(sub, per)
            some = block[:, 128 * k : 128 * (k + 1)].reshape(parts, rows2, 128)
            own[half, piece, sub * parts : (sub + 1) * parts] = some

    def ahead(half, level, step):
        return lax.rem(mine(half, level) + step, ring)

    def behind(half, level, step):
        return lax.rem(mine(half, level) + ring - step, ring)

    sequence = order + [0]

    def level1(half, step, group):
        return remote(
            s1.at[half, step - 1, 2 * group : 2 * group + 2], r1.at[half, step - 1, 2 * group : 2 * group + 2],
            c1s.at[half, step - 1, group], c1r.at[half, step - 1, group], along(half, 1, step),
        )

    for half in range(2):
        for piece in range(ring):
            level0(half, piece).wait_recv()
    for slot, chunk in enumerate(sequence):
        for step in order:
            for half in range(2):
                at = ahead(half, 1, step), ahead(half, 2, chunk)
                s1[half, step - 1, slot] = (own[half, at[0], at[1]] + r0[half, at[0], at[1]].astype(f32)).astype(bf16)
                if slot % 2:
                    level1(half, step, slot // 2).start()

    learn(1)
    for load in loads:
        load.wait()
    for block in range(2):
        at = block * (ROWS // 2)
        rows = slice(at, at + ROWS // 2)
        more = slice(LEAD + at, LEAD + at + ROWS // 2)
        back = lax.dot_general(
            shifted[rows, : 5 * C], wt[...], (((1,), (1,)), ((), ())), preferred_element_type=f32
        )
        dpool = cotx[more] + back * pslope[more]
        d_pooled[rows] = dpool.astype(bf16)
        dstem[rows, 0:C] = (dpool * slopes[more, 0:C]).astype(bf16)
        dstem[rows, C:] = (dpool * slopes[more, C:]).astype(bf16)
    wins_t[...] = jnp.concatenate(
        [pltpu.roll(hot, LANES - (PAIRS + LEAD + q), 1)[:, :ROWS] for q in range(8)], axis=0
    ).astype(bf16)
    grad = jnp.dot(wins_t[...], dstem[...], preferred_element_type=f32)
    for k in range(3):
        tsum[k * 64 : k * 64 + 64] = grad[:, 128 * k : 128 * (k + 1)]
    for k in range(3):
        tsum[k * 64 : k * 64 + 60] = tsum[k * 64 : k * 64 + 60] + grad[4:64, C + 128 * k : C + 128 * (k + 1)]

    def stem0():
        return remote(t0, u0, e0s, e0r, sibling)

    t0[...] = tsum[pl.ds(pl.multiple_of(other * 96, 96), 96)].astype(bf16)
    stem0().start()

    for t in range(5):
        spread[:, t * C : (t + 1) * C] = gx[LEAD - 2 + t : LEAD - 2 + t + ROWS].astype(bf16)
    for block in range(2):
        at = block * (ROWS // 2)
        rows = slice(at, at + ROWS // 2)
        conv = jnp.dot(spread[rows], wf[...], preferred_element_type=f32)
        features[rows] = (pooled[LEAD + at : LEAD + at + ROWS // 2] + conv).astype(bf16)

    def stem1(step):
        return remote(t1, u1.at[step - 1], e1s.at[step - 1], e1r.at[step - 1], along(0, 1, step))

    def stem2(step):
        return remote(t2, u2.at[step - 1], e2s.at[step - 1], e2r.at[step - 1], along(0, 2, step))

    stem0().wait_recv()
    small = tsum[pl.ds(pl.multiple_of(core * 96, 96), 96)] + u0[...].astype(f32)
    t1[...] = small.astype(bf16)
    for step in order:
        stem1(step).start()

    def level2(half, step):
        return remote(
            s2.at[half, step - 1], r2.at[half, step - 1], c2s.at[half, step - 1], c2r.at[half, step - 1],
            along(half, 2, step),
        )

    for slot, chunk in enumerate(sequence):
        for half in range(2):
            at = mine(half, 1), ahead(half, 2, chunk)
            total = own[half, at[0], at[1]] + r0[half, at[0], at[1]].astype(f32)
            for step in range(1, ring):
                if slot % 2 == 0:
                    level1(half, step, slot // 2).wait_recv()
                total = total + r1[half, step - 1, slot].astype(f32)
            if chunk:
                s2[half, chunk - 1] = total.astype(bf16)
                level2(half, chunk).start()
            else:
                v3[half * rows2 : (half + 1) * rows2] = total

    for step in range(1, ring):
        stem1(step).wait_recv()
        small = small + u1[step - 1].astype(f32)
    t2[...] = small.astype(bf16)
    for step in order:
        stem2(step).start()

    def far(i):
        half_way = deep // 2 - lax.div(i + 1, 2)
        return jnp.where(lax.rem(i, 2) == 0, half_way, deep - half_way)

    def down(send, land, sends, recvs):
        return lambda step: remote(
            send.at[lax.rem(z + step, deep)], land.at[step - 1], sends.at[step - 1], recvs.at[step - 1], deeper(step)
        )

    def up(all_of, sends, recvs):
        return lambda step: remote(all_of.at[z], all_of.at[z], sends.at[step - 1], recvs.at[step - 1], deeper(step))

    def start_all(copy):
        def one(i, carry):
            copy(far(i)).start()
            return carry

        lax.fori_loop(0, deep - 1, one, 0)

    def each(method, *copies):
        def one(i, carry):
            for copy in copies:
                getattr(copy(i + 1), method)()
            return carry

        lax.fori_loop(0, deep - 1, one, 0)

    def cut(source, send, share):
        for piece in range(deep):
            send[piece] = source[piece * share : piece * share + send.shape[1]].astype(bf16)

    def join(all_of, target, share):
        for piece in range(deep):
            target[piece * share : piece * share + all_of.shape[1]] = all_of[piece].astype(f32)

    def summed(copy, send, land):
        def one(i, total):
            step = far(deep - 2 - i)
            copy(step).wait_recv()
            return total + land[step - 1].astype(f32)

        return lax.fori_loop(0, deep - 1, one, send[z].astype(f32)).astype(bf16)

    for half in range(2):
        total = v3[half * rows2 : (half + 1) * rows2]
        for step in near:
            level2(half, step).wait_recv()
            total = total + r2[half, step - 1].astype(f32)
        v3[half * rows2 : (half + 1) * rows2] = total
    conv_down, conv_up = down(s3, r3, c3s, c3r), up(g3, d3s, d3r)
    stem_down, stem_up = down(s4, r4, c4s, c4r), up(g4, d4s, d4r)
    for m in range(2, len(reach)):
        learn(m)
    cut(v3, s3, 2 * rows2 // deep)
    start_all(conv_down)
    for step in range(1, ring):
        stem2(step).wait_recv()
        small = small + u2[step - 1].astype(f32)
    v4[0:96] = small
    cut(v4, s4, 96 // deep)
    start_all(stem_down)
    for half in range(2):
        for step in range(ring):
            level0(half, step).wait_send()
        for step in range(1, ring):
            level2(half, step).wait_send()
            for group in range(ring // 2):
                level1(half, step, group).wait_send()
    stem0().wait_send()
    for step in range(1, ring):
        stem1(step).wait_send()
        stem2(step).wait_send()
    for copy in halos:
        copy.wait_send()
    g3[z] = summed(conv_down, s3, r3)
    start_all(conv_up)
    g4[z] = summed(stem_down, s4, r4)
    start_all(stem_up)
    each("wait_send", conv_down, stem_down)
    each("wait_recv", conv_up)
    join(g3, w3, 2 * rows2 // deep)

    def back2(half, step):
        spot = gathered.at[core, half, mine(half, 1), mine(half, 2)]
        return remote(spot, spot, d2s.at[half, step - 1], d2r.at[half, step - 1], along(half, 2, step))

    def back1(half, step, chunk):
        spot = gathered.at[core, half, mine(half, 1), behind(half, 2, chunk)]
        return remote(spot, spot, d1s.at[half, step - 1, chunk], d1r.at[half, step - 1, chunk], along(half, 1, step))

    def back0(half, step, chunk):
        spot = gathered.at[core, half, behind(half, 1, step), behind(half, 2, chunk)]
        return remote(spot, spot, d0s.at[half, step, chunk], d0r.at[half, step, chunk], sibling)

    for half in range(2):
        gathered[core, half, mine(half, 1), mine(half, 2)] = w3[half * rows2 : (half + 1) * rows2].astype(bf16)
        for step in order:
            back2(half, step).start()
    for chunk in [0] + near:
        for half in range(2):
            if chunk:
                back2(half, chunk).wait_recv()
            for step in order:
                back1(half, step, chunk).start()
            back0(half, 0, chunk).start()

    each("wait_recv", stem_up)
    join(g4, w4, 96 // deep)

    def back_stem():
        return remote(stem_all.at[core], stem_all.at[core], h0s, h0r, sibling)

    stem_all[core] = w4[0:96].astype(bf16)
    back_stem().start()
    each("wait_send", conv_up, stem_up)
    last = []
    for chunk in [0] + near:
        fresh = [(half, 0, chunk) for half in range(2)]
        for step in near:
            for half in range(2):
                back1(half, step, chunk).wait_recv()
                back0(half, step, chunk).start()
                fresh.append((half, step, chunk))
        for spot in last:
            back0(*spot).wait()
        last = fresh
    for half in range(2):
        for step in range(1, ring):
            back2(half, step).wait_send()
            for chunk in range(ring):
                back1(half, step, chunk).wait_send()
    back_stem().wait()
    for spot in last:
        back0(*spot).wait()


def main(ring, deep, high, vpos, vshift, codes, cot, stem_weight, weight):
    per = 4 // ring
    rows1 = per * C
    rows2 = rows1 // ring
    talls = [-(-total // (8 * deep)) * 8 for total in (2 * rows2, 96)]
    count = 2 * (ring // high) * deep
    dma = pltpu.SemaphoreType.DMA
    halves = lambda *lead: pltpu.VMEM((2,) + lead, bf16)
    pair = lambda *dims: [dma(dims), dma(dims)]
    vmem = pl.BlockSpec(memory_space=pltpu.VMEM)
    hbm = pl.BlockSpec(memory_space=pltpu.HBM)
    return pl.pallas_call(
        functools.partial(main_kernel, ring, deep, high, count),
        out_shape=(
            jax.ShapeDtypeStruct((ROWS, C), bf16),
            jax.ShapeDtypeStruct((ROWS, C), bf16),
            jax.ShapeDtypeStruct((2, 2, ring, ring, rows2, 128), bf16),
            jax.ShapeDtypeStruct((2, 96, 128), bf16),
        ),
        in_specs=[hbm] * 6,
        out_specs=(vmem,) * 4,
        scratch_shapes=[
            pltpu.SMEM(vpos.shape, jnp.int32),
            pltpu.SMEM(vshift.shape, jnp.int32),
            pltpu.VMEM((8, 128), jnp.int32),
            pltpu.VMEM((ROWS, C), bf16),
            pltpu.VMEM((15, 4, C), f32),
            dma((5,)),
            pltpu.VMEM((2, 8, 128), jnp.int32),
            pltpu.VMEM((2, LEAD, C), bf16),
            *pair(4),
            pltpu.SemaphoreType.REGULAR((3,)),
            pltpu.VMEM((128, 2 * C), bf16),
            pltpu.VMEM((C, 5 * C), bf16),
            pltpu.VMEM((5 * C, C), bf16),
            dma((10,)),
            pltpu.VMEM((64, 2 * C), f32),
            pltpu.VMEM((TALL, 2 * C), f32),
            pltpu.VMEM((TALL, 2 * C), f32),
            pltpu.VMEM((TALL, C), f32),
            pltpu.VMEM((TALL, C), f32),
            pltpu.VMEM((TALL, C), f32),
            pltpu.VMEM((TALL, C), f32),
            pltpu.VMEM((ROWS, 2048), bf16),
            pltpu.VMEM((ROWS, 5 * C), bf16),
            pltpu.VMEM((64, ROWS), bf16),
            pltpu.VMEM((C, ROWS), bf16),
            pltpu.VMEM((ROWS, 2 * C), bf16),
            pltpu.VMEM((2, ring, ring, rows2, 128), f32),
            halves(ring, ring, rows2, 128),
            halves(ring, ring, rows2, 128),
            halves(ring - 1, ring, rows2, 128),
            halves(ring - 1, ring, rows2, 128),
            halves(ring - 1, rows2, 128),
            halves(ring - 1, rows2, 128),
            pltpu.VMEM((96, 128), bf16),
            pltpu.VMEM((96, 128), bf16),
            pltpu.VMEM((192, 128), f32),
            pltpu.VMEM((96, 128), bf16),
            pltpu.VMEM((ring - 1, 96, 128), bf16),
            pltpu.VMEM((96, 128), bf16),
            pltpu.VMEM((ring - 1, 96, 128), bf16),
            *[
                scratch
                for tall, total in zip(talls, (2 * rows2, 96))
                for scratch in (
                    pltpu.VMEM((total + tall, 128), f32),
                    pltpu.VMEM((deep, tall, 128), bf16),
                    pltpu.VMEM((deep - 1, tall, 128), bf16),
                    pltpu.VMEM((deep, tall, 128), bf16),
                    pltpu.VMEM((total + tall, 128), f32),
                )
            ],
            *pair(2, ring), *pair(2, ring - 1, ring), *pair(2, ring - 1), *pair(deep - 1),
            *pair(deep - 1), *pair(2, ring - 1), *pair(2, ring - 1, ring), *pair(2, ring, ring),
            *pair(), *pair(ring - 1), *pair(ring - 1), *pair(),
            *pair(deep - 1), *pair(deep - 1),
        ],
        compiler_params=pltpu.CompilerParams(
            collective_id=0, has_side_effects=True, vmem_limit_bytes=36 * 1024 * 1024
        ),
        name="block",
    )(vpos, vshift, codes, cot, stem_weight, weight)


def finish_kernel(summed, small, features, d_pooled, conv, stem, features_out, d_pooled_out, widened, sems):
    copies = [
        pltpu.make_async_copy(features, features_out, sems.at[5]),
        pltpu.make_async_copy(d_pooled, d_pooled_out, sems.at[6]),
    ]
    for t in range(5):
        for k in range(3):
            widened[t, :, k * 128 : (k + 1) * 128] = summed[3 * t + k].astype(f32)
        copies.append(pltpu.make_async_copy(widened.at[t], conv.at[t], sems.at[t]))
        copies[-1].start()
    for copy in copies[:2]:
        copy.start()
    rows = jnp.concatenate([small[0], small[1]], axis=0).astype(f32)
    for k in range(3):
        for tap in range(15):
            stem[tap, :, k * 128 : (k + 1) * 128] = rows[k * 64 + 4 * tap : k * 64 + 4 * tap + 4]
    for copy in copies:
        copy.wait()


def finish(summed, small, features, d_pooled):
    vmem = pl.BlockSpec(memory_space=pltpu.VMEM)
    apart = pl.BlockSpec(memory_space=pl.ANY)
    return pl.pallas_call(
        finish_kernel,
        out_shape=(
            jax.ShapeDtypeStruct((5, C, C), f32),
            jax.ShapeDtypeStruct((15, 4, C), f32),
            jax.ShapeDtypeStruct((ROWS, C), bf16),
            jax.ShapeDtypeStruct((ROWS, C), bf16),
        ),
        in_specs=[vmem] * 4,
        out_specs=(apart, vmem, apart, apart),
        scratch_shapes=[pltpu.VMEM((5, C, C), f32), pltpu.SemaphoreType.DMA((7,))],
        compiler_params=pltpu.CompilerParams(vmem_limit_bytes=8 * 1024 * 1024),
        name="finish",
    )(summed.reshape(16, C, 128), small, features, d_pooled)


def per_device(ring, deep, high, codes, variant_pos, variant_shift, stem_weight, conv_weight, cotangent):
    codes = codes.reshape(8, 128)
    cot = cotangent.reshape(ROWS, C)
    codes, cot, variant_pos, variant_shift, stem_weight, conv_weight = (
        pltpu.with_memory_space_constraint(array, pltpu.HBM)
        for array in (codes, cot, variant_pos, variant_shift, stem_weight, conv_weight)
    )
    features, d_pooled, summed, small = main(
        ring, deep, high, variant_pos, variant_shift, codes, cot, stem_weight, conv_weight
    )
    conv_grad, stem_grad, features, d_pooled = finish(summed, small, features, d_pooled)
    return features[None], d_pooled[None], conv_grad, stem_grad


def build(mesh, ring, deep, high):
    placed = (P("dp", "context"), P("dp", None), P("dp", None), P(), P(), P("dp", "context", None))
    return jax.shard_map(
        functools.partial(per_device, ring, deep, high),
        mesh=mesh,
        in_specs=placed,
        out_specs=(P("dp", "context", None), P("dp", "context", None), P(), P()),
        check_vma=False,
    )


def solution(mesh):
    return build(mesh, 4, 16, 2)
```
